32 devices in a mesh: stream: 2 (over y), dp: 16 (over z, x, core).
Axes of the slice: x: 2, y: 2, z: 4, core: 2. Of those that a mesh axis runs over, the one named last changes fastest.
Arguments:
- hidden: bfloat16 [2, 64, 100, 1024], P('stream', 'dp'), may hold values from -6 to 6
- text_lengths: int32 [64], P('dp'), may hold values from 24 to 64
- region_counts: int32 [64], P('dp'), may hold values from 10 to 100
- co_qkv: bfloat16 [2, 3, 1024, 1024], P('stream'), may hold values from -0.1875 to 0.1875
- co_out: bfloat16 [2, 1024, 1024], P('stream'), may hold values from -1 to 1
- self_qkv: bfloat16 [2, 3, 1024, 1024], P('stream'), may hold values from -0.1875 to 0.1875
- self_out: bfloat16 [2, 1024, 1024], P('stream'), may hold values from -1 to 1
- mlp_up: bfloat16 [2, 2, 1024, 3072], P('stream'), may hold values from -0.1875 to 0.1875
- mlp_down: bfloat16 [2, 2, 3072, 1024], P('stream'), may hold values from -0.21875 to 0.21875
- proj_bias: bfloat16 [2, 2, 3, 1024], P('stream'), may hold values from -1.796875 to 1.796875
- mlp_bias_up: bfloat16 [2, 2, 3072], P('stream'), may hold values from -1.796875 to 1.796875
- mlp_bias_down: bfloat16 [2, 2, 1024], P('stream'), may hold values from -1.796875 to 1.796875
- norm_gain_table: bfloat16 [2, 4, 1024], P('stream'), may hold values from 0.099609375 to 1.8984375
- norm_bias: bfloat16 [2, 4, 1024], P('stream'), may hold values from -1.796875 to 1.796875
- cotangent: bfloat16 [2, 64, 100, 1024], P('stream', 'dp'), may hold values from -6 to 6
Outputs:
- result: bfloat16 [2, 64, 100, 1024], P('stream', 'dp')
- hidden_grad: bfloat16 [2, 64, 100, 1024], P('stream', 'dp')
- grad_co_qkv: float32 [2, 3, 1024, 1024], P('stream', None, 'dp')
- grad_co_out: float32 [2, 1024, 1024], P('stream', 'dp')
- grad_self_qkv: float32 [2, 3, 1024, 1024], P('stream', None, 'dp')
- grad_self_out: float32 [2, 1024, 1024], P('stream', 'dp')
- grad_mlp_up: float32 [2, 2, 1024, 3072], P('stream', None, 'dp')
- grad_mlp_down: float32 [2, 2, 3072, 1024], P('stream', None, 'dp')
- grad_proj_bias: float32 [2, 2, 3, 1024], P('stream', None, None, 'dp')
- grad_mlp_bias_up: float32 [2, 2, 3072], P('stream', None, 'dp')
- grad_mlp_bias_down: float32 [2, 2, 1024], P('stream', None, 'dp')
- grad_norm_gain: float32 [2, 4, 1024], P('stream', None, 'dp')
- grad_norm_bias: float32 [2, 4, 1024], P('stream', None, 'dp')
The draws below stay inside these ranges and needn't reach their ends.
All inputs are finite; a program needn't handle non-finite values.
Results may differ from the reference program's by a relative error of at most 0.023.
Values may be sent and summed in bfloat16 or wider, within the bound.
A program may use at most 384 MiB of HBM per device.

```python
import math
import jax
import jax.numpy as jnp
from jax import lax

DT = 768
DV = 1024
DB = 1024
FT = 3072
FV = 1024
TEXT_HEADS = 12
IMAGE_HEADS = 8
CO_HEADS = 8
DMAX = 1024
FMAX = 3072
SLOTS = 100
TEXT_MIN = 24
TEXT_MAX = 64
REGION_MIN = 10
PAIRS = 64


def touch_ends(values, own_key, least, largest):
    dims = values.shape
    spot = [jax.random.randint(jax.random.fold_in(own_key, axis), (), 0, dims[axis]) for axis in range(len(dims))]
    values = values.at[tuple(spot)].set(least)
    longest = dims.index(max(dims))
    spot[longest] = (spot[longest] + 1) % dims[longest]
    return values.at[tuple(spot)].set(largest)


def block_scale(key, extent, cuts, least, top_value):
    def one(position, blocks):
        draws = jax.random.uniform(jax.random.fold_in(jax.random.fold_in(key, 6), position), (blocks,), jnp.float32, least / len(cuts), top_value / len(cuts))
        return jnp.repeat(jnp.exp(draws), extent[position] // blocks).reshape((-1,) + (1,) * (len(extent) - position - 1))

    gain = one(*cuts[0])
    for cut in cuts[1:]:
        gain = gain * one(*cut)
    return gain


def centred(own_key, extent, spread, most, shards=(), kind=jnp.bfloat16):
    values = jax.random.normal(own_key, extent, jnp.float32) * spread
    if len(shards) > 0:
        values = block_scale(own_key, extent, shards, -0.22, 0.18) * values
    return jnp.clip(values, min=-most, max=most).astype(kind)


def setup_inputs(seed: int = 0) -> dict:
    key_list = jax.random.split(jax.random.key(seed), 16)
    return {
        "hidden": centred(key_list[0], (2, PAIRS, SLOTS, DMAX), 1.0, 6.0, ((0, 2), (1, 16))),
        "text_lengths": touch_ends(jax.random.randint(key_list[1], (PAIRS,), TEXT_MIN, TEXT_MAX + 1), jax.random.fold_in(key_list[1], 1), TEXT_MIN, TEXT_MAX).astype(jnp.int32),
        "region_counts": touch_ends(jax.random.randint(key_list[2], (PAIRS,), REGION_MIN, SLOTS + 1), jax.random.fold_in(key_list[2], 1), REGION_MIN, SLOTS).astype(jnp.int32),
        "co_qkv": centred(key_list[3], (2, 3, DMAX, DB), DMAX ** -0.5, 0.1875, ((0, 2),)),
        "co_out": centred(key_list[4], (2, DB, DMAX), (DB // 32) ** -0.5, 1.0, ((0, 2),)),
        "self_qkv": centred(key_list[5], (2, 3, DMAX, DMAX), DMAX ** -0.5, 0.1875, ((0, 2),)),
        "self_out": centred(key_list[6], (2, DMAX, DMAX), (DMAX // 32) ** -0.5, 1.0, ((0, 2),)),
        "mlp_up": centred(key_list[7], (2, 2, DMAX, FMAX), DMAX ** -0.5, 0.1875, ((0, 2),)),
        "mlp_down": centred(key_list[8], (2, 2, FMAX, DMAX), (FMAX // 4) ** -0.5, 0.21875, ((0, 2),)),
        "proj_bias": centred(key_list[9], (2, 2, 3, DMAX), 0.3, 1.796875, ((0, 2),)),
        "mlp_bias_up": centred(key_list[10], (2, 2, FMAX), 0.3, 1.796875, ((0, 2),)),
        "mlp_bias_down": centred(key_list[11], (2, 2, DMAX), 0.3, 1.796875, ((0, 2),)),
        "norm_gain_table": jnp.clip(1.0 + 0.18 * jax.random.normal(key_list[12], (2, 4, DMAX), jnp.float32), 0.099609375, 1.8984375).astype(jnp.bfloat16),
        "norm_bias": centred(key_list[13], (2, 4, DMAX), 0.3, 1.796875, ((0, 2),)),
        "cotangent": centred(key_list[14], (2, PAIRS, SLOTS, DMAX), 1.0, 6.0, ((0, 2), (1, 16))),
    }


EPSILON = 1e-05
NEGATIVE = -1000000000.0
HIGHEST = lax.Precision.HIGHEST

@jax.custom_vjp
def low(v):
    return lax.optimization_barrier(v.astype(jnp.bfloat16)).astype(jnp.float32)

@jax.custom_vjp
def low_back(v):
    return v

def low_keep(v):
    return (low(v), None)

def low_pass(kept, grad):
    return (grad,)

def back_keep(v):
    return (v, None)

def back_low(kept, grad):
    return (low(grad),)
low.defvjp(low_keep, low_pass)
low_back.defvjp(back_keep, back_low)

def product(left, right):
    return jnp.matmul(left, right, precision=HIGHEST)

def layer_norm(summed, scaling, offset):
    average = lax.optimization_barrier(jnp.mean(summed, axis=-1, keepdims=True))
    centered = summed - average
    variance = lax.optimization_barrier(jnp.mean(centered * centered, axis=-1, keepdims=True))
    return centered * lax.rsqrt(variance + EPSILON) * scaling + offset

def attention(query, keys, values, key_valid, head_count):
    group_pairs, slot_count, model_width = query.shape
    head_size = model_width // head_count
    query_heads = query.reshape(group_pairs, slot_count, head_count, head_size)
    key_heads = keys.reshape(group_pairs, slot_count, head_count, head_size)
    value_heads = values.reshape(group_pairs, slot_count, head_count, head_size)
    scores = low_back(jnp.einsum('pqhe,pkhe->phqk', query_heads, key_heads, precision=HIGHEST)) * (1.0 / math.sqrt(head_size))
    scores = jnp.where(key_valid[:, None, None, :], scores, NEGATIVE)
    probability = low(jax.nn.softmax(scores, axis=-1))
    mixture = jnp.einsum('phqk,pkhe->pqhe', probability, value_heads, precision=HIGHEST)
    return mixture.reshape(group_pairs, slot_count, model_width)

def cross_inputs(states, params, stream, model_width):
    co_qkv, proj_bias = (params[0], params[6])
    query = low(low_back(product(states, co_qkv[stream, 0, :model_width]) + proj_bias[stream, 0, 0, :DB]))
    keys = low(low_back(product(states, co_qkv[stream, 1, :model_width])))
    values = low(low_back(product(states, co_qkv[stream, 2, :model_width]) + proj_bias[stream, 0, 1, :DB]))
    return (query, keys, values)

def feed(normed, params, stream, block, model_width, inner_width):
    mlp_up, mlp_down, bias_up, bias_down, norm_gain_table, norm_bias = (params[4], params[5], params[7], params[8], params[9], params[10])
    hidden_in = low_back(product(low(normed), mlp_up[stream, block, :model_width, :inner_width]) + bias_up[stream, block, :inner_width])
    activated = low(jax.nn.gelu(hidden_in, approximate=False))
    branch = low_back(product(activated, mlp_down[stream, block, :inner_width, :model_width]) + bias_down[stream, block, :model_width])
    return layer_norm(normed + branch, norm_gain_table[stream, 2 * block + 1, :model_width], norm_bias[stream, 2 * block + 1, :model_width])

def stream_rest(states, context, params, stream, model_width, inner_width, head_count, key_valid):
    co_out, self_qkv, self_out, proj_bias, norm_gain_table, norm_bias = (params[1], params[2], params[3], params[6], params[9], params[10])
    context = low(low_back(context))
    branch = low_back(product(context, co_out[stream, :, :model_width]) + proj_bias[stream, 0, 2, :model_width])
    first_operand = layer_norm(states + branch, norm_gain_table[stream, 0, :model_width], norm_bias[stream, 0, :model_width])
    middle_operand = feed(first_operand, params, stream, 0, model_width, inner_width)
    normed = low(middle_operand)
    query = low(low_back(product(normed, self_qkv[stream, 0, :model_width, :model_width]) + proj_bias[stream, 1, 0, :model_width]))
    keys = low(low_back(product(normed, self_qkv[stream, 1, :model_width, :model_width])))
    values = low(low_back(product(normed, self_qkv[stream, 2, :model_width, :model_width]) + proj_bias[stream, 1, 1, :model_width]))
    mixture = low(low_back(attention(query, keys, values, key_valid, head_count)))
    branch_two = low_back(product(mixture, self_out[stream, :model_width, :model_width]) + proj_bias[stream, 1, 2, :model_width])
    trailing_operand = layer_norm(middle_operand + branch_two, norm_gain_table[stream, 2, :model_width], norm_bias[stream, 2, :model_width])
    return feed(trailing_operand, params, stream, 1, model_width, inner_width)

def forward(text_states, image_states, text_valid, image_valid, params):
    text_query, text_keys, text_values = cross_inputs(text_states, params, 0, DT)
    image_query, image_keys, image_values = cross_inputs(image_states, params, 1, DV)
    text_context = attention(text_query, image_keys, image_values, image_valid, CO_HEADS)
    image_context = attention(image_query, text_keys, text_values, text_valid, CO_HEADS)
    text_out = stream_rest(text_states, text_context, params, 0, DT, FT, TEXT_HEADS, text_valid)
    image_out = stream_rest(image_states, image_context, params, 1, DV, FV, IMAGE_HEADS, image_valid)
    return (text_out, image_out)

def reference(hidden, text_lengths, region_counts, co_qkv, co_out, self_qkv, self_out, mlp_up, mlp_down, proj_bias, mlp_bias_up, mlp_bias_down, norm_gain_table, norm_bias, cotangent):
    params = tuple((member.astype(jnp.float32) for member in (co_qkv, co_out, self_qkv, self_out, mlp_up, mlp_down, proj_bias, mlp_bias_up, mlp_bias_down, norm_gain_table, norm_bias)))
    group_size = math.gcd(PAIRS, 32)
    step_count = PAIRS // group_size
    states = hidden.astype(jnp.float32)
    seeds = cotangent.astype(jnp.float32)

    def blocks(array):
        return array.reshape((step_count, group_size) + array.shape[1:])
    inputs = (blocks(states[0, :, :, :DT]), blocks(states[1, :, :, :DV]), blocks(seeds[0, :, :, :DT]), blocks(seeds[1, :, :, :DV]), blocks(text_lengths.astype(jnp.int32)), blocks(region_counts.astype(jnp.int32)))
    positions = jnp.arange(SLOTS, dtype=jnp.int32)

    def scan_step(totals, scan_item):
        text_states, image_states, text_seed, image_seed, text_count, image_count = scan_item
        text_valid = positions[None, :] < text_count[:, None]
        image_valid = positions[None, :] < image_count[:, None]

        def forward_group(text_in, image_in, group_params):
            return forward(text_in, image_in, text_valid, image_valid, group_params)
        outputs, pullback = jax.vjp(forward_group, text_states, image_states, params)
        grad_text, grad_image, grad_params = pullback((text_seed, image_seed))
        totals = jax.tree.map(jnp.add, totals, grad_params)
        return (totals, (outputs[0], outputs[1], grad_text, grad_image))
    zero_grads = tuple((jnp.zeros_like(member) for member in params))
    totals, gathered = lax.scan(scan_step, zero_grads, inputs)
    text_out, image_out, text_grad, image_grad = gathered

    def assemble(text_part, image_part):
        text_full = jnp.pad(text_part.reshape(PAIRS, SLOTS, DT), ((0, 0), (0, 0), (0, DMAX - DT)))
        image_full = jnp.pad(image_part.reshape(PAIRS, SLOTS, DV), ((0, 0), (0, 0), (0, DMAX - DV)))
        return jnp.stack([text_full, image_full]).astype(jnp.bfloat16)
    return (assemble(text_out, image_out), assemble(text_grad, image_grad), totals[0], totals[1], totals[2], totals[3], totals[4], totals[5], totals[6], totals[7], totals[8], totals[9], totals[10])
```

```python
from functools import partial
import math

import jax
import jax.numpy as jnp
from jax import lax
from jax.experimental import pallas as pl
from jax.experimental.pallas import tpu as pltpu
from jax.sharding import PartitionSpec as P

DT = 768
DV = 1024
FT = 3072
FV = 1024
TEXT_HEADS = 12
IMAGE_HEADS = 8
CO_HEADS = 8


EPSILON = 1e-05
NEGATIVE = -1000000000.0
ROOT_HALF = 1.0 / math.sqrt(2.0)
GAUSS_NORM = 1.0 / math.sqrt(2.0 * math.pi)


def from_partner(value, axis, stride):
    mask = 2**stride
    pairs = [(source, source ^ mask) for source in range(lax.axis_size(axis))]
    return lax.ppermute(value, axis, pairs)


def widen(array, target):
    return jnp.pad(array, [(0, wanted - current) for current, wanted in zip(array.shape, target)])


MESH = pl.DeviceIdType.MESH
UNIT = 256
OUT_BLOCKS = 81
CORE_SLOTS = 4
LAG_X = 4
X_SLOTS = 2 * LAG_X
LAG_Z = 2
Z_SLOTS = 4

TEXT_UNITS = (
    (3, 3, 9, 1, 60, 0, 68, 4, 256),
    (1, 12, 5, 0, 44, 0, 44, 0, 192),
    (1, 3, 3, 0, 28, 0, 28, 0, 192),
    (3, 3, 2, 0, 16, 4, 16, 4, 192),
    (3, 3, 6, 1, 56, 0, 56, 4, 256),
    (1, 12, 4, 0, 32, 0, 32, 0, 192),
    (1, 3, 1, 0, 12, 0, 12, 0, 256),
    (3, 4, 0, 0, 0, 4, 0, 4, 192),
    (1, 1, 0, 0, 0, 0, 80, 0, 256),
)
IMAGE_UNITS = (
    (3, 4, 9, 1, 60, 0, 68, 4, 128),
    (1, 4, 5, 0, 44, 0, 44, 0, 256),
    (1, 4, 3, 0, 28, 0, 28, 0, 256),
    (3, 4, 2, 0, 16, 4, 16, 4, 256),
    (3, 4, 6, 1, 56, 0, 56, 4, 128),
    (1, 4, 4, 0, 32, 0, 32, 0, 256),
    (1, 4, 1, 0, 12, 0, 12, 0, 256),
    (3, 4, 0, 0, 0, 4, 0, 4, 256),
    (1, 1, 0, 0, 0, 0, 80, 0, 256),
)


def unit_count(table):
    return sum(entry[0] * entry[1] for entry in table)


def decode_one(table, unit):
    start = 0
    result = None
    for groups, blocks, a0, a1, g0, g1, o0, o1, kept in table:
        local = unit - start
        group = local // blocks
        block = local % blocks
        fields = (a0 + a1 * group, g0 + g1 * group + block, o0 + o1 * group + block, jnp.int32(kept))
        if result is None:
            result = fields
        else:
            result = tuple(jnp.where(unit >= start, new, old) for new, old in zip(fields, result))
        start += groups * blocks
    return result


def decode(is_text, unit):
    text = decode_one(TEXT_UNITS, unit)
    image = decode_one(IMAGE_UNITS, unit)
    return tuple(jnp.where(is_text, one, other) for one, other in zip(text, image))


def reduce_kernel(
    line,
    at_ref,
    g_ref,
    vec_ref,
    out_ref,
    core_out,
    core_in,
    partial_own,
    x_out,
    x_in,
    own,
    down_out,
    down_in,
    up_out,
    up_in,
    core_sems,
    x_sems,
    down_sems,
    up_sems,
    down_free,
    up_free,
):
    piece = 256 // line
    stream = lax.axis_index("stream")
    place = lax.axis_index("dp")
    core = lax.rem(place, 2)
    side = lax.rem(place // 2, 2)
    spot = place // 4
    is_text = stream == 0
    total = jnp.where(is_text, unit_count(TEXT_UNITS), unit_count(IMAGE_UNITS))
    core_device = (stream, place + 1 - 2 * core)
    side_device = (stream, place + 2 - 4 * side)
    lower_device = (stream, place - 4)
    upper_device = (stream, place + 4)
    own_slots = LAG_X + (line - 1) * LAG_Z + 1
    last = line - 1

    barrier = pltpu.get_barrier_semaphore()
    pl.semaphore_signal(barrier, inc=1, device_id=core_device, device_id_type=MESH)
    pl.semaphore_signal(barrier, inc=1, device_id=side_device, device_id_type=MESH)

    @pl.when(spot > 0)
    def _():
        pl.semaphore_signal(barrier, inc=1, device_id=lower_device, device_id_type=MESH)

    @pl.when(spot < last)
    def _():
        pl.semaphore_signal(barrier, inc=1, device_id=upper_device, device_id_type=MESH)

    pl.semaphore_wait(
        barrier, 2 + (spot > 0).astype(jnp.int32) + (spot < last).astype(jnp.int32)
    )
    out_ref[...] = jnp.zeros_like(out_ref)

    def for_rows(kept, body):
        for rows in (128, 192, 256):

            @pl.when(kept == rows)
            def _():
                body(rows)

    def core_copy(unit, rows):
        slot = lax.rem(unit, CORE_SLOTS)
        return pltpu.make_async_remote_copy(
            src_ref=core_out.at[slot, :, pl.ds(0, rows)],
            dst_ref=core_in.at[slot, :, pl.ds(0, rows)],
            send_sem=core_sems.at[0, slot],
            recv_sem=core_sems.at[1, slot],
            device_id=core_device,
            device_id_type=MESH,
        )

    def side_copy(unit, rows):
        slot = lax.rem(unit, X_SLOTS)
        return pltpu.make_async_remote_copy(
            src_ref=x_out.at[slot, pl.ds(0, rows)],
            dst_ref=x_in.at[slot, pl.ds(0, rows)],
            send_sem=x_sems.at[0, slot],
            recv_sem=x_sems.at[1, slot],
            device_id=side_device,
            device_id_type=MESH,
        )

    def line_copy(source, target, sems, device, slot, index):
        at = pl.ds(pl.multiple_of(index * piece, piece), piece)
        return pltpu.make_async_remote_copy(
            src_ref=source.at[slot, at],
            dst_ref=target.at[slot, at],
            send_sem=sems.at[0, slot, index],
            recv_sem=sems.at[1, slot, index],
            device_id=device,
            device_id_type=MESH,
        )

    def columns(block):
        return pl.ds(pl.multiple_of(block * UNIT, UNIT), UNIT)

    def multiply(unit):
        a_block, g_block, out_block, kept = decode(is_text, unit)
        slot = lax.rem(unit, CORE_SLOTS)
        keep = lax.rem(unit, 2)
        is_vector = unit == total - 1

        @pl.when(jnp.logical_not(is_vector))
        def _():
            gradient = g_ref[g_block // 4, :, columns(lax.rem(g_block, 4))]

            def body(rows):
                for half in range(2):
                    core_out[slot, half, pl.ds(0, rows)] = jnp.dot(
                        at_ref[a_block, 1 - core, half, pl.ds(0, rows)],
                        gradient,
                        preferred_element_type=jnp.float32,
                    ).astype(jnp.bfloat16)
                core_copy(unit, rows).start()
                for half in range(2):
                    partial_own[keep, half, pl.ds(0, rows)] = jnp.dot(
                        at_ref[a_block, core, half, pl.ds(0, rows)],
                        gradient,
                        preferred_element_type=jnp.float32,
                    )

            for_rows(kept, body)

        @pl.when(is_vector)
        def _():
            core_out[slot] = vec_ref[1 - core].astype(jnp.bfloat16)
            core_copy(unit, 256).start()
            partial_own[keep] = vec_ref[core]

    def add_core(unit):
        kept = decode(is_text, unit)[3]
        slot = lax.rem(unit, CORE_SLOTS)
        keep = lax.rem(unit, 2)
        far = lax.rem(unit, X_SLOTS)
        store = lax.rem(unit, own_slots)

        def body(rows):
            core_copy(unit, rows).wait()
            at = pl.ds(0, rows)
            x_out[far, at] = (
                partial_own[keep, 1 - side, at] + core_in[slot, 1 - side, at].astype(jnp.float32)
            ).astype(jnp.bfloat16)
            side_copy(unit, rows).start()
            own[store, at] = partial_own[keep, side, at] + core_in[slot, side, at].astype(
                jnp.float32
            )

        for_rows(kept, body)

    def add_side(unit):
        _, _, out_block, kept = decode(is_text, unit)
        far = lax.rem(unit, X_SLOTS)
        store = lax.rem(unit, own_slots)

        def body(rows):
            side_copy(unit, rows).wait()
            at = pl.ds(0, rows)
            own[store, at] += x_in[far, at].astype(jnp.float32)

        for_rows(kept, body)

        @pl.when((spot + 1) * piece <= kept)
        def _():
            at = pl.ds(pl.multiple_of(spot * piece, piece), piece)
            out_ref[:, columns(out_block)] = own[store, at]

    def line_step(unit, source, target, sems, free, sender, reader, low, high, gives, takes):
        slot = lax.rem(unit + Z_SLOTS, Z_SLOTS)

        @pl.when(jnp.logical_and(unit >= Z_SLOTS, gives))
        def _():
            count = decode(is_text, unit - Z_SLOTS)[3] // piece
            pl.semaphore_wait(free, 1)

            def settle(index, carry):
                line_copy(source, target, sems, reader, slot, index).wait_send()
                return carry

            lax.fori_loop(low(count), high(count), settle, 0)

        @pl.when(unit < total)
        def _():
            _, _, out_block, kept = decode(is_text, unit)
            count = kept // piece
            store = lax.rem(unit, own_slots)

            def at(index):
                return pl.ds(pl.multiple_of(index * piece, piece), piece)

            @pl.when(gives)
            def _():
                def forward(index, carry):
                    @pl.when(takes)
                    def _():
                        line_copy(source, target, sems, reader, slot, index).wait_recv()
                        source[slot, at(index)] = (
                            own[store, at(index)] + target[slot, at(index)].astype(jnp.float32)
                        ).astype(jnp.bfloat16)

                    @pl.when(jnp.logical_not(takes))
                    def _():
                        source[slot, at(index)] = own[store, at(index)].astype(jnp.bfloat16)

                    line_copy(source, target, sems, reader, slot, index).start()
                    return carry

                lax.fori_loop(low(count), high(count), forward, 0)

            @pl.when(takes)
            def _():
                @pl.when(spot < count)
                def _():
                    line_copy(source, target, sems, reader, slot, spot).wait_recv()
                    out_ref[:, columns(out_block)] += target[slot, at(spot)].astype(jnp.float32)

                pl.semaphore_signal(free, inc=1, device_id=sender, device_id_type=MESH)

    def tick(step, carry):
        @pl.when(step < total)
        def _():
            multiply(step)

        @pl.when(jnp.logical_and(step >= 1, step < total + 1))
        def _():
            add_core(step - 1)

        @pl.when(jnp.logical_and(step >= LAG_X, step < total + LAG_X))
        def _():
            add_side(step - LAG_X)

        falling = step - LAG_X - (last - spot) * LAG_Z

        @pl.when(jnp.logical_and(falling >= 0, falling < total + Z_SLOTS))
        def _():
            line_step(
                falling,
                down_out,
                down_in,
                down_sems,
                down_free,
                upper_device,
                lower_device,
                lambda count: 0,
                lambda count: jnp.minimum(spot, count),
                spot > 0,
                spot < last,
            )

        rising = step - LAG_X - spot * LAG_Z

        @pl.when(jnp.logical_and(rising >= 0, rising < total + Z_SLOTS))
        def _():
            line_step(
                rising,
                up_out,
                up_in,
                up_sems,
                up_free,
                lower_device,
                upper_device,
                lambda count: jnp.minimum(spot + 1, count),
                lambda count: count,
                spot < last,
                spot > 0,
            )

        return carry

    lax.fori_loop(0, total + LAG_X + last * LAG_Z + Z_SLOTS, tick, 0)


def reduce_gradients(line, operands, gradients, vectors):
    piece = 256 // line
    own_slots = LAG_X + (line - 1) * LAG_Z + 1
    whole = pl.BlockSpec(memory_space=pltpu.VMEM)
    return pl.pallas_call(
        partial(reduce_kernel, line),
        out_shape=jax.ShapeDtypeStruct((piece, OUT_BLOCKS * UNIT), jnp.float32),
        in_specs=[whole] * 3,
        out_specs=whole,
        scratch_shapes=[
            pltpu.VMEM((CORE_SLOTS, 2, 256, UNIT), jnp.bfloat16),
            pltpu.VMEM((CORE_SLOTS, 2, 256, UNIT), jnp.bfloat16),
            pltpu.VMEM((2, 2, 256, UNIT), jnp.float32),
            pltpu.VMEM((X_SLOTS, 256, UNIT), jnp.bfloat16),
            pltpu.VMEM((X_SLOTS, 256, UNIT), jnp.bfloat16),
            pltpu.VMEM((own_slots, 256, UNIT), jnp.float32),
            pltpu.VMEM((Z_SLOTS, 256, UNIT), jnp.bfloat16),
            pltpu.VMEM((Z_SLOTS, 256, UNIT), jnp.bfloat16),
            pltpu.VMEM((Z_SLOTS, 256, UNIT), jnp.bfloat16),
            pltpu.VMEM((Z_SLOTS, 256, UNIT), jnp.bfloat16),
            pltpu.SemaphoreType.DMA((2, CORE_SLOTS)),
            pltpu.SemaphoreType.DMA((2, X_SLOTS)),
            pltpu.SemaphoreType.DMA((2, Z_SLOTS, line)),
            pltpu.SemaphoreType.DMA((2, Z_SLOTS, line)),
            pltpu.SemaphoreType.REGULAR,
            pltpu.SemaphoreType.REGULAR,
        ],
        compiler_params=pltpu.CompilerParams(
            collective_id=0, has_side_effects=True, vmem_limit_bytes=60 * 1024 * 1024
        ),
        name="reduce_gradients",
    )(operands, gradients, vectors)


def place_rows(array, line):
    lead, count = (array.shape[:-2], array.shape[-1])
    piece = 256 // line
    split = array.reshape(lead + (line, 2, 2, piece, count))
    axis = len(lead)
    order = tuple(range(axis)) + (axis + 2, axis + 1, axis, axis + 3, axis + 4)
    return split.transpose(order).reshape(lead + (2, 2, 256, count))


def operand_rows(array, line):
    turned = widen(array, (array.shape[0], 1024)).T
    return place_rows(turned, line)[None]


def hidden_rows(array, line):
    turned = widen(array, (array.shape[0], 3072)).T
    split = turned.reshape(line * 4, 3, 256 // line, array.shape[0]).transpose(1, 0, 2, 3)
    return place_rows(split.reshape(3, 1024, array.shape[0]), line)


def gradient_columns(array, width):
    filled = widen(array, (array.shape[0], width))
    return filled.reshape(array.shape[0], width // 1024, 1024).transpose(1, 0, 2)


def linear(operand, weight, offset):
    return jnp.dot(operand, weight, preferred_element_type=jnp.float32) + offset.astype(jnp.float32)


def linear_back(operand, weight, grad_low):
    grad_operand = jnp.einsum("ro,io->ri", grad_low, weight, preferred_element_type=jnp.float32)
    return (grad_operand, (operand, grad_low), jnp.sum(grad_low.astype(jnp.float32), axis=0))


def norm_apply_forward(summed, scaling, offset):
    average = jnp.mean(summed, axis=-1, keepdims=True)
    centered = summed - average
    reciprocal = lax.rsqrt(jnp.mean(centered * centered, axis=-1, keepdims=True) + EPSILON)
    normal_rows = centered * reciprocal
    return (normal_rows * scaling + offset, normal_rows, reciprocal)


def norm_backward(gradient_result, normal_rows, reciprocal, scaling):
    scaled = gradient_result * scaling
    grad_in = reciprocal * (
        scaled
        - jnp.mean(scaled, axis=-1, keepdims=True)
        - normal_rows * jnp.mean(scaled * normal_rows, axis=-1, keepdims=True)
    )
    return (
        grad_in,
        jnp.sum(gradient_result * normal_rows, axis=0),
        jnp.sum(gradient_result, axis=0),
    )


def gelu_slope(hidden_in):
    return (
        0.5 * (1.0 + lax.erf(hidden_in * ROOT_HALF))
        + hidden_in * jnp.exp(-0.5 * hidden_in * hidden_in) * GAUSS_NORM
    )


def dense_block_forward(normed, layer, scaling, offset):
    operand = normed.astype(jnp.bfloat16)
    hidden_in = linear(operand, layer[0], layer[1])
    activated = jax.nn.gelu(hidden_in, approximate=False).astype(jnp.bfloat16)
    summed = normed + linear(activated, layer[2], layer[3])
    block_output, normal_rows, reciprocal = norm_apply_forward(summed, scaling, offset)
    return (block_output, (operand, hidden_in, activated, normal_rows, reciprocal))


def dense_block_backward(gradient_result, stored, layer, scaling):
    operand, hidden_in, activated, normal_rows, reciprocal = stored
    grad_summed, scale_grad, shift_grad = norm_backward(
        gradient_result, normal_rows, reciprocal, scaling
    )
    grad_active, down_grad, sink_grad = linear_back(
        activated, layer[2], grad_summed.astype(jnp.bfloat16)
    )
    grad_hidden = (grad_active * gelu_slope(hidden_in)).astype(jnp.bfloat16)
    grad_rows, up_grad, lift_grad = linear_back(operand, layer[0], grad_hidden)
    return (
        grad_summed + grad_rows,
        (up_grad, lift_grad, down_grad, sink_grad, scale_grad, shift_grad),
    )


def split_heads(array, head_count):
    group_pairs, slot_count, model_width = array.shape
    return array.reshape(group_pairs, slot_count, head_count, model_width // head_count)


def masked_scores(query_heads, key_heads, key_valid):
    scale = 1.0 / math.sqrt(query_heads.shape[3])
    scores = (
        jnp.einsum("pqhe,pkhe->phqk", query_heads, key_heads, preferred_element_type=jnp.float32)
        * scale
    )
    return jnp.where(key_valid[:, None, None, :], scores, NEGATIVE)


def attend(query, keys, values, key_valid, head_count):
    query_heads = split_heads(query, head_count)
    scores = masked_scores(query_heads, split_heads(keys, head_count), key_valid)
    maximum = jnp.max(scores, axis=-1, keepdims=True)
    expanded = jnp.exp(scores - maximum)
    totals = jnp.sum(expanded, axis=-1, keepdims=True)
    probability = (expanded / totals).astype(jnp.bfloat16)
    mixture = jnp.einsum(
        "phqk,pkhe->pqhe",
        probability,
        split_heads(values, head_count),
        preferred_element_type=jnp.float32,
    )
    return (mixture.reshape(query.shape), maximum + jnp.log(totals))


def attend_back(query, keys, values, key_valid, head_count, log_total, grad_mixed):
    query_heads = split_heads(query, head_count)
    key_heads = split_heads(keys, head_count)
    grad_heads = split_heads(grad_mixed, head_count)
    scale = 1.0 / math.sqrt(query_heads.shape[3])
    shares = jnp.exp(masked_scores(query_heads, key_heads, key_valid) - log_total)
    probability = shares.astype(jnp.bfloat16)
    grad_values = jnp.einsum(
        "phqk,pqhe->pkhe", probability, grad_heads, preferred_element_type=jnp.float32
    )
    grad_shares = jnp.einsum(
        "pqhe,pkhe->phqk",
        grad_heads,
        split_heads(values, head_count),
        preferred_element_type=jnp.float32,
    )
    grad_scores = (
        shares * (grad_shares - jnp.sum(grad_shares * shares, axis=-1, keepdims=True)) * scale
    ).astype(jnp.bfloat16)
    grad_query = jnp.einsum(
        "phqk,pkhe->pqhe", grad_scores, key_heads, preferred_element_type=jnp.float32
    )
    grad_keys = jnp.einsum(
        "phqk,pqhe->pkhe", grad_scores, query_heads, preferred_element_type=jnp.float32
    )
    return (
        grad_query.reshape(query.shape),
        grad_keys.reshape(keys.shape),
        grad_values.reshape(values.shape),
    )


def cross_inputs(model_width, source, weights):
    co_qkv, proj_bias = (weights[0], weights[6])
    pair_count, slot_count, full_width = source.shape
    co_width = co_qkv.shape[-1]
    rows_in = source.reshape(pair_count * slot_count, full_width)[:, :model_width]
    query = linear(rows_in, co_qkv[0, :model_width], proj_bias[0, 0, :co_width]).astype(
        jnp.bfloat16
    )
    keys = jnp.dot(rows_in, co_qkv[1, :model_width], preferred_element_type=jnp.float32).astype(
        jnp.bfloat16
    )
    values = linear(rows_in, co_qkv[2, :model_width], proj_bias[0, 1, :co_width]).astype(
        jnp.bfloat16
    )
    shaped = (pair_count, slot_count, co_width)
    return (query.reshape(shaped), keys.reshape(shaped), values.reshape(shaped))


def stream_rest(
    line, model_width, inner_width, head_count, source, context, seed_rows, key_valid, weights
):
    (
        co_qkv,
        co_out,
        self_qkv,
        self_out,
        mlp_up,
        mlp_down,
        proj_bias,
        mlp_bias_up,
        mlp_bias_down,
        norm_gain_table,
        norm_bias,
    ) = weights
    pair_count, slot_count, full_width = source.shape
    inner_full = mlp_up.shape[-1]
    co_width = co_out.shape[0]
    row_count = pair_count * slot_count
    rows_in = source.reshape(row_count, full_width)[:, :model_width]
    context_rows = context.reshape(row_count, co_width)
    scale_factors = norm_gain_table[:, :model_width].astype(jnp.float32)
    shift_terms = norm_bias[:, :model_width].astype(jnp.float32)
    out_weight = co_out[:, :model_width]
    total_leading = rows_in.astype(jnp.float32) + linear(
        context_rows, out_weight, proj_bias[0, 2, :model_width]
    )
    first_operand, normalized_leading, inverse_spread_leading = norm_apply_forward(
        total_leading, scale_factors[0], shift_terms[0]
    )
    layer_leading = (
        mlp_up[0, :model_width, :inner_width],
        mlp_bias_up[0, :inner_width],
        mlp_down[0, :inner_width, :model_width],
        mlp_bias_down[0, :model_width],
    )
    middle_operand, retained_leading = dense_block_forward(
        first_operand, layer_leading, scale_factors[1], shift_terms[1]
    )
    normed = middle_operand.astype(jnp.bfloat16)
    query_weight = self_qkv[0, :model_width, :model_width]
    key_weight = self_qkv[1, :model_width, :model_width]
    value_weight = self_qkv[2, :model_width, :model_width]
    query = linear(normed, query_weight, proj_bias[1, 0, :model_width]).astype(jnp.bfloat16)
    keys = jnp.dot(normed, key_weight, preferred_element_type=jnp.float32).astype(jnp.bfloat16)
    values = linear(normed, value_weight, proj_bias[1, 1, :model_width]).astype(jnp.bfloat16)
    shaped = (pair_count, slot_count, model_width)
    mixture, log_total = attend(
        query.reshape(shaped), keys.reshape(shaped), values.reshape(shaped), key_valid, head_count
    )
    mixed_low = mixture.reshape(row_count, model_width).astype(jnp.bfloat16)
    final_weight = self_out[:model_width, :model_width]
    total_trailing = middle_operand + linear(mixed_low, final_weight, proj_bias[1, 2, :model_width])
    trailing_operand, normalized_trailing, inverse_spread_trailing = norm_apply_forward(
        total_trailing, scale_factors[2], shift_terms[2]
    )
    layer_middle = (
        mlp_up[1, :model_width, :inner_width],
        mlp_bias_up[1, :inner_width],
        mlp_down[1, :inner_width, :model_width],
        mlp_bias_down[1, :model_width],
    )
    block_output, retained_middle = dense_block_forward(
        trailing_operand, layer_middle, scale_factors[3], shift_terms[3]
    )
    gradient_result = seed_rows.reshape(row_count, full_width)[:, :model_width].astype(jnp.float32)
    gradient_trailing, middle_gradients = dense_block_backward(
        gradient_result, retained_middle, layer_middle, scale_factors[3]
    )
    grad_summed, scale_two, shift_two = norm_backward(
        gradient_trailing, normalized_trailing, inverse_spread_trailing, scale_factors[2]
    )
    grad_mixed, final_grad, final_bias = linear_back(
        mixed_low, final_weight, grad_summed.astype(jnp.bfloat16)
    )
    grad_mixed = grad_mixed.astype(jnp.bfloat16).reshape(shaped)
    grad_query, grad_keys, grad_values = attend_back(
        query.reshape(shaped),
        keys.reshape(shaped),
        values.reshape(shaped),
        key_valid,
        head_count,
        log_total,
        grad_mixed,
    )
    back_query, query_grad, query_bias = linear_back(
        normed, query_weight, grad_query.reshape(row_count, model_width).astype(jnp.bfloat16)
    )
    back_keys, keys_grad, unused_bias = linear_back(
        normed, key_weight, grad_keys.reshape(row_count, model_width).astype(jnp.bfloat16)
    )
    back_values, values_grad, values_bias = linear_back(
        normed, value_weight, grad_values.reshape(row_count, model_width).astype(jnp.bfloat16)
    )
    gradient_middle = grad_summed + back_query + back_keys + back_values
    gradient_leading, leading_gradients = dense_block_backward(
        gradient_middle, retained_leading, layer_leading, scale_factors[1]
    )
    grad_resid, scale_zero, shift_zero = norm_backward(
        gradient_leading, normalized_leading, inverse_spread_leading, scale_factors[0]
    )
    grad_context, out_grad, out_bias = linear_back(
        context_rows, out_weight, grad_resid.astype(jnp.bfloat16)
    )
    operands = jnp.concatenate(
        [
            operand_rows(context_rows, line),
            operand_rows(normed, line),
            operand_rows(mixed_low, line),
            operand_rows(leading_gradients[0][0], line),
            operand_rows(middle_gradients[0][0], line),
            hidden_rows(leading_gradients[2][0], line),
            hidden_rows(middle_gradients[2][0], line),
        ]
    )
    gradients = jnp.concatenate(
        [
            gradient_columns(out_grad[1], full_width),
            gradient_columns(query_grad[1], full_width),
            gradient_columns(keys_grad[1], full_width),
            gradient_columns(values_grad[1], full_width),
            gradient_columns(final_grad[1], full_width),
            gradient_columns(leading_gradients[0][1], inner_full),
            gradient_columns(middle_gradients[0][1], inner_full),
            gradient_columns(leading_gradients[2][1], full_width),
            gradient_columns(middle_gradients[2][1], full_width),
        ]
    )

    def hidden_vector(vector):
        return widen(vector, (inner_full,)).reshape(4 * line, 3, -1).transpose(1, 0, 2).reshape(3, -1)

    def plain_vectors(*vectors):
        return widen(jnp.stack(vectors), (len(vectors), full_width))

    vectors = jnp.concatenate(
        [
            plain_vectors(out_bias, query_bias, values_bias, final_bias),
            hidden_vector(leading_gradients[1]),
            hidden_vector(middle_gradients[1]),
            plain_vectors(
                leading_gradients[3],
                middle_gradients[3],
                scale_zero,
                leading_gradients[4],
                scale_two,
                middle_gradients[4],
                shift_zero,
                leading_gradients[5],
                shift_two,
                middle_gradients[5],
            ),
        ]
    )
    output_rows = (
        widen(block_output, (row_count, full_width))
        .reshape(pair_count, slot_count, full_width)
        .astype(jnp.bfloat16)
    )
    return (
        output_rows,
        grad_context.astype(jnp.bfloat16).reshape(pair_count, slot_count, co_width),
        widen(grad_resid, (row_count, full_width)),
        operands,
        gradients,
        vectors,
    )


def cross_back(model_width, source, query_low, keys_low, values_low, grad_resid, weights):
    co_qkv = weights[0]
    pair_count, slot_count, full_width = source.shape
    co_width = co_qkv.shape[-1]
    row_count = pair_count * slot_count
    rows_in = source.reshape(row_count, full_width)[:, :model_width]
    back_query, query_grad, query_bias = linear_back(
        rows_in, co_qkv[0, :model_width], query_low.reshape(row_count, co_width)
    )
    back_keys, keys_grad, unused_bias = linear_back(
        rows_in, co_qkv[1, :model_width], keys_low.reshape(row_count, co_width)
    )
    back_values, values_grad, values_bias = linear_back(
        rows_in, co_qkv[2, :model_width], values_low.reshape(row_count, co_width)
    )
    grad_input = grad_resid + widen(back_query + back_keys + back_values, (row_count, full_width))
    gradients = jnp.stack([query_grad[1], keys_grad[1], values_grad[1]])
    pair_bias = widen(jnp.stack([query_bias, values_bias]), (2, full_width))
    return (
        grad_input.reshape(pair_count, slot_count, full_width).astype(jnp.bfloat16),
        gradients,
        pair_bias,
    )


def on_device(
    hidden,
    text_lengths,
    region_counts,
    co_qkv,
    co_out,
    self_qkv,
    self_out,
    mlp_up,
    mlp_down,
    proj_bias,
    mlp_bias_up,
    mlp_bias_down,
    norm_gain_table,
    norm_bias,
    cotangent,
):
    is_text = lax.axis_index("stream") == 0
    weights = tuple(
        (
            member[0]
            for member in (
                co_qkv,
                co_out,
                self_qkv,
                self_out,
                mlp_up,
                mlp_down,
                proj_bias,
                mlp_bias_up,
                mlp_bias_down,
                norm_gain_table,
                norm_bias,
            )
        )
    )
    source = hidden[0]
    seed_rows = cotangent[0]
    positions = jnp.arange(source.shape[1], dtype=jnp.int32)
    text_valid = positions[None, :] < text_lengths[:, None]
    image_valid = positions[None, :] < region_counts[:, None]
    own_valid = jnp.where(is_text, text_valid, image_valid)
    other_valid = jnp.where(is_text, image_valid, text_valid)
    query, keys, values = lax.cond(
        is_text,
        partial(cross_inputs, DT, source, weights),
        partial(cross_inputs, DV, source, weights),
    )
    far_keys, far_values = from_partner((keys, values), "stream", 0)
    context, context_total = attend(query, far_keys, far_values, other_valid, CO_HEADS)
    context_low = context.astype(jnp.bfloat16)
    line = lax.axis_size("dp") // 4
    block_output, grad_context, grad_resid, operands, gradients, vectors = lax.cond(
        is_text,
        partial(
            stream_rest, line, DT, FT, TEXT_HEADS, source, context_low, seed_rows, own_valid, weights
        ),
        partial(
            stream_rest, line, DV, FV, IMAGE_HEADS, source, context_low, seed_rows, own_valid, weights
        ),
    )
    grad_query, grad_keys, grad_values = attend_back(
        query, far_keys, far_values, other_valid, CO_HEADS, context_total, grad_context
    )
    back_keys, back_values = from_partner(
        (grad_keys.astype(jnp.bfloat16), grad_values.astype(jnp.bfloat16)), "stream", 0
    )
    query_low = grad_query.astype(jnp.bfloat16)
    grad_input, cross_gradients, pair_bias = lax.cond(
        is_text,
        partial(cross_back, DT, source, query_low, back_keys, back_values, grad_resid, weights),
        partial(cross_back, DV, source, query_low, back_keys, back_values, grad_resid, weights),
    )
    all_operands = jnp.concatenate(
        [operand_rows(source.reshape(-1, source.shape[-1]), line), operands]
    )
    all_gradients = jnp.concatenate([cross_gradients, gradients])
    all_vectors = widen(jnp.concatenate([pair_bias, vectors]), (UNIT, 1024))
    vector_rows = place_rows(all_vectors.T, line)
    summed = reduce_gradients(line, all_operands, all_gradients, vector_rows)
    piece = summed.shape[0]

    def parts(first, count):
        block = summed[:, first * UNIT : (first + count * 4) * UNIT]
        return block.reshape(piece, count, 1024).transpose(1, 0, 2)

    vector_sums = summed[:, 80 * UNIT : 80 * UNIT + 22].T
    return (
        block_output[None],
        grad_input[None],
        parts(0, 3)[None],
        parts(12, 1),
        parts(16, 3)[None],
        parts(28, 1),
        jnp.stack([summed[:, 32 * UNIT : 44 * UNIT], summed[:, 44 * UNIT : 56 * UNIT]])[None],
        jnp.stack([parts(56, 3).reshape(3 * piece, 1024), parts(68, 3).reshape(3 * piece, 1024)])[
            None
        ],
        vector_sums[:6].reshape(1, 2, 3, piece),
        vector_sums[6:12].reshape(1, 2, 3 * piece),
        vector_sums[12:14][None],
        vector_sums[14:18][None],
        vector_sums[18:22][None],
    )


def solution(mesh):
    return jax.shard_map(
        on_device,
        mesh=mesh,
        in_specs=(
            P("stream", "dp", None, None),
            P("dp"),
            P("dp"),
            P("stream", None, None, None),
            P("stream", None, None),
            P("stream", None, None, None),
            P("stream", None, None),
            P("stream", None, None, None),
            P("stream", None, None, None),
            P("stream", None, None, None),
            P("stream", None, None),
            P("stream", None, None),
            P("stream", None, None),
            P("stream", None, None),
            P("stream", "dp", None, None),
        ),
        out_specs=(
            P("stream", "dp", None, None),
            P("stream", "dp", None, None),
            P("stream", None, "dp", None),
            P("stream", "dp", None),
            P("stream", None, "dp", None),
            P("stream", "dp", None),
            P("stream", None, "dp", None),
            P("stream", None, "dp", None),
            P("stream", None, None, "dp"),
            P("stream", None, "dp"),
            P("stream", None, "dp"),
            P("stream", None, "dp"),
            P("stream", None, "dp"),
        ),
        check_vma=False,
    )
```

```python
from functools import partial
from typing import NamedTuple
import math

import jax
import jax.numpy as jnp
from jax import lax
from jax.experimental import pallas as pl
from jax.experimental.pallas import tpu as pltpu
from jax.sharding import PartitionSpec as P

EPSILON = 1e-05
NEGATIVE = -1000000000.0
ROOT_HALF = 1.0 / math.sqrt(2.0)
GAUSS_NORM = 1.0 / math.sqrt(2.0 * math.pi)

MESH = pl.DeviceIdType.MESH
UNIT = 256
OUT_BLOCKS = 81
CORE_SLOTS = 4
LAG_X = 4
X_SLOTS = 2 * LAG_X
LAG_Z = 2
Z_SLOTS = 4

TEXT_UNITS = (
    (3, 3, 9, 1, 60, 0, 68, 4, 256),
    (1, 12, 5, 0, 44, 0, 44, 0, 192),
    (1, 3, 3, 0, 28, 0, 28, 0, 192),
    (3, 3, 2, 0, 16, 4, 16, 4, 192),
    (3, 3, 6, 1, 56, 0, 56, 4, 256),
    (1, 12, 4, 0, 32, 0, 32, 0, 192),
    (1, 3, 1, 0, 12, 0, 12, 0, 256),
    (3, 4, 0, 0, 0, 4, 0, 4, 192),
    (1, 1, 0, 0, 0, 0, 80, 0, 256),
)
IMAGE_UNITS = (
    (3, 4, 9, 1, 60, 0, 68, 4, 128),
    (1, 4, 5, 0, 44, 0, 44, 0, 256),
    (1, 4, 3, 0, 28, 0, 28, 0, 256),
    (3, 4, 2, 0, 16, 4, 16, 4, 256),
    (3, 4, 6, 1, 56, 0, 56, 4, 128),
    (1, 4, 4, 0, 32, 0, 32, 0, 256),
    (1, 4, 1, 0, 12, 0, 12, 0, 256),
    (3, 4, 0, 0, 0, 4, 0, 4, 256),
    (1, 1, 0, 0, 0, 0, 80, 0, 256),
)


def unit_count(table):
    return sum(entry[0] * entry[1] for entry in table)


def decode_one(table, unit):
    start = 0
    result = None
    for groups, blocks, a0, a1, g0, g1, o0, o1, kept in table:
        local = unit - start
        group = local // blocks
        block = local % blocks
        fields = (a0 + a1 * group, g0 + g1 * group + block, o0 + o1 * group + block, jnp.int32(kept))
        if result is None:
            result = fields
        else:
            result = tuple(jnp.where(unit >= start, new, old) for new, old in zip(fields, result))
        start += groups * blocks
    return result


def decode(is_text, unit):
    text = decode_one(TEXT_UNITS, unit)
    image = decode_one(IMAGE_UNITS, unit)
    return tuple(jnp.where(is_text, one, other) for one, other in zip(text, image))


def reduce_kernel(
    line,
    at_ref,
    g_ref,
    vec_ref,
    out_ref,
    core_out,
    core_in,
    partial_own,
    x_out,
    x_in,
    own,
    down_out,
    down_in,
    up_out,
    up_in,
    core_sems,
    x_sems,
    down_sems,
    up_sems,
    down_free,
    up_free,
):
    piece = 256 // line
    stream = lax.axis_index("stream")
    place = lax.axis_index("dp")
    core = lax.rem(place, 2)
    side = lax.rem(place // 2, 2)
    spot = place // 4
    is_text = stream == 0
    total = jnp.where(is_text, unit_count(TEXT_UNITS), unit_count(IMAGE_UNITS))
    core_device = (stream, place + 1 - 2 * core)
    side_device = (stream, place + 2 - 4 * side)
    lower_device = (stream, place - 4)
    upper_device = (stream, place + 4)
    own_slots = LAG_X + (line - 1) * LAG_Z + 1
    last = line - 1

    barrier = pltpu.get_barrier_semaphore()
    pl.semaphore_signal(barrier, inc=1, device_id=core_device, device_id_type=MESH)
    pl.semaphore_signal(barrier, inc=1, device_id=side_device, device_id_type=MESH)

    @pl.when(spot > 0)
    def _():
        pl.semaphore_signal(barrier, inc=1, device_id=lower_device, device_id_type=MESH)

    @pl.when(spot < last)
    def _():
        pl.semaphore_signal(barrier, inc=1, device_id=upper_device, device_id_type=MESH)

    pl.semaphore_wait(
        barrier, 2 + (spot > 0).astype(jnp.int32) + (spot < last).astype(jnp.int32)
    )
    out_ref[...] = jnp.zeros_like(out_ref)

    def for_rows(kept, body):
        for rows in (128, 192, 256):

            @pl.when(kept == rows)
            def _():
                body(rows)

    def core_copy(unit, rows):
        slot = lax.rem(unit, CORE_SLOTS)
        return pltpu.make_async_remote_copy(
            src_ref=core_out.at[slot, :, pl.ds(0, rows)],
            dst_ref=core_in.at[slot, :, pl.ds(0, rows)],
            send_sem=core_sems.at[0, slot],
            recv_sem=core_sems.at[1, slot],
            device_id=core_device,
            device_id_type=MESH,
        )

    def side_copy(unit, rows):
        slot = lax.rem(unit, X_SLOTS)
        return pltpu.make_async_remote_copy(
            src_ref=x_out.at[slot, pl.ds(0, rows)],
            dst_ref=x_in.at[slot, pl.ds(0, rows)],
            send_sem=x_sems.at[0, slot],
            recv_sem=x_sems.at[1, slot],
            device_id=side_device,
            device_id_type=MESH,
        )

    def line_copy(source, target, sems, device, slot, index):
        at = pl.ds(pl.multiple_of(index * piece, piece), piece)
        return pltpu.make_async_remote_copy(
            src_ref=source.at[slot, at],
            dst_ref=target.at[slot, at],
            send_sem=sems.at[0, slot, index],
            recv_sem=sems.at[1, slot, index],
            device_id=device,
            device_id_type=MESH,
        )

    def columns(block):
        return pl.ds(pl.multiple_of(block * UNIT, UNIT), UNIT)

    def multiply(unit):
        a_block, g_block, out_block, kept = decode(is_text, unit)
        slot = lax.rem(unit, CORE_SLOTS)
        keep = lax.rem(unit, 2)
        is_vector = unit == total - 1

        @pl.when(jnp.logical_not(is_vector))
        def _():
            gradient = g_ref[g_block // 4, :, columns(lax.rem(g_block, 4))]

            def body(rows):
                for half in range(2):
                    core_out[slot, half, pl.ds(0, rows)] = jnp.dot(
                        at_ref[a_block, 1 - core, half, pl.ds(0, rows)],
                        gradient,
                        preferred_element_type=jnp.float32,
                    ).astype(jnp.bfloat16)
                core_copy(unit, rows).start()
                for half in range(2):
                    partial_own[keep, half, pl.ds(0, rows)] = jnp.dot(
                        at_ref[a_block, core, half, pl.ds(0, rows)],
                        gradient,
                        preferred_element_type=jnp.float32,
                    )

            for_rows(kept, body)

        @pl.when(is_vector)
        def _():
            core_out[slot] = vec_ref[1 - core].astype(jnp.bfloat16)
            core_copy(unit, 256).start()
            partial_own[keep] = vec_ref[core]

    def add_core(unit):
        kept = decode(is_text, unit)[3]
        slot = lax.rem(unit, CORE_SLOTS)
        keep = lax.rem(unit, 2)
        far = lax.rem(unit, X_SLOTS)
        store = lax.rem(unit, own_slots)

        def body(rows):
            core_copy(unit, rows).wait()
            at = pl.ds(0, rows)
            x_out[far, at] = (
                partial_own[keep, 1 - side, at] + core_in[slot, 1 - side, at].astype(jnp.float32)
            ).astype(jnp.bfloat16)
            side_copy(unit, rows).start()
            own[store, at] = partial_own[keep, side, at] + core_in[slot, side, at].astype(
                jnp.float32
            )

        for_rows(kept, body)

    def add_side(unit):
        _, _, out_block, kept = decode(is_text, unit)
        far = lax.rem(unit, X_SLOTS)
        store = lax.rem(unit, own_slots)

        def body(rows):
            side_copy(unit, rows).wait()
            at = pl.ds(0, rows)
            own[store, at] += x_in[far, at].astype(jnp.float32)

        for_rows(kept, body)

        @pl.when((spot + 1) * piece <= kept)
        def _():
            at = pl.ds(pl.multiple_of(spot * piece, piece), piece)
            out_ref[:, columns(out_block)] = own[store, at]

    def line_step(unit, source, target, sems, free, sender, reader, low, high, gives, takes):
        slot = lax.rem(unit + Z_SLOTS, Z_SLOTS)

        @pl.when(jnp.logical_and(unit >= Z_SLOTS, gives))
        def _():
            count = decode(is_text, unit - Z_SLOTS)[3] // piece
            pl.semaphore_wait(free, 1)

            def settle(index, carry):
                line_copy(source, target, sems, reader, slot, index).wait_send()
                return carry

            lax.fori_loop(low(count), high(count), settle, 0)

        @pl.when(unit < total)
        def _():
            _, _, out_block, kept = decode(is_text, unit)
            count = kept // piece
            store = lax.rem(unit, own_slots)

            def at(index):
                return pl.ds(pl.multiple_of(index * piece, piece), piece)

            @pl.when(gives)
            def _():
                def forward(index, carry):
                    @pl.when(takes)
                    def _():
                        line_copy(source, target, sems, reader, slot, index).wait_recv()
                        source[slot, at(index)] = (
                            own[store, at(index)] + target[slot, at(index)].astype(jnp.float32)
                        ).astype(jnp.bfloat16)

                    @pl.when(jnp.logical_not(takes))
                    def _():
                        source[slot, at(index)] = own[store, at(index)].astype(jnp.bfloat16)

                    line_copy(source, target, sems, reader, slot, index).start()
                    return carry

                lax.fori_loop(low(count), high(count), forward, 0)

            @pl.when(takes)
            def _():
                @pl.when(spot < count)
                def _():
                    line_copy(source, target, sems, reader, slot, spot).wait_recv()
                    out_ref[:, columns(out_block)] += target[slot, at(spot)].astype(jnp.float32)

                pl.semaphore_signal(free, inc=1, device_id=sender, device_id_type=MESH)

    def tick(step, carry):
        @pl.when(step < total)
        def _():
            multiply(step)

        @pl.when(jnp.logical_and(step >= 1, step < total + 1))
        def _():
            add_core(step - 1)

        @pl.when(jnp.logical_and(step >= LAG_X, step < total + LAG_X))
        def _():
            add_side(step - LAG_X)

        falling = step - LAG_X - (last - spot) * LAG_Z

        @pl.when(jnp.logical_and(falling >= 0, falling < total + Z_SLOTS))
        def _():
            line_step(
                falling,
                down_out,
                down_in,
                down_sems,
                down_free,
                upper_device,
                lower_device,
                lambda count: 0,
                lambda count: jnp.minimum(spot, count),
                spot > 0,
                spot < last,
            )

        rising = step - LAG_X - spot * LAG_Z

        @pl.when(jnp.logical_and(rising >= 0, rising < total + Z_SLOTS))
        def _():
            line_step(
                rising,
                up_out,
                up_in,
                up_sems,
                up_free,
                lower_device,
                upper_device,
                lambda count: jnp.minimum(spot + 1, count),
                lambda count: count,
                spot < last,
                spot > 0,
            )

        return carry

    lax.fori_loop(0, total + LAG_X + last * LAG_Z + Z_SLOTS, tick, 0)


def reduce_gradients(line, operands, gradients, vectors):
    piece = 256 // line
    own_slots = LAG_X + (line - 1) * LAG_Z + 1
    whole = pl.BlockSpec(memory_space=pltpu.VMEM)
    return pl.pallas_call(
        partial(reduce_kernel, line),
        out_shape=jax.ShapeDtypeStruct((piece, OUT_BLOCKS * UNIT), jnp.float32),
        in_specs=[whole] * 3,
        out_specs=whole,
        scratch_shapes=[
            pltpu.VMEM((CORE_SLOTS, 2, 256, UNIT), jnp.bfloat16),
            pltpu.VMEM((CORE_SLOTS, 2, 256, UNIT), jnp.bfloat16),
            pltpu.VMEM((2, 2, 256, UNIT), jnp.float32),
            pltpu.VMEM((X_SLOTS, 256, UNIT), jnp.bfloat16),
            pltpu.VMEM((X_SLOTS, 256, UNIT), jnp.bfloat16),
            pltpu.VMEM((own_slots, 256, UNIT), jnp.float32),
            pltpu.VMEM((Z_SLOTS, 256, UNIT), jnp.bfloat16),
            pltpu.VMEM((Z_SLOTS, 256, UNIT), jnp.bfloat16),
            pltpu.VMEM((Z_SLOTS, 256, UNIT), jnp.bfloat16),
            pltpu.VMEM((Z_SLOTS, 256, UNIT), jnp.bfloat16),
            pltpu.SemaphoreType.DMA((2, CORE_SLOTS)),
            pltpu.SemaphoreType.DMA((2, X_SLOTS)),
            pltpu.SemaphoreType.DMA((2, Z_SLOTS, line)),
            pltpu.SemaphoreType.DMA((2, Z_SLOTS, line)),
            pltpu.SemaphoreType.REGULAR,
            pltpu.SemaphoreType.REGULAR,
        ],
        compiler_params=pltpu.CompilerParams(
            collective_id=0, has_side_effects=True, vmem_limit_bytes=60 * 1024 * 1024
        ),
        name="reduce_gradients",
    )(operands, gradients, vectors)


def place_rows(array, line):
    lead, count = (array.shape[:-2], array.shape[-1])
    piece = 256 // line
    split = array.reshape(lead + (line, 2, 2, piece, count))
    axis = len(lead)
    order = tuple(range(axis)) + (axis + 2, axis + 1, axis, axis + 3, axis + 4)
    return split.transpose(order).reshape(lead + (2, 2, 256, count))


def widen(array, target):
    return jnp.pad(array, [(0, wanted - current) for current, wanted in zip(array.shape, target)])


class Stream(NamedTuple):
    width: int
    inner: int
    split: int
    head: int
    own_keys: int
    far_keys: int


TEXT = Stream(768, 3072, 2, 64, 64, 112)
IMAGE = Stream(1024, 1024, 1, 128, 112, 64)
RING = 4
LANES = 128
TAIL = (
    0.28208317669832234,
    0.2824362970929616,
    0.24263030272423752,
    0.20467309203585946,
    -0.03157028123874516,
    0.28558060664263174,
    -0.4940359058844012,
    0.2879944144937219,
    -0.0597917499304742,
)


def gelu_parts(value):
    root = jnp.abs(value) * ROOT_HALF
    near = 1.0 / (1.0 + 0.5 * root)
    bell = jnp.exp(-(root * root))
    series = TAIL[-1] * near
    for factor in TAIL[-2::-1]:
        series = (series + factor) * near
    tail = 0.5 * bell * series
    below = jnp.where(value >= 0.0, 1.0 - tail, tail)
    return value * below, below + value * bell * GAUSS_NORM


def layer_kernel(
    line,
    pairs,
    slots,
    tall,
    text_lengths,
    region_counts,
    hidden_ref,
    cotangent_ref,
    co_qkv,
    co_out,
    self_qkv,
    self_out,
    mlp_up,
    mlp_down,
    proj_bias,
    bias_up,
    bias_down,
    gain,
    shift,
    result_ref,
    grad_ref,
    at_ref,
    g_ref,
    vec_ref,
    hidden_vec_ref,
    ring,
    far_keys,
    far_values,
    state,
    total,
    low,
    active,
    normal,
    spread,
    self_probs,
    co_probs,
    params,
    up_params,
    ring_sems,
    send_sems,
    recv_sems,
    back_send_sems,
    back_recv_sems,
    landing_free,
):
    stream = lax.axis_index("stream")
    place = lax.axis_index("dp")
    partner = (1 - stream, place)
    height = pairs * tall
    piece = 256 // line
    per_block = 256 // piece

    barrier = pltpu.get_barrier_semaphore()
    pl.semaphore_signal(barrier, inc=1, device_id=partner, device_id_type=MESH)
    pl.semaphore_wait(barrier, 1)

    params[0:6] = proj_bias[...].astype(jnp.float32)
    params[6:8] = bias_down[...].astype(jnp.float32)
    params[8:12] = gain[...].astype(jnp.float32)
    params[12:16] = shift[...].astype(jnp.float32)
    up_params[0:2] = bias_up[...].astype(jnp.float32)
    vec_ref[...] = jnp.zeros_like(vec_ref)
    hidden_vec_ref[...] = jnp.zeros_like(hidden_vec_ref)

    def block(index):
        return pl.ds(pl.multiple_of(index * UNIT, UNIT), UNIT)

    def pair_rows(pair, count=tall):
        return pl.ds(pl.multiple_of(pair * tall, tall), count)

    def exchange(sources, targets, sends, receives, which, pair, count):
        return pltpu.make_async_remote_copy(
            src_ref=sources[which].at[pair_rows(pair, count)],
            dst_ref=targets[which].at[pair_rows(pair, count)],
            send_sem=sends.at[which, pair],
            recv_sem=receives.at[which, pair],
            device_id=partner,
            device_id_type=MESH,
        )

    def run(cfg, own_lengths, far_lengths):
        width, inner = cfg.width, cfg.inner
        chunks = inner // 1024
        groups = width // LANES

        plan = [co_qkv.at[index, pl.ds(0, width)] for index in (1, 2, 0)]
        plan.append(co_out.at[:, pl.ds(0, width)])

        def mlp_plan(index, chunk):
            at = pl.ds(chunk * 1024, 1024)
            return mlp_up.at[index, pl.ds(0, width), at], mlp_down.at[index, at, pl.ds(0, width)]

        def square(index):
            return self_qkv.at[index, pl.ds(0, width), pl.ds(0, width)]

        for chunk in range(chunks):
            plan.extend(mlp_plan(0, chunk))
        plan.extend(square(index) for index in range(3))
        plan.append(self_out.at[pl.ds(0, width), pl.ds(0, width)])
        for chunk in range(chunks):
            plan.extend(mlp_plan(1, chunk))
        for chunk in range(chunks):
            plan.extend(mlp_plan(1, chunk)[::-1])
        plan.append(self_out.at[pl.ds(0, width), pl.ds(0, width)])
        plan.extend(square(index) for index in range(3))
        for chunk in range(chunks):
            plan.extend(mlp_plan(0, chunk)[::-1])
        plan.append(co_out.at[:, pl.ds(0, width)])
        plan.extend(co_qkv.at[index, pl.ds(0, width)] for index in range(3))

        def fetch(index):
            rows, columns = plan[index].shape
            return pltpu.make_async_copy(
                plan[index],
                ring.at[index % RING, pl.ds(0, rows), pl.ds(0, columns)],
                ring_sems.at[index % RING],
            )

        used = [0]
        for index in range(RING):
            fetch(index).start()

        def with_weight(body):
            index = used[0]
            used[0] += 1
            fetch(index).wait()
            rows, columns = plan[index].shape
            body(ring.at[index % RING], rows, columns)
            if index + RING < len(plan):
                fetch(index + RING).start()

        def forward_product(source, consume):
            def body(weight, rows, columns):
                def step(index, carry):
                    consume(
                        index,
                        jnp.dot(
                            source[:, 0:rows],
                            weight[0:rows, block(index)],
                            preferred_element_type=jnp.float32,
                        ),
                    )
                    return carry

                lax.fori_loop(0, columns // UNIT, step, 0)

            with_weight(body)

        def backward_product(source, consume):
            def body(weight, rows, columns):
                def step(index, carry):
                    consume(
                        index,
                        lax.dot_general(
                            source[:, 0:columns],
                            weight[block(index), 0:columns],
                            (((1,), (1,)), ((), ())),
                            preferred_element_type=jnp.float32,
                        ),
                    )
                    return carry

                lax.fori_loop(0, rows // UNIT, step, 0)

            with_weight(body)

        def add_total(first):
            def consume(index, value):
                if first:
                    total[:, block(index)] = value
                else:
                    total[:, block(index)] += value

            return consume

        def put_rows(at_block, index, value):
            turned = value.T
            for part in range(per_block):
                at_ref[
                    at_block,
                    part % 2,
                    (part // 2) % 2,
                    pl.ds(pl.multiple_of((index * (per_block // 4) + part // 4) * piece, piece), piece),
                ] = turned[part * piece : (part + 1) * piece]

        def put_hidden_rows(at_block, index, value):
            turned = value.T
            for part in range(per_block):
                number = index * per_block + part
                owner = number // 3
                at_ref[
                    at_block + lax.rem(number, 3),
                    lax.rem(owner, 2),
                    lax.rem(owner // 2, 2),
                    pl.ds(pl.multiple_of((owner // 4) * piece, piece), piece),
                ] = turned[part * piece : (part + 1) * piece]

        def put_low(at_block, columns):
            def step(index, carry):
                put_rows(at_block, index, low[:, block(index)])
                return carry

            lax.fori_loop(0, columns // UNIT, step, 0)

        def for_pairs(body):
            def step(pair, carry):
                body(pair)
                return carry

            lax.fori_loop(0, pairs, step, 0)

        def mean(value):
            return jnp.sum(value, axis=-1, keepdims=True) * (1.0 / width)

        def normalize(value):
            centered = value - mean(value)
            inverse = lax.rsqrt(mean(centered * centered) + EPSILON)
            return centered * inverse, inverse

        def norm_forward(index, bias_row, at_block):
            def body(pair):
                at = pair_rows(pair)
                rows, inverse = normalize(
                    state[at, 0:width] + total[at, 0:width] + params[bias_row : bias_row + 1, 0:width]
                )
                result = (
                    rows * params[8 + index : 9 + index, 0:width]
                    + params[12 + index : 13 + index, 0:width]
                )
                state[at, 0:width] = result
                low[at, 0:width] = result.astype(jnp.bfloat16)
                normal[index, at, 0:width] = rows.astype(jnp.bfloat16)
                spread[index, at] = inverse

            for_pairs(body)
            put_low(at_block, width)

        def add_row(ref, row, value):
            ref[row : row + 1, 0 : value.shape[-1]] += jnp.sum(value, axis=0, keepdims=True)

        def norm_gradient(index, at, gradient, rows, inverse, g_block, bias_row):
            scaled = gradient * params[8 + index : 9 + index, 0:width]
            result = inverse * (scaled - mean(scaled) - rows * mean(scaled * rows))
            state[at, 0:width] = result
            rounded = result.astype(jnp.bfloat16)
            g_ref[g_block, at, 0:width] = rounded
            add_row(vec_ref, 8 + index, gradient * rows)
            add_row(vec_ref, 12 + index, gradient)
            add_row(vec_ref, bias_row, rounded.astype(jnp.float32))

        def norm_backward(index, g_block, bias_row):
            def body(pair):
                at = pair_rows(pair)
                norm_gradient(
                    index,
                    at,
                    state[at, 0:width] + total[at, 0:width],
                    normal[index, at, 0:width].astype(jnp.float32),
                    spread[index, at],
                    g_block,
                    bias_row,
                )

            for_pairs(body)

        def mlp_forward(index):
            for chunk in range(chunks):

                def activate(number, value):
                    act, slope = gelu_parts(
                        value
                        + up_params[
                            index : index + 1,
                            pl.ds(pl.multiple_of(chunk * 1024 + number * UNIT, UNIT), UNIT),
                        ]
                    )
                    act = act.astype(jnp.bfloat16)
                    active[:, block(number)] = act
                    g_ref[8 + 3 * index + chunk, :, block(number)] = slope.astype(jnp.bfloat16)
                    put_hidden_rows(6 + 3 * index, chunk * 4 + number, act)

                forward_product(low, activate)
                forward_product(active, add_total(chunk == 0))

        def mlp_backward(index):
            for chunk in range(chunks):
                g_block = 8 + 3 * index + chunk

                def through(number, value):
                    slope = g_ref[g_block, :, block(number)].astype(jnp.float32)
                    rounded = (value * slope).astype(jnp.bfloat16)
                    g_ref[g_block, :, block(number)] = rounded
                    hidden_vec_ref[
                        index : index + 1,
                        pl.ds(pl.multiple_of(chunk * 1024 + number * UNIT, UNIT), UNIT),
                    ] = jnp.sum(rounded.astype(jnp.float32), axis=0, keepdims=True)

                backward_product(g_ref.at[14 + index], through)
                backward_product(g_ref.at[g_block], add_total(chunk == 0))

        def biased(target, bias_row):
            def consume(index, value):
                if bias_row is not None:
                    value = value + params[bias_row : bias_row + 1, block(index)]
                target[:, block(index)] = value.astype(jnp.bfloat16)

            return consume

        def column_sums(g_block, row, columns):
            def step(index, carry):
                vec_ref[row : row + 1, block(index)] = jnp.sum(
                    g_ref[g_block, :, block(index)].astype(jnp.float32), axis=0, keepdims=True
                )
                return carry

            lax.fori_loop(0, columns // UNIT, step, 0)

        def stacked(value, split):
            if split == 1:
                return value
            lane = lax.broadcasted_iota(jnp.int32, value.shape, 1)
            zero = jnp.zeros_like(value)
            return jnp.concatenate(
                [jnp.where(lane < 64, value, zero), jnp.where(lane < 64, zero, value)], axis=0
            )

        def unstacked(value, split):
            if split == 1:
                return value
            half = value.shape[0] // 2
            lane = lax.broadcasted_iota(jnp.int32, (half, LANES), 1)
            return jnp.where(lane < 64, value[:half], value[half:])

        def over_keys(reduce, value, split):
            if split == 1:
                return reduce(value, axis=0, keepdims=True)
            half = value.shape[0] // 2
            return jnp.concatenate(
                [
                    jnp.broadcast_to(
                        reduce(part, axis=0, keepdims=True), part.shape
                    )
                    for part in (value[:half], value[half:])
                ],
                axis=0,
            )

        last_last = (((1,), (1,)), ((), ()))
        first_first = (((0,), (0,)), ((), ()))

        def attend_forward(query, keys, values, probs, lengths, count, split, head, group_count):
            scale = 1.0 / math.sqrt(head)

            def body(pair):
                length = lengths[pair]
                for group in range(group_count):
                    at = pl.ds(group * LANES, LANES)
                    key = stacked(keys[pair_rows(pair, count), at], split)
                    value = stacked(values[pair_rows(pair, count), at], split)
                    scores = (
                        lax.dot_general(
                            key,
                            query[pair_rows(pair), at],
                            last_last,
                            preferred_element_type=jnp.float32,
                        )
                        * scale
                    )
                    number = lax.broadcasted_iota(jnp.int32, scores.shape, 0)
                    if split == 2:
                        number = jnp.where(number < count, number, number - count)
                    scores = jnp.where(number < length, scores, NEGATIVE)
                    raised = jnp.exp(scores - over_keys(jnp.max, scores, split))
                    shares = raised * (1.0 / over_keys(jnp.sum, raised, split))
                    probs[pair, group, 0 : count * split] = shares
                    low[pair_rows(pair), at] = lax.dot_general(
                        shares.astype(jnp.bfloat16),
                        value,
                        first_first,
                        preferred_element_type=jnp.float32,
                    ).astype(jnp.bfloat16)

            for_pairs(body)

        def attend_backward(query, keys, values, probs, count, split, head, group_count):
            scale = 1.0 / math.sqrt(head)

            def body(pair):
                for group in range(group_count):
                    at = pl.ds(group * LANES, LANES)
                    key = stacked(keys[pair_rows(pair, count), at], split)
                    value = stacked(values[pair_rows(pair, count), at], split)
                    asked = query[pair_rows(pair), at]
                    gradient = low[pair_rows(pair), at]
                    shares = probs[pair, group, 0 : count * split]
                    grad_shares = lax.dot_general(
                        value, gradient, last_last, preferred_element_type=jnp.float32
                    )
                    grad_scores = (
                        shares
                        * (grad_shares - over_keys(jnp.sum, grad_shares * shares, split))
                        * scale
                    ).astype(jnp.bfloat16)
                    grad_value = unstacked(
                        jnp.dot(
                            shares.astype(jnp.bfloat16),
                            gradient,
                            preferred_element_type=jnp.float32,
                        ),
                        split,
                    )
                    grad_key = unstacked(
                        jnp.dot(grad_scores, asked, preferred_element_type=jnp.float32), split
                    )
                    grad_query = lax.dot_general(
                        grad_scores, key, first_first, preferred_element_type=jnp.float32
                    )
                    query[pair_rows(pair), at] = grad_query.astype(jnp.bfloat16)
                    keys[pair_rows(pair, count), at] = grad_key.astype(jnp.bfloat16)
                    values[pair_rows(pair, count), at] = grad_value.astype(jnp.bfloat16)

            for_pairs(body)

        def clear_tail(ref, count):
            if count < tall:

                def body(pair):
                    at = pl.ds(pl.multiple_of(pair * tall + count, 16), tall - count)
                    ref[at, :] = jnp.zeros((tall - count, ref.shape[-1]), ref.dtype)

                for_pairs(body)

        if inner < 3072:
            for which in range(6, 12):
                at_ref[which, :, :, 0:128] = jnp.zeros((2, 2, 128, height), jnp.bfloat16)
        low[...] = jnp.zeros_like(low)
        for pair in range(pairs):
            low[pair * tall : pair * tall + slots, 0:width] = hidden_ref[pair, :, 0:width]
        own_refs = (g_ref.at[1], g_ref.at[2])
        far_refs = (far_keys, far_values)
        for which, bias_row in ((0, None), (1, 1)):
            forward_product(low, biased(own_refs[which], bias_row))
            for pair in range(pairs):
                exchange(own_refs, far_refs, send_sems, recv_sems, which, pair, cfg.own_keys).start()
        forward_product(low, biased(g_ref.at[0], 0))
        put_low(0, width)
        state[:, 0:width] = low[:, 0:width].astype(jnp.float32)
        for which in range(2):
            for pair in range(pairs):
                exchange(
                    own_refs, far_refs, send_sems, recv_sems, which, pair, cfg.own_keys
                ).wait_send()
                exchange(
                    own_refs, far_refs, send_sems, recv_sems, which, pair, cfg.far_keys
                ).wait_recv()
        for ref in own_refs:
            clear_tail(ref, cfg.own_keys)
        pl.semaphore_signal(landing_free, inc=1, device_id=partner, device_id_type=MESH)
        attend_forward(
            g_ref.at[0], far_keys, far_values, co_probs, far_lengths, cfg.far_keys, 1, 128, 8
        )
        put_low(1, 1024)
        forward_product(low, add_total(True))
        norm_forward(0, 2, 4)
        mlp_forward(0)
        norm_forward(1, 6, 2)
        self_refs = (g_ref.at[4], g_ref.at[5], g_ref.at[6])
        for index, bias_row in ((0, 3), (1, None), (2, 4)):
            forward_product(low, biased(self_refs[index], bias_row))
        attend_forward(
            *self_refs, self_probs, own_lengths, cfg.own_keys, cfg.split, cfg.head, groups
        )
        put_low(3, width)
        forward_product(low, add_total(True))
        norm_forward(2, 5, 5)
        mlp_forward(1)

        if width < 1024:
            result_ref[...] = jnp.zeros_like(result_ref)
            grad_ref[...] = jnp.zeros_like(grad_ref)

        def last_norm(pair):
            at = pair_rows(pair)
            rows, inverse = normalize(
                state[at, 0:width] + total[at, 0:width] + params[7:8, 0:width]
            )
            result = rows * params[11:12, 0:width] + params[15:16, 0:width]
            result_ref[pair, :, 0:width] = result[0:slots].astype(jnp.bfloat16)
            total[at, 0:width] = jnp.zeros((tall, width), jnp.float32)
            total[pl.ds(pl.multiple_of(pair * tall, tall), slots), 0:width] = cotangent_ref[
                pair, :, 0:width
            ].astype(jnp.float32)
            norm_gradient(3, at, total[at, 0:width], rows, inverse, 15, 7)

        for_pairs(last_norm)

        mlp_backward(1)
        norm_backward(2, 7, 5)
        backward_product(g_ref.at[7], biased(low, None))
        attend_backward(*self_refs, self_probs, cfg.own_keys, cfg.split, cfg.head, groups)
        for ref in self_refs[1:]:
            clear_tail(ref, cfg.own_keys)
        for index in range(3):
            backward_product(self_refs[index], add_total(index == 0))
        column_sums(4, 3, width)
        column_sums(6, 4, width)
        norm_backward(1, 14, 6)
        mlp_backward(0)
        norm_backward(0, 3, 2)
        backward_product(g_ref.at[3], biased(low, None))
        attend_backward(g_ref.at[0], far_keys, far_values, co_probs, cfg.far_keys, 1, 128, 8)
        pl.semaphore_wait(landing_free, 1)
        for which in range(2):
            for pair in range(pairs):
                exchange(
                    far_refs, own_refs, back_send_sems, back_recv_sems, which, pair, cfg.far_keys
                ).start()
        backward_product(g_ref.at[0], add_total(True))
        column_sums(0, 0, 1024)
        for which in range(2):
            for pair in range(pairs):
                exchange(
                    far_refs, own_refs, back_send_sems, back_recv_sems, which, pair, cfg.far_keys
                ).wait_send()
                exchange(
                    far_refs, own_refs, back_send_sems, back_recv_sems, which, pair, cfg.own_keys
                ).wait_recv()
            backward_product(own_refs[which], add_total(False))
        column_sums(2, 1, 1024)

        def finish(pair):
            at = pl.ds(pl.multiple_of(pair * tall, tall), slots)
            grad_ref[pair, :, 0:width] = (state[at, 0:width] + total[at, 0:width]).astype(
                jnp.bfloat16
            )

        for_pairs(finish)

    @pl.when(stream == 0)
    def _():
        run(TEXT, text_lengths, region_counts)

    @pl.when(stream != 0)
    def _():
        run(IMAGE, region_counts, text_lengths)


def layer(line, text_lengths, region_counts, hidden, cotangent, weights):
    pairs, slots, width = hidden.shape
    tall = (slots + 15) // 16 * 16
    height = pairs * tall
    vmem = pl.BlockSpec(memory_space=pltpu.VMEM)
    smem = pl.BlockSpec(memory_space=pltpu.SMEM)
    anywhere = pl.BlockSpec(memory_space=pl.ANY)
    return pl.pallas_call(
        partial(layer_kernel, line, pairs, slots, tall),
        out_shape=(
            jax.ShapeDtypeStruct(hidden.shape, jnp.bfloat16),
            jax.ShapeDtypeStruct(hidden.shape, jnp.bfloat16),
            jax.ShapeDtypeStruct((12, 2, 2, 256, height), jnp.bfloat16),
            jax.ShapeDtypeStruct((16, height, 1024), jnp.bfloat16),
            jax.ShapeDtypeStruct((16, 1024), jnp.float32),
            jax.ShapeDtypeStruct((8, 3072), jnp.float32),
        ),
        in_specs=[smem] * 2 + [vmem] * 2 + [anywhere] * 6 + [vmem] * 5,
        out_specs=(vmem,) * 6,
        scratch_shapes=[
            pltpu.VMEM((RING, 1024, 1024), jnp.bfloat16),
            pltpu.VMEM((height, 1024), jnp.bfloat16),
            pltpu.VMEM((height, 1024), jnp.bfloat16),
            pltpu.VMEM((height, 1024), jnp.float32),
            pltpu.VMEM((height, 1024), jnp.float32),
            pltpu.VMEM((height, 1024), jnp.bfloat16),
            pltpu.VMEM((height, 1024), jnp.bfloat16),
            pltpu.VMEM((3, height, 1024), jnp.bfloat16),
            pltpu.VMEM((3, height, 1), jnp.float32),
            pltpu.VMEM((pairs, 8, 128, tall), jnp.float32),
            pltpu.VMEM((pairs, 8, 112, tall), jnp.float32),
            pltpu.VMEM((16, 1024), jnp.float32),
            pltpu.VMEM((8, 3072), jnp.float32),
            pltpu.SemaphoreType.DMA((RING,)),
            pltpu.SemaphoreType.DMA((2, pairs)),
            pltpu.SemaphoreType.DMA((2, pairs)),
            pltpu.SemaphoreType.DMA((2, pairs)),
            pltpu.SemaphoreType.DMA((2, pairs)),
            pltpu.SemaphoreType.REGULAR,
        ],
        compiler_params=pltpu.CompilerParams(
            collective_id=1, has_side_effects=True, vmem_limit_bytes=62 * 1024 * 1024
        ),
        name="layer",
    )(text_lengths, region_counts, hidden, cotangent, *weights)


def on_device(
    hidden,
    text_lengths,
    region_counts,
    co_qkv,
    co_out,
    self_qkv,
    self_out,
    mlp_up,
    mlp_down,
    proj_bias,
    mlp_bias_up,
    mlp_bias_down,
    norm_gain_table,
    norm_bias,
    cotangent,
):
    line = lax.axis_size("dp") // 4
    piece = 256 // line
    result, grad, operands, gradients, vectors, hidden_vectors = layer(
        line,
        text_lengths,
        region_counts,
        hidden[0],
        cotangent[0],
        (
            co_qkv[0],
            co_out[0],
            self_qkv[0],
            self_out[0],
            mlp_up[0],
            mlp_down[0],
            proj_bias[0].reshape(6, 1024),
            mlp_bias_up[0],
            mlp_bias_down[0],
            norm_gain_table[0],
            norm_bias[0],
        ),
    )
    hidden_rows = (
        hidden_vectors[:2].reshape(2, 4 * line, 3, piece).transpose(0, 2, 1, 3).reshape(6, 1024)
    )
    all_vectors = jnp.concatenate([vectors[:6], hidden_rows, vectors[6:]])
    vector_rows = place_rows(widen(all_vectors, (UNIT, 1024)).T, line)
    summed = reduce_gradients(line, operands, gradients, vector_rows)

    def parts(first, count):
        block = summed[:, first * UNIT : (first + count * 4) * UNIT]
        return block.reshape(piece, count, 1024).transpose(1, 0, 2)

    vector_sums = summed[:, 80 * UNIT : 80 * UNIT + 22].T
    return (
        result[None],
        grad[None],
        parts(0, 3)[None],
        parts(12, 1),
        parts(16, 3)[None],
        parts(28, 1),
        jnp.stack([summed[:, 32 * UNIT : 44 * UNIT], summed[:, 44 * UNIT : 56 * UNIT]])[None],
        jnp.stack([parts(56, 3).reshape(3 * piece, 1024), parts(68, 3).reshape(3 * piece, 1024)])[
            None
        ],
        vector_sums[:6].reshape(1, 2, 3, piece),
        vector_sums[6:12].reshape(1, 2, 3 * piece),
        vector_sums[12:14][None],
        vector_sums[14:18][None],
        vector_sums[18:22][None],
    )


def solution(mesh):
    return jax.shard_map(
        on_device,
        mesh=mesh,
        in_specs=(
            P("stream", "dp", None, None),
            P("dp"),
            P("dp"),
            P("stream", None, None, None),
            P("stream", None, None),
            P("stream", None, None, None),
            P("stream", None, None),
            P("stream", None, None, None),
            P("stream", None, None, None),
            P("stream", None, None, None),
            P("stream", None, None),
            P("stream", None, None),
            P("stream", None, None),
            P("stream", None, None),
            P("stream", "dp", None, None),
        ),
        out_specs=(
            P("stream", "dp", None, None),
            P("stream", "dp", None, None),
            P("stream", None, "dp", None),
            P("stream", "dp", None),
            P("stream", None, "dp", None),
            P("stream", "dp", None),
            P("stream", None, "dp", None),
            P("stream", None, "dp", None),
            P("stream", None, None, "dp"),
            P("stream", None, "dp"),
            P("stream", None, "dp"),
            P("stream", None, "dp"),
            P("stream", None, "dp"),
        ),
        check_vma=False,
    )
```

```python
from functools import partial
from typing import NamedTuple
import math

import jax
import jax.numpy as jnp
from jax import lax
from jax.experimental import pallas as pl
from jax.experimental.pallas import tpu as pltpu
from jax.sharding import PartitionSpec as P

EPSILON = 1e-05
NEGATIVE = -1000000000.0
ROOT_HALF = 1.0 / math.sqrt(2.0)
GAUSS_NORM = 1.0 / math.sqrt(2.0 * math.pi)

MESH = pl.DeviceIdType.MESH
UNIT = 256
OUT_BLOCKS = 81
CORE_SLOTS = 4
LAG_X = 4
X_SLOTS = 2 * LAG_X
Z_SLOTS = 4
VMEM_BYTES = 65200 * 1024

TEXT_UNITS = (
    (3, 3, 9, 1, 60, 0, 68, 4, 256),
    (1, 12, 5, 0, 44, 0, 44, 0, 192),
    (1, 3, 3, 0, 28, 0, 28, 0, 192),
    (3, 3, 2, 0, 16, 4, 16, 4, 192),
    (3, 3, 6, 1, 56, 0, 56, 4, 256),
    (1, 12, 4, 0, 32, 0, 32, 0, 192),
    (1, 3, 1, 0, 12, 0, 12, 0, 256),
    (3, 4, 0, 0, 0, 4, 0, 4, 192),
    (1, 1, 0, 0, 0, 0, 80, 0, 256),
)
IMAGE_UNITS = (
    (3, 4, 9, 1, 60, 0, 68, 4, 128),
    (1, 4, 5, 0, 44, 0, 44, 0, 256),
    (1, 4, 3, 0, 28, 0, 28, 0, 256),
    (3, 4, 2, 0, 16, 4, 16, 4, 256),
    (3, 4, 6, 1, 56, 0, 56, 4, 128),
    (1, 4, 4, 0, 32, 0, 32, 0, 256),
    (1, 4, 1, 0, 12, 0, 12, 0, 256),
    (3, 4, 0, 0, 0, 4, 0, 4, 256),
    (1, 1, 0, 0, 0, 0, 80, 0, 256),
)


def line_lag(line):
    return 2 if line <= 8 else 1


def slots_held(line):
    return LAG_X + (line - 1) * line_lag(line) + 1


def unit_count(table):
    return sum(entry[0] * entry[1] for entry in table)


def decode_one(table, unit):
    start = 0
    result = None
    for groups, blocks, a0, a1, g0, g1, o0, o1, kept in table:
        local = unit - start
        group = local // blocks
        block = local % blocks
        fields = (a0 + a1 * group, g0 + g1 * group + block, o0 + o1 * group + block, jnp.int32(kept))
        if result is None:
            result = fields
        else:
            result = tuple(jnp.where(unit >= start, new, old) for new, old in zip(fields, result))
        start += groups * blocks
    return result


def decode(is_text, unit):
    text = decode_one(TEXT_UNITS, unit)
    image = decode_one(IMAGE_UNITS, unit)
    return tuple(jnp.where(is_text, one, other) for one, other in zip(text, image))


SENT = 112


class Stream(NamedTuple):
    width: int
    inner: int
    split: int
    head: int
    own_keys: int
    far_keys: int
    own_sent: int
    far_sent: int


TEXT = Stream(768, 3072, 2, 64, 64, 112, 64, SENT)
IMAGE = Stream(1024, 1024, 1, 128, 112, 64, SENT, 64)
PACE = (12, 5)
LANDING_TURN = 54
RING = 3
LANES = 128
TAIL = (
    0.28208317669832234,
    0.2824362970929616,
    0.24263030272423752,
    0.20467309203585946,
    -0.03157028123874516,
    0.28558060664263174,
    -0.4940359058844012,
    0.2879944144937219,
    -0.0597917499304742,
)


def gelu_parts(value):
    root = jnp.abs(value) * ROOT_HALF
    near = 1.0 / (1.0 + 0.5 * root)
    bell = jnp.exp(-(root * root))
    series = TAIL[-1] * near
    for factor in TAIL[-2::-1]:
        series = (series + factor) * near
    tail = 0.5 * bell * series
    below = jnp.where(value >= 0.0, 1.0 - tail, tail)
    return value * below, below + value * bell * GAUSS_NORM


def layer_kernel(
    line,
    pairs,
    slots,
    tall,
    text_lengths,
    region_counts,
    hidden,
    cotangent,
    co_qkv_whole,
    co_out_whole,
    self_qkv_whole,
    self_out_whole,
    mlp_up_whole,
    mlp_down_whole,
    proj_bias,
    bias_up,
    bias_down,
    gain,
    shift,
    result,
    grad,
    sums_out,
    at_ref,
    g_ref,
    sums,
    vectors,
    hidden_vectors,
    staged,
    ring,
    far_keys,
    far_values,
    state,
    total,
    low,
    active,
    normal,
    spread,
    self_probs,
    co_probs,
    params,
    up_params,
    ring_sems,
    send_sems,
    recv_sems,
    back_send_sems,
    back_recv_sems,
    landing_free,
    staged_sems,
    core_out,
    core_in,
    partial_own,
    x_out,
    x_in,
    own,
    down_out,
    down_in,
    up_out,
    up_in,
    core_sems,
    x_sems,
    down_sems,
    up_sems,
    down_free,
    up_free,
):
    stream = lax.axis_index("stream")
    place = lax.axis_index("dp")
    partner = (1 - stream, place)
    height = pairs * tall
    piece = 256 // line
    per_block = 256 // piece

    core = lax.rem(place, 2)
    side = lax.rem(place // 2, 2)
    spot = place // 4
    is_text = stream == 0
    unit_total = jnp.where(is_text, unit_count(TEXT_UNITS), unit_count(IMAGE_UNITS))
    core_device = (stream, place + 1 - 2 * core)
    side_device = (stream, place + 2 - 4 * side)
    lower_device = (stream, place - 4)
    upper_device = (stream, place + 4)
    own_slots = slots_held(line)
    last = line - 1
    co_qkv, co_out, self_qkv, self_out, mlp_up, mlp_down = (
        ref.at[0]
        for ref in (
            co_qkv_whole,
            co_out_whole,
            self_qkv_whole,
            self_out_whole,
            mlp_up_whole,
            mlp_down_whole,
        )
    )
    hidden_ref, cotangent_ref = staged.at[0], staged.at[1]
    result_ref, grad_ref = staged.at[0], staged.at[1]

    def stage(index):
        source = (hidden, cotangent)[index]
        return pltpu.make_async_copy(source.at[0], staged.at[index], staged_sems.at[index])

    def unstage(index):
        target = (result, grad)[index]
        return pltpu.make_async_copy(staged.at[index], target.at[0], staged_sems.at[index])

    stage(0).start()
    stage(1).start()
    far_keys[...] = jnp.zeros_like(far_keys)
    far_values[...] = jnp.zeros_like(far_values)

    barrier = pltpu.get_barrier_semaphore()
    for device in (partner, core_device, side_device):
        pl.semaphore_signal(barrier, inc=1, device_id=device, device_id_type=MESH)

    @pl.when(spot > 0)
    def _():
        pl.semaphore_signal(barrier, inc=1, device_id=lower_device, device_id_type=MESH)

    @pl.when(spot < last)
    def _():
        pl.semaphore_signal(barrier, inc=1, device_id=upper_device, device_id_type=MESH)

    pl.semaphore_wait(
        barrier, 3 + (spot > 0).astype(jnp.int32) + (spot < last).astype(jnp.int32)
    )
    for half in range(2):
        params[3 * half : 3 * half + 3] = proj_bias[0, half].astype(jnp.float32)
    params[6:8] = bias_down[0].astype(jnp.float32)
    params[8:12] = gain[0].astype(jnp.float32)
    params[12:16] = shift[0].astype(jnp.float32)
    up_params[0:2] = bias_up[0].astype(jnp.float32)
    vectors[...] = jnp.zeros_like(vectors)
    hidden_vectors[...] = jnp.zeros_like(hidden_vectors)
    sums[...] = jnp.zeros_like(sums)

    def block(index):
        return pl.ds(pl.multiple_of(index * UNIT, UNIT), UNIT)

    def pair_rows(pair, count=tall):
        return pl.ds(pl.multiple_of(pair * tall, tall), count)

    def exchange(sources, targets, sends, receives, which, pair, count):
        return pltpu.make_async_remote_copy(
            src_ref=sources[which].at[pair_rows(pair, count)],
            dst_ref=targets[which].at[pair_rows(pair, count)],
            send_sem=sends.at[which, pair],
            recv_sem=receives.at[which, pair],
            device_id=partner,
            device_id_type=MESH,
        )

    def for_rows(kept, body):
        for rows in (128, 192, 256):

            @pl.when(kept == rows)
            def _():
                body(rows)

    def core_copy(unit, rows):
        slot = lax.rem(unit, CORE_SLOTS)
        return pltpu.make_async_remote_copy(
            src_ref=core_out.at[slot, :, pl.ds(0, rows)],
            dst_ref=core_in.at[slot, :, pl.ds(0, rows)],
            send_sem=core_sems.at[0, slot],
            recv_sem=core_sems.at[1, slot],
            device_id=core_device,
            device_id_type=MESH,
        )

    def side_copy(unit, rows):
        slot = lax.rem(unit, X_SLOTS)
        return pltpu.make_async_remote_copy(
            src_ref=x_out.at[slot, pl.ds(0, rows)],
            dst_ref=x_in.at[slot, pl.ds(0, rows)],
            send_sem=x_sems.at[0, slot],
            recv_sem=x_sems.at[1, slot],
            device_id=side_device,
            device_id_type=MESH,
        )

    def line_copy(source, target, sems, device, slot, index):
        at = pl.ds(pl.multiple_of(index * piece, piece), piece)
        return pltpu.make_async_remote_copy(
            src_ref=source.at[slot, at],
            dst_ref=target.at[slot, at],
            send_sem=sems.at[0, slot, index],
            recv_sem=sems.at[1, slot, index],
            device_id=device,
            device_id_type=MESH,
        )

    def columns(block):
        return pl.ds(pl.multiple_of(block * UNIT, UNIT), UNIT)

    def multiply(unit):
        a_block, g_block, out_block, kept = decode(is_text, unit)
        slot = lax.rem(unit, CORE_SLOTS)
        keep = lax.rem(unit, 2)
        is_vector = unit == unit_total - 1

        @pl.when(jnp.logical_not(is_vector))
        def _():
            gradient = g_ref[g_block // 4, :, columns(lax.rem(g_block, 4))]

            def body(rows):
                for half in range(2):
                    core_out[slot, half, pl.ds(0, rows)] = jnp.dot(
                        at_ref[a_block, 1 - core, half, pl.ds(0, rows)],
                        gradient,
                        preferred_element_type=jnp.float32,
                    ).astype(jnp.bfloat16)
                core_copy(unit, rows).start()
                for half in range(2):
                    partial_own[keep, half, pl.ds(0, rows)] = jnp.dot(
                        at_ref[a_block, core, half, pl.ds(0, rows)],
                        gradient,
                        preferred_element_type=jnp.float32,
                    )

            for_rows(kept, body)

        @pl.when(is_vector)
        def _():
            place_vectors(slot, keep)
            core_copy(unit, 256).start()

    def add_core(unit):
        kept = decode(is_text, unit)[3]
        slot = lax.rem(unit, CORE_SLOTS)
        keep = lax.rem(unit, 2)
        far = lax.rem(unit, X_SLOTS)
        store = lax.rem(unit, own_slots)

        def body(rows):
            core_copy(unit, rows).wait()
            at = pl.ds(0, rows)
            x_out[far, at] = (
                partial_own[keep, 1 - side, at] + core_in[slot, 1 - side, at].astype(jnp.float32)
            ).astype(jnp.bfloat16)
            side_copy(unit, rows).start()
            own[store, at] = partial_own[keep, side, at] + core_in[slot, side, at].astype(
                jnp.float32
            )

        for_rows(kept, body)

    def add_side(unit):
        _, _, out_block, kept = decode(is_text, unit)
        far = lax.rem(unit, X_SLOTS)
        store = lax.rem(unit, own_slots)

        def body(rows):
            side_copy(unit, rows).wait()
            at = pl.ds(0, rows)
            own[store, at] += x_in[far, at].astype(jnp.float32)

        for_rows(kept, body)

        @pl.when((spot + 1) * piece <= kept)
        def _():
            at = pl.ds(pl.multiple_of(spot * piece, piece), piece)
            sums[:, columns(out_block)] = own[store, at]

    def line_step(unit, source, target, sems, free, sender, reader, low, high, gives, takes):
        slot = lax.rem(unit + Z_SLOTS, Z_SLOTS)

        @pl.when(jnp.logical_and(unit >= Z_SLOTS, gives))
        def _():
            count = decode(is_text, unit - Z_SLOTS)[3] // piece
            pl.semaphore_wait(free, 1)

            def settle(index, carry):
                line_copy(source, target, sems, reader, slot, index).wait_send()
                return carry

            lax.fori_loop(low(count), high(count), settle, 0)

        @pl.when(unit < unit_total)
        def _():
            _, _, out_block, kept = decode(is_text, unit)
            count = kept // piece
            store = lax.rem(unit, own_slots)

            def at(index):
                return pl.ds(pl.multiple_of(index * piece, piece), piece)

            @pl.when(gives)
            def _():
                def forward(index, carry):
                    @pl.when(takes)
                    def _():
                        line_copy(source, target, sems, reader, slot, index).wait_recv()
                        source[slot, at(index)] = (
                            own[store, at(index)] + target[slot, at(index)].astype(jnp.float32)
                        ).astype(jnp.bfloat16)

                    @pl.when(jnp.logical_not(takes))
                    def _():
                        source[slot, at(index)] = own[store, at(index)].astype(jnp.bfloat16)

                    line_copy(source, target, sems, reader, slot, index).start()
                    return carry

                lax.fori_loop(low(count), high(count), forward, 0)

            @pl.when(takes)
            def _():
                @pl.when(spot < count)
                def _():
                    line_copy(source, target, sems, reader, slot, spot).wait_recv()
                    sums[:, columns(out_block)] += target[slot, at(spot)].astype(jnp.float32)

                pl.semaphore_signal(free, inc=1, device_id=sender, device_id_type=MESH)

    def tick(step):
        @pl.when(step < unit_total)
        def _():
            multiply(step)

        @pl.when(jnp.logical_and(step >= 1, step < unit_total + 1))
        def _():
            add_core(step - 1)

        @pl.when(jnp.logical_and(step >= LAG_X, step < unit_total + LAG_X))
        def _():
            add_side(step - LAG_X)

        falling = step - LAG_X - (last - spot) * line_lag(line)

        @pl.when(jnp.logical_and(falling >= 0, falling < unit_total + Z_SLOTS))
        def _():
            line_step(
                falling,
                down_out,
                down_in,
                down_sems,
                down_free,
                upper_device,
                lower_device,
                lambda count: 0,
                lambda count: jnp.minimum(spot, count),
                spot > 0,
                spot < last,
            )

        rising = step - LAG_X - spot * line_lag(line)

        @pl.when(jnp.logical_and(rising >= 0, rising < unit_total + Z_SLOTS))
        def _():
            line_step(
                rising,
                up_out,
                up_in,
                up_sems,
                up_free,
                lower_device,
                upper_device,
                lambda count: jnp.minimum(spot + 1, count),
                lambda count: count,
                spot < last,
                spot > 0,
            )

    def place_vectors(slot, keep):
        turned = vectors[...].T
        tall_sums = hidden_vectors[...].T
        lane = lax.broadcasted_iota(jnp.int32, (piece, LANES), 1)
        for owner in range(4 * line):
            value = turned[owner * piece : (owner + 1) * piece]
            for group in range(3):
                number = owner * 3 + group
                part = tall_sums[number * piece : (number + 1) * piece]
                for which in range(2):
                    value = jnp.where(
                        lane == 6 + 3 * which + group, part[:, which : which + 1], value
                    )
            total[
                owner // 8 * piece : (owner // 8 + 1) * piece,
                owner % 8 * LANES : (owner % 8 + 1) * LANES,
            ] = value
        core_out[slot] = jnp.zeros((2, 256, UNIT), jnp.bfloat16)
        partial_own[keep] = jnp.zeros((2, 256, UNIT), jnp.float32)

        def step(owner, carry):
            value = total[
                pl.ds(pl.multiple_of(owner // 8 * piece, piece), piece),
                pl.ds(pl.multiple_of(lax.rem(owner, 8) * LANES, LANES), LANES),
            ]
            at = pl.ds(pl.multiple_of((owner // 4) * piece, piece), piece)
            half = lax.rem(owner // 2, 2)

            @pl.when(lax.rem(owner, 2) == core)
            def _():
                partial_own[keep, half, at, 0:LANES] = value

            @pl.when(lax.rem(owner, 2) != core)
            def _():
                core_out[slot, half, at, 0:LANES] = value.astype(jnp.bfloat16)

            return carry

        lax.fori_loop(0, 4 * line, step, 0)

    def run(cfg, own_lengths, far_lengths):
        width, inner = cfg.width, cfg.inner
        chunks = inner // 1024
        groups = width // LANES

        plan = [co_qkv.at[index, pl.ds(0, width)] for index in (1, 2, 0)]
        plan.append(co_out.at[:, pl.ds(0, width)])

        def mlp_plan(index, chunk):
            at = pl.ds(chunk * 1024, 1024)
            return mlp_up.at[index, pl.ds(0, width), at], mlp_down.at[index, at, pl.ds(0, width)]

        def square(index):
            return self_qkv.at[index, pl.ds(0, width), pl.ds(0, width)]

        for chunk in range(chunks):
            plan.extend(mlp_plan(0, chunk))
        plan.extend(square(index) for index in range(3))
        plan.append(self_out.at[pl.ds(0, width), pl.ds(0, width)])
        for chunk in range(chunks):
            plan.extend(mlp_plan(1, chunk))
        for chunk in range(chunks):
            plan.extend(mlp_plan(1, chunk)[::-1])
        plan.append(self_out.at[pl.ds(0, width), pl.ds(0, width)])
        plan.extend(square(index) for index in range(3))
        for chunk in range(chunks):
            plan.extend(mlp_plan(0, chunk)[::-1])
        plan.append(co_out.at[:, pl.ds(0, width)])
        plan.extend(co_qkv.at[index, pl.ds(0, width)] for index in range(3))

        def fetch(index):
            rows, columns = plan[index].shape
            return pltpu.make_async_copy(
                plan[index],
                ring.at[index % RING, pl.ds(0, rows), pl.ds(0, columns)],
                ring_sems.at[index % RING],
            )

        used = [0]
        def with_weight(body):
            index = used[0]
            used[0] += 1
            fetch(index).wait()
            rows, columns = plan[index].shape
            body(ring.at[index % RING], rows, columns)
            if index + RING < len(plan):
                fetch(index + RING).start()

        def forward_product(source, consume):
            def body(weight, rows, columns):
                def step(index, carry):
                    consume(
                        index,
                        jnp.dot(
                            source[:, 0:rows],
                            weight[0:rows, block(index)],
                            preferred_element_type=jnp.float32,
                        ),
                    )
                    return carry

                lax.fori_loop(0, columns // UNIT, step, 0)

            with_weight(body)

        segments = []

        def backward_items(source, consume):
            index = used[0]
            used[0] += 1
            rows, columns = plan[index].shape
            weight = ring.at[index % RING]
            count = rows // UNIT

            def item(number):
                @pl.when(number == 0)
                def _():
                    fetch(index).wait()

                consume(
                    number,
                    lax.dot_general(
                        source[:, 0:columns],
                        weight[block(number), 0:columns],
                        (((1,), (1,)), ((), ())),
                        preferred_element_type=jnp.float32,
                    ),
                )
                if index + RING < len(plan):

                    @pl.when(number == count - 1)
                    def _():
                        fetch(index + RING).start()

            segments.append((count, item))

        def add_total(first):
            def consume(index, value):
                if first:
                    total[:, block(index)] = value
                else:
                    total[:, block(index)] += value

            return consume

        def put_rows(at_block, index, value):
            turned = value.T
            for part in range(per_block):
                at_ref[
                    at_block,
                    part % 2,
                    (part // 2) % 2,
                    pl.ds(pl.multiple_of((index * (per_block // 4) + part // 4) * piece, piece), piece),
                ] = turned[part * piece : (part + 1) * piece]

        def put_hidden_rows(at_block, index, value):
            turned = value.T
            for part in range(per_block):
                number = index * per_block + part
                owner = number // 3
                at_ref[
                    at_block + lax.rem(number, 3),
                    lax.rem(owner, 2),
                    lax.rem(owner // 2, 2),
                    pl.ds(pl.multiple_of((owner // 4) * piece, piece), piece),
                ] = turned[part * piece : (part + 1) * piece]

        def put_low(at_block, columns):
            def step(index, carry):
                put_rows(at_block, index, low[:, block(index)])
                return carry

            lax.fori_loop(0, columns // UNIT, step, 0)

        def for_pairs(body):
            def step(pair, carry):
                body(pair)
                return carry

            lax.fori_loop(0, pairs, step, 0)

        def mean(value):
            return jnp.sum(value, axis=-1, keepdims=True) * (1.0 / width)

        def normalize(value):
            centered = value - mean(value)
            inverse = lax.rsqrt(mean(centered * centered) + EPSILON)
            return centered * inverse, inverse

        def norm_forward(index, bias_row, at_block):
            def body(pair):
                at = pair_rows(pair)
                rows, inverse = normalize(
                    state[at, 0:width] + total[at, 0:width] + params[bias_row : bias_row + 1, 0:width]
                )
                result = (
                    rows * params[8 + index : 9 + index, 0:width]
                    + params[12 + index : 13 + index, 0:width]
                )
                state[at, 0:width] = result
                low[at, 0:width] = result.astype(jnp.bfloat16)
                normal[index, at, 0:width] = rows.astype(jnp.bfloat16)
                spread[at, index : index + 1] = inverse

            for_pairs(body)
            put_low(at_block, width)

        def add_row(ref, row, value):
            ref[row : row + 1, 0 : value.shape[-1]] += jnp.sum(value, axis=0, keepdims=True)

        def norm_gradient(index, at, gradient, rows, inverse, g_block, bias_row):
            scaled = gradient * params[8 + index : 9 + index, 0:width]
            result = inverse * (scaled - mean(scaled) - rows * mean(scaled * rows))
            state[at, 0:width] = result
            rounded = result.astype(jnp.bfloat16)
            g_ref[g_block, at, 0:width] = rounded
            add_row(vectors, 14 + index, gradient * rows)
            add_row(vectors, 18 + index, gradient)
            add_row(vectors, bias_row if bias_row < 6 else bias_row + 6, rounded.astype(jnp.float32))

        def norm_backward(index, g_block, bias_row):
            def body(pair):
                at = pair_rows(pair)
                norm_gradient(
                    index,
                    at,
                    state[at, 0:width] + total[at, 0:width],
                    normal[index, at, 0:width].astype(jnp.float32),
                    spread[at, index : index + 1],
                    g_block,
                    bias_row,
                )

            segments.append((pairs, body))

        def mlp_forward(index):
            for chunk in range(chunks):

                def activate(number, value):
                    act, slope = gelu_parts(
                        value
                        + up_params[
                            index : index + 1,
                            pl.ds(pl.multiple_of(chunk * 1024 + number * UNIT, UNIT), UNIT),
                        ]
                    )
                    act = act.astype(jnp.bfloat16)
                    active[:, block(number)] = act
                    g_ref[8 + 3 * index + chunk, :, block(number)] = slope.astype(jnp.bfloat16)
                    put_hidden_rows(6 + 3 * index, chunk * 4 + number, act)

                forward_product(low, activate)
                forward_product(active, add_total(chunk == 0))

        def mlp_backward(index):
            for chunk in range(chunks):
                g_block = 8 + 3 * index + chunk

                def through(number, value, g_block=g_block, chunk=chunk):
                    slope = g_ref[g_block, :, block(number)].astype(jnp.float32)
                    rounded = (value * slope).astype(jnp.bfloat16)
                    g_ref[g_block, :, block(number)] = rounded
                    hidden_vectors[
                        index : index + 1,
                        pl.ds(pl.multiple_of(chunk * 1024 + number * UNIT, UNIT), UNIT),
                    ] = jnp.sum(rounded.astype(jnp.float32), axis=0, keepdims=True)

                backward_items(g_ref.at[14 + index], through)
                backward_items(g_ref.at[g_block], add_total(chunk == 0))

        def biased(target, bias_row):
            def consume(index, value):
                if bias_row is not None:
                    value = value + params[bias_row : bias_row + 1, block(index)]
                target[:, block(index)] = value.astype(jnp.bfloat16)

            return consume

        def column_sums(g_block, row, columns):
            def item(index):
                vectors[row : row + 1, block(index)] = jnp.sum(
                    g_ref[g_block, :, block(index)].astype(jnp.float32), axis=0, keepdims=True
                )

            segments.append((columns // UNIT, item))

        def stacked(value, split):
            if split == 1:
                return value
            lane = lax.broadcasted_iota(jnp.int32, value.shape, 1)
            zero = jnp.zeros_like(value)
            return jnp.concatenate(
                [jnp.where(lane < 64, value, zero), jnp.where(lane < 64, zero, value)], axis=0
            )

        def unstacked(value, split):
            if split == 1:
                return value
            half = value.shape[0] // 2
            lane = lax.broadcasted_iota(jnp.int32, (half, LANES), 1)
            return jnp.where(lane < 64, value[:half], value[half:])

        def over_keys(reduce, value, split):
            if split == 1:
                return reduce(value, axis=0, keepdims=True)
            half = value.shape[0] // 2
            return jnp.concatenate(
                [
                    jnp.broadcast_to(
                        reduce(part, axis=0, keepdims=True), part.shape
                    )
                    for part in (value[:half], value[half:])
                ],
                axis=0,
            )

        last_last = (((1,), (1,)), ((), ()))
        first_first = (((0,), (0,)), ((), ()))

        def attend_forward(query, keys, values, probs, lengths, count, split, head, group_count):
            scale = 1.0 / math.sqrt(head)

            def body(pair):
                length = lengths[pair]
                for group in range(group_count):
                    at = pl.ds(group * LANES, LANES)
                    key = stacked(keys[pair_rows(pair, count), at], split)
                    value = stacked(values[pair_rows(pair, count), at], split)
                    scores = (
                        lax.dot_general(
                            key,
                            query[pair_rows(pair), at],
                            last_last,
                            preferred_element_type=jnp.float32,
                        )
                        * scale
                    )
                    number = lax.broadcasted_iota(jnp.int32, scores.shape, 0)
                    if split == 2:
                        number = jnp.where(number < count, number, number - count)
                    scores = jnp.where(number < length, scores, NEGATIVE)
                    raised = jnp.exp(scores - over_keys(jnp.max, scores, split))
                    shares = (raised * (1.0 / over_keys(jnp.sum, raised, split))).astype(
                        jnp.bfloat16
                    )
                    probs[pair, group, 0 : count * split] = shares
                    low[pair_rows(pair), at] = lax.dot_general(
                        shares,
                        value,
                        first_first,
                        preferred_element_type=jnp.float32,
                    ).astype(jnp.bfloat16)

            for_pairs(body)

        def attend_backward(query, keys, values, probs, count, split, head, group_count):
            scale = 1.0 / math.sqrt(head)

            def body(pair):
                for group in range(group_count):
                    at = pl.ds(group * LANES, LANES)
                    key = stacked(keys[pair_rows(pair, count), at], split)
                    value = stacked(values[pair_rows(pair, count), at], split)
                    asked = query[pair_rows(pair), at]
                    gradient = low[pair_rows(pair), at]
                    rounded_shares = probs[pair, group, 0 : count * split]
                    shares = rounded_shares.astype(jnp.float32)
                    grad_shares = lax.dot_general(
                        value, gradient, last_last, preferred_element_type=jnp.float32
                    )
                    grad_scores = (
                        shares
                        * (grad_shares - over_keys(jnp.sum, grad_shares * shares, split))
                        * scale
                    ).astype(jnp.bfloat16)
                    grad_value = unstacked(
                        jnp.dot(
                            rounded_shares,
                            gradient,
                            preferred_element_type=jnp.float32,
                        ),
                        split,
                    )
                    grad_key = unstacked(
                        jnp.dot(grad_scores, asked, preferred_element_type=jnp.float32), split
                    )
                    grad_query = lax.dot_general(
                        grad_scores, key, first_first, preferred_element_type=jnp.float32
                    )
                    query[pair_rows(pair), at] = grad_query.astype(jnp.bfloat16)
                    keys[pair_rows(pair, count), at] = grad_key.astype(jnp.bfloat16)
                    values[pair_rows(pair, count), at] = grad_value.astype(jnp.bfloat16)

            return body

        def clear_tail(ref, pair, count):
            if count < tall:
                at = pl.ds(pl.multiple_of(pair * tall + count, 16), tall - count)
                ref[at, :] = jnp.zeros((tall - count, ref.shape[-1]), ref.dtype)

        own_refs = (g_ref.at[1], g_ref.at[2])
        far_refs = (far_keys, far_values)
        self_refs = (g_ref.at[4], g_ref.at[5], g_ref.at[6])

        def forward():
            for index in range(RING):
                fetch(index).start()
            if inner < 3072:
                for which in range(6, 12):
                    at_ref[which, :, :, 0:128] = jnp.zeros((2, 2, 128, height), jnp.bfloat16)
            low[...] = jnp.zeros_like(low)
            stage(0).wait()
            for pair in range(pairs):
                low[pair * tall : pair * tall + slots, 0:width] = hidden_ref[pair, :, 0:width]
            for which, bias_row in ((0, None), (1, 1)):
                forward_product(low, biased(own_refs[which], bias_row))
                for pair in range(pairs):
                    exchange(own_refs, far_refs, send_sems, recv_sems, which, pair, cfg.own_sent).start()
            forward_product(low, biased(g_ref.at[0], 0))
            put_low(0, width)
            state[:, 0:width] = low[:, 0:width].astype(jnp.float32)
            for which in range(2):
                for pair in range(pairs):
                    exchange(
                        own_refs, far_refs, send_sems, recv_sems, which, pair, cfg.own_sent
                    ).wait_send()
                    exchange(
                        own_refs, far_refs, send_sems, recv_sems, which, pair, cfg.far_sent
                    ).wait_recv()
            for ref in own_refs:
                for pair in range(pairs):
                    clear_tail(ref, pair, cfg.own_keys)
            pl.semaphore_signal(landing_free, inc=1, device_id=partner, device_id_type=MESH)
            attend_forward(
                g_ref.at[0], far_keys, far_values, co_probs, far_lengths, cfg.far_keys, 1, 128, 8
            )
            put_low(1, 1024)
            forward_product(low, add_total(True))
            norm_forward(0, 2, 4)
            mlp_forward(0)
            norm_forward(1, 6, 2)
            for index, bias_row in ((0, 3), (1, None), (2, 4)):
                forward_product(low, biased(self_refs[index], bias_row))
            attend_forward(
                *self_refs, self_probs, own_lengths, cfg.own_keys, cfg.split, cfg.head, groups
            )
            put_low(3, width)
            forward_product(low, add_total(True))
            norm_forward(2, 5, 5)
            mlp_forward(1)

            if width < 1024:
                result_ref[...] = jnp.zeros_like(result_ref)
            stage(1).wait()

            def last_norm(pair):
                at = pair_rows(pair)
                rows, inverse = normalize(
                    state[at, 0:width] + total[at, 0:width] + params[7:8, 0:width]
                )
                result = rows * params[11:12, 0:width] + params[15:16, 0:width]
                result_ref[pair, :, 0:width] = result[0:slots].astype(jnp.bfloat16)
                total[at, 0:width] = jnp.zeros((tall, width), jnp.float32)
                total[pl.ds(pl.multiple_of(pair * tall, tall), slots), 0:width] = cotangent_ref[
                    pair, :, 0:width
                ].astype(jnp.float32)
                norm_gradient(3, at, total[at, 0:width], rows, inverse, 15, 7)

            for_pairs(last_norm)
            unstage(0).start()


        def back_exchange(which, pair, count):
            return exchange(
                far_refs, own_refs, back_send_sems, back_recv_sems, which, pair, count
            )

        def self_attention_item(pair):
            attend_backward(*self_refs, self_probs, cfg.own_keys, cfg.split, cfg.head, groups)(pair)
            for ref in self_refs[1:]:
                clear_tail(ref, pair, cfg.own_keys)

        def co_attention_item(pair):
            attend_backward(
                g_ref.at[0], far_keys, far_values, co_probs, cfg.far_keys, 1, 128, 8
            )(pair)

            @pl.when(pair == 0)
            def _():
                pl.semaphore_wait(landing_free, 1)

            for which in range(2):
                back_exchange(which, pair, cfg.far_sent).start()

        def landed(which):
            def item(number):
                for pair in range(pairs):
                    back_exchange(which, pair, cfg.far_sent).wait_send()
                    back_exchange(which, pair, cfg.own_sent).wait_recv()

            return item

        def clear_item(number):
            unstage(0).wait()
            if width < 1024:
                grad_ref[...] = jnp.zeros_like(grad_ref)

        def finish_item(pair):
            at = pl.ds(pl.multiple_of(pair * tall, tall), slots)
            grad_ref[pair, :, 0:width] = (state[at, 0:width] + total[at, 0:width]).astype(
                jnp.bfloat16
            )

            @pl.when(pair == pairs - 1)
            def _():
                unstage(1).start()

        def list_backward():
            mlp_backward(1)
            norm_backward(2, 7, 5)
            backward_items(g_ref.at[7], biased(low, None))
            segments.append((pairs, self_attention_item))
            for index in range(3):
                backward_items(self_refs[index], add_total(index == 0))
            column_sums(4, 3, width)
            column_sums(6, 4, width)
            norm_backward(1, 14, 6)
            mlp_backward(0)
            norm_backward(0, 3, 2)
            backward_items(g_ref.at[3], biased(low, None))
            segments.append((pairs, co_attention_item))
            backward_items(g_ref.at[0], add_total(True))
            column_sums(0, 0, 1024)
            segments.append((1, clear_item))
            done = sum(count for count, _ in segments)
            segments.append((LANDING_TURN * PACE[0] // PACE[1] - done, None))
            for which in range(2):
                segments.append((1, landed(which)))
                backward_items(own_refs[which], add_total(False))
            column_sums(2, 1, 1024)
            segments.append((pairs, finish_item))
            return segments

        return forward, list_backward

    text_forward, text_backward = run(TEXT, text_lengths, region_counts)
    image_forward, image_backward = run(IMAGE, region_counts, text_lengths)
    pl.when(is_text)(text_forward)
    pl.when(jnp.logical_not(is_text))(image_forward)

    def run_items(segments, low_item, high_item):
        def one(item, carry):
            start = 0
            for count, work in segments:
                if work is not None:

                    @pl.when(jnp.logical_and(item >= start, item < start + count))
                    def _():
                        work(item - start)

                start += count
            return carry

        every = sum(count for count, _ in segments)
        lax.fori_loop(jnp.minimum(low_item, every), jnp.minimum(high_item, every), one, 0)

    def turn(step, carry):
        low_item = step * PACE[0] // PACE[1]
        high_item = (step + 1) * PACE[0] // PACE[1]

        @pl.when(is_text)
        def _():
            run_items(text_backward(), low_item, high_item)

        @pl.when(jnp.logical_not(is_text))
        def _():
            run_items(image_backward(), low_item, high_item)

        tick(step)
        return carry

    lax.fori_loop(0, unit_total + LAG_X + last * line_lag(line) + Z_SLOTS, turn, 0)
    finished = pltpu.make_async_copy(sums, sums_out, staged_sems.at[0])
    finished.start()
    unstage(1).wait()
    finished.wait()


def layer(line, text_lengths, region_counts, hidden, cotangent, weights):
    _, pairs, slots, width = hidden.shape
    tall = (slots + 15) // 16 * 16
    height = pairs * tall
    piece = 256 // line
    own_slots = slots_held(line)
    vmem = pl.BlockSpec(memory_space=pltpu.VMEM)
    smem = pl.BlockSpec(memory_space=pltpu.SMEM)
    anywhere = pl.BlockSpec(memory_space=pl.ANY)
    bf16, f32 = jnp.bfloat16, jnp.float32
    return pl.pallas_call(
        partial(layer_kernel, line, pairs, slots, tall),
        out_shape=(
            jax.ShapeDtypeStruct(hidden.shape, bf16),
            jax.ShapeDtypeStruct(hidden.shape, bf16),
            jax.ShapeDtypeStruct((piece, OUT_BLOCKS * UNIT), f32),
        ),
        in_specs=[smem] * 2 + [anywhere] * 8 + [vmem] * 5,
        out_specs=(anywhere,) * 3,
        scratch_shapes=[
            pltpu.VMEM((12, 2, 2, 256, height), bf16),
            pltpu.VMEM((16, height, 1024), bf16),
            pltpu.VMEM((piece, OUT_BLOCKS * UNIT), f32),
            pltpu.VMEM((LANES, 1024), f32),
            pltpu.VMEM((8, 3072), f32),
            pltpu.VMEM((2,) + hidden.shape[1:], bf16),
            pltpu.VMEM((RING, 1024, 1024), bf16),
            pltpu.VMEM((height, 1024), bf16),
            pltpu.VMEM((height, 1024), bf16),
            pltpu.VMEM((height, 1024), f32),
            pltpu.VMEM((height, 1024), f32),
            pltpu.VMEM((height, 1024), bf16),
            pltpu.VMEM((height, 1024), bf16),
            pltpu.VMEM((3, height, 1024), bf16),
            pltpu.VMEM((height, 4), f32),
            pltpu.VMEM((pairs, 8, 128, tall), bf16),
            pltpu.VMEM((pairs, 8, 112, tall), bf16),
            pltpu.VMEM((16, 1024), f32),
            pltpu.VMEM((8, 3072), f32),
            pltpu.SemaphoreType.DMA((RING,)),
            pltpu.SemaphoreType.DMA((2, pairs)),
            pltpu.SemaphoreType.DMA((2, pairs)),
            pltpu.SemaphoreType.DMA((2, pairs)),
            pltpu.SemaphoreType.DMA((2, pairs)),
            pltpu.SemaphoreType.REGULAR,
            pltpu.SemaphoreType.DMA((2,)),
            pltpu.VMEM((CORE_SLOTS, 2, 256, UNIT), bf16),
            pltpu.VMEM((CORE_SLOTS, 2, 256, UNIT), bf16),
            pltpu.VMEM((2, 2, 256, UNIT), f32),
            pltpu.VMEM((X_SLOTS, 256, UNIT), bf16),
            pltpu.VMEM((X_SLOTS, 256, UNIT), bf16),
            pltpu.VMEM((own_slots, 256, UNIT), f32),
            pltpu.VMEM((Z_SLOTS, 256, UNIT), bf16),
            pltpu.VMEM((Z_SLOTS, 256, UNIT), bf16),
            pltpu.VMEM((Z_SLOTS, 256, UNIT), bf16),
            pltpu.VMEM((Z_SLOTS, 256, UNIT), bf16),
            pltpu.SemaphoreType.DMA((2, CORE_SLOTS)),
            pltpu.SemaphoreType.DMA((2, X_SLOTS)),
            pltpu.SemaphoreType.DMA((2, Z_SLOTS, line)),
            pltpu.SemaphoreType.DMA((2, Z_SLOTS, line)),
            pltpu.SemaphoreType.REGULAR,
            pltpu.SemaphoreType.REGULAR,
        ],
        compiler_params=pltpu.CompilerParams(
            collective_id=0, has_side_effects=True, vmem_limit_bytes=VMEM_BYTES
        ),
        name="layer",
    )(text_lengths, region_counts, hidden, cotangent, *weights)


def place_kernel(
    line,
    result_in,
    grad_in,
    sums,
    result,
    grad,
    co_qkv,
    co_out,
    self_qkv,
    self_out,
    mlp_up,
    mlp_down,
    proj_bias,
    bias_up,
    bias_down,
    gain,
    shift,
    sems,
):
    piece = 256 // line

    def taken(first, width):
        return sums.at[:, pl.ds(first * UNIT, width)]

    moves = [
        (result_in, result),
        (grad_in, grad),
        (taken(12, 1024), co_out.at[0]),
        (taken(28, 1024), self_out.at[0]),
        (taken(32, 3072), mlp_up.at[0, 0]),
        (taken(44, 3072), mlp_up.at[0, 1]),
    ]
    for index in range(3):
        rows = pl.ds(index * piece, piece)
        moves += [
            (taken(4 * index, 1024), co_qkv.at[0, index]),
            (taken(16 + 4 * index, 1024), self_qkv.at[0, index]),
            (taken(56 + 4 * index, 1024), mlp_down.at[0, 0, rows]),
            (taken(68 + 4 * index, 1024), mlp_down.at[0, 1, rows]),
        ]
    copies = [
        pltpu.make_async_copy(source, target, sems.at[index])
        for index, (source, target) in enumerate(moves)
    ]
    for copy in copies:
        copy.start()
    rows = sums[:, 80 * UNIT : 80 * UNIT + LANES].T
    for half in range(2):
        proj_bias[0, half] = rows[3 * half : 3 * half + 3]
        for group in range(3):
            bias_up[0, half : half + 1, group * piece : (group + 1) * piece] = rows[
                6 + 3 * half + group : 7 + 3 * half + group
            ]
    bias_down[0] = rows[12:14]
    gain[0] = rows[14:18]
    shift[0] = rows[18:22]
    for copy in copies:
        copy.wait()


def place(line, result, grad, sums):
    piece = sums.shape[0]
    vmem = pl.BlockSpec(memory_space=pltpu.VMEM)
    anywhere = pl.BlockSpec(memory_space=pl.ANY)
    shapes = (
        (1, 3, piece, 1024),
        (1, piece, 1024),
        (1, 3, piece, 1024),
        (1, piece, 1024),
        (1, 2, piece, 3072),
        (1, 2, 3 * piece, 1024),
        (1, 2, 3, piece),
        (1, 2, 3 * piece),
        (1, 2, piece),
        (1, 4, piece),
        (1, 4, piece),
    )
    return pl.pallas_call(
        partial(place_kernel, line),
        out_shape=tuple(jax.ShapeDtypeStruct(result.shape, result.dtype) for _ in range(2))
        + tuple(jax.ShapeDtypeStruct(shape, jnp.float32) for shape in shapes),
        in_specs=[vmem] * 3,
        out_specs=(anywhere,) * 8 + (vmem,) * 5,
        scratch_shapes=[
            pltpu.SemaphoreType.DMA((18,)),
        ],
        name="place",
    )(result, grad, sums)


def on_device(
    hidden,
    text_lengths,
    region_counts,
    co_qkv,
    co_out,
    self_qkv,
    self_out,
    mlp_up,
    mlp_down,
    proj_bias,
    mlp_bias_up,
    mlp_bias_down,
    norm_gain_table,
    norm_bias,
    cotangent,
):
    line = lax.axis_size("dp") // 4
    result, grad, sums = layer(
        line,
        text_lengths,
        region_counts,
        hidden,
        cotangent,
        (
            co_qkv,
            co_out,
            self_qkv,
            self_out,
            mlp_up,
            mlp_down,
            proj_bias,
            mlp_bias_up,
            mlp_bias_down,
            norm_gain_table,
            norm_bias,
        ),
    )
    return place(line, result, grad, sums)


def solution(mesh):
    return jax.shard_map(
        on_device,
        mesh=mesh,
        in_specs=(
            P("stream", "dp", None, None),
            P("dp"),
            P("dp"),
            P("stream", None, None, None),
            P("stream", None, None),
            P("stream", None, None, None),
            P("stream", None, None),
            P("stream", None, None, None),
            P("stream", None, None, None),
            P("stream", None, None, None),
            P("stream", None, None),
            P("stream", None, None),
            P("stream", None, None),
            P("stream", None, None),
            P("stream", "dp", None, None),
        ),
        out_specs=(
            P("stream", "dp", None, None),
            P("stream", "dp", None, None),
            P("stream", None, "dp", None),
            P("stream", "dp", None),
            P("stream", None, "dp", None),
            P("stream", "dp", None),
            P("stream", None, "dp", None),
            P("stream", None, "dp", None),
            P("stream", None, None, "dp"),
            P("stream", None, "dp"),
            P("stream", None, "dp"),
            P("stream", None, "dp"),
            P("stream", None, "dp"),
        ),
        check_vma=False,
    )
```

```python
from functools import partial
from typing import NamedTuple
import math

import jax
import jax.numpy as jnp
from jax import lax
from jax.experimental import pallas as pl
from jax.experimental.pallas import tpu as pltpu
from jax.sharding import PartitionSpec as P

EPSILON = 1e-05
NEGATIVE = -1000000000.0
ROOT_HALF = 1.0 / math.sqrt(2.0)
GAUSS_NORM = 1.0 / math.sqrt(2.0 * math.pi)

MESH = pl.DeviceIdType.MESH
UNIT = 256
OUT_BLOCKS = 81
CORE_SLOTS = 4
Z_SLOTS = 6
SUM_LAG = 1
SUM_SLOTS = 4
VMEM_BYTES = 65200 * 1024

TEXT_UNITS = (
    (3, 3, 9, 1, 60, 0, 68, 4, 256),
    (1, 12, 5, 0, 44, 0, 44, 0, 192),
    (1, 3, 3, 0, 28, 0, 28, 0, 192),
    (3, 3, 2, 0, 16, 4, 16, 4, 192),
    (3, 3, 6, 1, 56, 0, 56, 4, 256),
    (1, 12, 4, 0, 32, 0, 32, 0, 192),
    (1, 3, 1, 0, 12, 0, 12, 0, 256),
    (3, 4, 0, 0, 0, 4, 0, 4, 192),
    (1, 1, 0, 0, 0, 0, 80, 0, 256),
)
IMAGE_UNITS = (
    (3, 4, 9, 1, 60, 0, 68, 4, 128),
    (1, 4, 5, 0, 44, 0, 44, 0, 256),
    (1, 4, 3, 0, 28, 0, 28, 0, 256),
    (3, 4, 2, 0, 16, 4, 16, 4, 256),
    (3, 4, 6, 1, 56, 0, 56, 4, 128),
    (1, 4, 4, 0, 32, 0, 32, 0, 256),
    (1, 4, 1, 0, 12, 0, 12, 0, 256),
    (3, 4, 0, 0, 0, 4, 0, 4, 256),
    (1, 1, 0, 0, 0, 0, 80, 0, 256),
)


def side_lag(line):
    return 6 if line <= 8 else 4


def line_lag(line):
    return 3 if line <= 8 else 1


def slots_held(line):
    return side_lag(line) + (line - 1) * line_lag(line) + 1 + SUM_LAG


def unit_count(table):
    return sum(entry[0] * entry[1] for entry in table)


def decode_one(table, unit):
    start = 0
    result = None
    for groups, blocks, a0, a1, g0, g1, o0, o1, kept in table:
        local = unit - start
        group = local // blocks
        block = local % blocks
        fields = (a0 + a1 * group, g0 + g1 * group + block, o0 + o1 * group + block, jnp.int32(kept))
        if result is None:
            result = fields
        else:
            result = tuple(jnp.where(unit >= start, new, old) for new, old in zip(fields, result))
        start += groups * blocks
    return result


def kept_one(table, unit):
    start = 0
    result = jnp.int32(table[0][-1])
    before = table[0][-1]
    for groups, blocks, *_, kept in table:
        if kept != before:
            result = jnp.where(unit >= start, kept, result)
            before = kept
        start += groups * blocks
    return result


def rows_kept(is_text, unit):
    return jnp.where(is_text, kept_one(TEXT_UNITS, unit), kept_one(IMAGE_UNITS, unit))


def decode(is_text, unit):
    text = decode_one(TEXT_UNITS, unit)
    image = decode_one(IMAGE_UNITS, unit)
    return tuple(jnp.where(is_text, one, other) for one, other in zip(text, image))


SENT = 104


class Stream(NamedTuple):
    asks: bool
    width: int
    inner: int
    split: int
    head: int
    own_keys: int
    order: tuple


SHORT = 64
TEXT = Stream(True, 768, 3072, 2, 64, SHORT, (0, 1, 2))
IMAGE = Stream(False, 1024, 1024, 1, 128, 112, (1, 2, 0))
TEXT_PACE = (36, 55, 4)
IMAGE_PACE = (42, 54, 4)
RING = 3
LANES = 128
TAIL = (
    0.28208317669832234,
    0.2824362970929616,
    0.24263030272423752,
    0.20467309203585946,
    -0.03157028123874516,
    0.28558060664263174,
    -0.4940359058844012,
    0.2879944144937219,
    -0.0597917499304742,
)


def gelu_parts(value):
    root = jnp.abs(value) * ROOT_HALF
    near = 1.0 / (1.0 + 0.5 * root)
    bell = jnp.exp(-(root * root))
    series = TAIL[-1] * near
    for factor in TAIL[-2::-1]:
        series = (series + factor) * near
    tail = 0.5 * bell * series
    below = jnp.where(value >= 0.0, 1.0 - tail, tail)
    return value * below, below + value * bell * GAUSS_NORM


def layer_kernel(
    line,
    pairs,
    slots,
    tall,
    text_lengths,
    region_counts,
    hidden,
    cotangent,
    co_qkv_whole,
    co_out_whole,
    self_qkv_whole,
    self_out_whole,
    mlp_up_whole,
    mlp_down_whole,
    proj_bias,
    bias_up,
    bias_down,
    gain,
    shift,
    result,
    grad,
    sums_out,
    at_ref,
    g_ref,
    vectors,
    hidden_vectors,
    staged,
    ring,
    far,
    far_query,
    state,
    total,
    low,
    active,
    normal,
    spread,
    self_probs,
    co_probs,
    params,
    up_params,
    ring_sems,
    send_sems,
    recv_sems,
    back_send_sems,
    back_recv_sems,
    landing_free,
    staged_sems,
    core_out,
    core_in,
    partial_own,
    x_out,
    x_in,
    own,
    down_out,
    down_in,
    up_out,
    up_in,
    core_sems,
    x_sems,
    down_sems,
    up_sems,
    down_free,
    up_free,
    sum_sems,
    blank_sems,
):
    stream = lax.axis_index("stream")
    place = lax.axis_index("dp")
    partner = (1 - stream, place)
    height = pairs * tall
    piece = 256 // line
    per_block = 256 // piece

    core = lax.rem(place, 2)
    side = lax.rem(place // 2, 2)
    spot = place // 4
    is_text = stream == 0
    unit_total = jnp.where(is_text, unit_count(TEXT_UNITS), unit_count(IMAGE_UNITS))
    core_device = (stream, place + 1 - 2 * core)
    side_device = (stream, place + 2 - 4 * side)
    lower_device = (stream, place - 4)
    upper_device = (stream, place + 4)
    own_slots = slots_held(line)
    last = line - 1
    co_qkv, co_out, self_qkv, self_out, mlp_up, mlp_down = (
        ref.at[0]
        for ref in (
            co_qkv_whole,
            co_out_whole,
            self_qkv_whole,
            self_out_whole,
            mlp_up_whole,
            mlp_down_whole,
        )
    )
    hidden_ref, cotangent_ref = staged.at[0], staged.at[1]
    result_ref, grad_ref = staged.at[0], staged.at[1]

    def stage(index):
        source = (hidden, cotangent)[index]
        return pltpu.make_async_copy(source.at[0], staged.at[index], staged_sems.at[index])

    def unstage(index):
        target = (result, grad)[index]
        return pltpu.make_async_copy(staged.at[index], target.at[0], staged_sems.at[index])

    stage(0).start()
    stage(1).start()
    far[...] = jnp.zeros_like(far)
    far_query[...] = jnp.zeros_like(far_query)

    barrier = pltpu.get_barrier_semaphore()
    for device in (partner, core_device, side_device):
        pl.semaphore_signal(barrier, inc=1, device_id=device, device_id_type=MESH)

    @pl.when(spot > 0)
    def _():
        pl.semaphore_signal(barrier, inc=1, device_id=lower_device, device_id_type=MESH)

    @pl.when(spot < last)
    def _():
        pl.semaphore_signal(barrier, inc=1, device_id=upper_device, device_id_type=MESH)

    pl.semaphore_wait(
        barrier, 3 + (spot > 0).astype(jnp.int32) + (spot < last).astype(jnp.int32)
    )
    for half in range(2):
        params[3 * half : 3 * half + 3] = proj_bias[0, half].astype(jnp.float32)
    params[6:8] = bias_down[0].astype(jnp.float32)
    params[8:12] = gain[0].astype(jnp.float32)
    params[12:16] = shift[0].astype(jnp.float32)
    up_params[0:2] = bias_up[0].astype(jnp.float32)
    vectors[...] = jnp.zeros_like(vectors)
    hidden_vectors[...] = jnp.zeros_like(hidden_vectors)

    state[0:piece] = jnp.zeros((piece, 1024), jnp.float32)

    def blank(index):
        width = min(1024, OUT_BLOCKS * UNIT - index * 1024)
        return pltpu.make_async_copy(
            state.at[pl.ds(0, piece), pl.ds(0, width)],
            sums_out.at[:, pl.ds(index * 1024, width)],
            blank_sems.at[index],
        )

    blanks = [blank(index) for index in range(-(-OUT_BLOCKS * UNIT // 1024))]
    for copy in blanks:
        copy.start()

    def block(index):
        return pl.ds(pl.multiple_of(index * UNIT, UNIT), UNIT)

    def pair_rows(pair, count=tall):
        return pl.ds(pl.multiple_of(pair * tall, tall), count)

    def exchange(source, source_at, target, target_at, sends, receives, which, pair):
        return pltpu.make_async_remote_copy(
            src_ref=source.at[source_at],
            dst_ref=target.at[target_at],
            send_sem=sends.at[which, pair],
            recv_sem=receives.at[which, pair],
            device_id=partner,
            device_id_type=MESH,
        )

    def short_rows(which, pair):
        return pl.ds(
            pl.multiple_of((which * pairs + pair) * SHORT, SHORT), SHORT
        )

    def ask(pair):
        at = pair_rows(pair, SENT)
        return exchange(g_ref.at[0], at, far_query, at, send_sems, recv_sems, 0, pair)

    def hand(which, pair):
        return exchange(
            g_ref.at[1 + which],
            pair_rows(pair, SHORT),
            far,
            short_rows(which, pair),
            send_sems,
            recv_sems,
            1 + which,
            pair,
        )

    def answer(pair):
        at = pair_rows(pair, SENT)
        return exchange(active, at, far, at, send_sems, recv_sems, 0, pair)

    def ask_back(pair):
        at = pair_rows(pair, SENT)
        return exchange(low, at, active, at, back_send_sems, back_recv_sems, 0, pair)

    def hand_back(which, pair):
        return exchange(
            far,
            short_rows(which, pair),
            g_ref.at[1 + which],
            pair_rows(pair, SHORT),
            back_send_sems,
            back_recv_sems,
            1 + which,
            pair,
        )

    def answer_back(pair):
        at = pair_rows(pair, SENT)
        return exchange(far_query, at, g_ref.at[0], at, back_send_sems, back_recv_sems, 0, pair)

    def for_rows(kept, body):
        for rows in (128, 192, 256):

            @pl.when(kept == rows)
            def _():
                body(rows)

    def core_copy(unit, rows):
        slot = lax.rem(unit, CORE_SLOTS)
        return pltpu.make_async_remote_copy(
            src_ref=core_out.at[slot, :, pl.ds(0, rows)],
            dst_ref=core_in.at[slot, :, pl.ds(0, rows)],
            send_sem=core_sems.at[0, slot],
            recv_sem=core_sems.at[1, slot],
            device_id=core_device,
            device_id_type=MESH,
        )

    def side_copy(unit, rows):
        slot = lax.rem(unit, 2 * side_lag(line))
        return pltpu.make_async_remote_copy(
            src_ref=x_out.at[slot, pl.ds(0, rows)],
            dst_ref=x_in.at[slot, pl.ds(0, rows)],
            send_sem=x_sems.at[0, slot],
            recv_sem=x_sems.at[1, slot],
            device_id=side_device,
            device_id_type=MESH,
        )

    def line_copy(source, target, sems, device, slot, index):
        at = pl.ds(pl.multiple_of(index * piece, piece), piece)
        return pltpu.make_async_remote_copy(
            src_ref=source.at[slot, at],
            dst_ref=target.at[slot, at],
            send_sem=sems.at[0, slot, index],
            recv_sem=sems.at[1, slot, index],
            device_id=device,
            device_id_type=MESH,
        )

    def columns(block):
        return pl.ds(pl.multiple_of(block * UNIT, UNIT), UNIT)

    def multiply(unit):
        a_block, g_block, out_block, kept = decode(is_text, unit)
        slot = lax.rem(unit, CORE_SLOTS)
        keep = lax.rem(unit, 2)
        is_vector = unit == unit_total - 1

        @pl.when(jnp.logical_not(is_vector))
        def _():
            gradient = g_ref[g_block // 4, :, columns(lax.rem(g_block, 4))]

            def body(rows):
                def product(which):
                    operand = at_ref[a_block, which, :, pl.ds(0, rows)]
                    return jnp.dot(
                        operand.reshape(2 * rows, operand.shape[-1]),
                        gradient,
                        preferred_element_type=jnp.float32,
                    ).reshape(2, rows, UNIT)

                core_out[slot, :, pl.ds(0, rows)] = product(1 - core).astype(jnp.bfloat16)
                core_copy(unit, rows).start()
                partial_own[keep, :, pl.ds(0, rows)] = product(core)

            for_rows(kept, body)

        @pl.when(is_vector)
        def _():
            place_vectors(slot, keep)
            core_copy(unit, 256).start()

    def add_core(unit):
        kept = rows_kept(is_text, unit)
        slot = lax.rem(unit, CORE_SLOTS)
        keep = lax.rem(unit, 2)
        far = lax.rem(unit, 2 * side_lag(line))
        store = lax.rem(unit, own_slots)

        def body(rows):
            core_copy(unit, rows).wait()
            at = pl.ds(0, rows)
            x_out[far, at] = (
                partial_own[keep, 1 - side, at] + core_in[slot, 1 - side, at].astype(jnp.float32)
            ).astype(jnp.bfloat16)
            side_copy(unit, rows).start()
            own[store, at] = partial_own[keep, side, at] + core_in[slot, side, at].astype(
                jnp.float32
            )

        for_rows(kept, body)

    def add_side(unit):
        kept = rows_kept(is_text, unit)
        far = lax.rem(unit, 2 * side_lag(line))
        store = lax.rem(unit, own_slots)

        def body(rows):
            side_copy(unit, rows).wait()
            at = pl.ds(0, rows)
            own[store, at] += x_in[far, at].astype(jnp.float32)

        for_rows(kept, body)

    def sum_copy(unit, out_block):
        at = pl.ds(pl.multiple_of(spot * piece, piece), piece)
        return pltpu.make_async_copy(
            own.at[lax.rem(unit, own_slots), at],
            sums_out.at[:, columns(out_block)],
            sum_sems.at[lax.rem(unit, SUM_SLOTS)],
        )

    def has_sum(unit):
        return (spot + 1) * piece <= rows_kept(is_text, unit)

    def line_step(unit, source, target, sems, free, sender, reader, low, high, gives, takes):
        slot = lax.rem(unit + Z_SLOTS, Z_SLOTS)

        @pl.when(jnp.logical_and(unit >= Z_SLOTS, gives))
        def _():
            count = rows_kept(is_text, unit - Z_SLOTS) // piece
            pl.semaphore_wait(free, 1)

            def settle(index, carry):
                line_copy(source, target, sems, reader, slot, index).wait_send()
                return carry

            lax.fori_loop(low(count), high(count), settle, 0)

        @pl.when(unit < unit_total)
        def _():
            count = rows_kept(is_text, unit) // piece
            store = lax.rem(unit, own_slots)

            def at(index):
                return pl.ds(pl.multiple_of(index * piece, piece), piece)

            @pl.when(gives)
            def _():
                def forward(index, carry):
                    @pl.when(takes)
                    def _():
                        line_copy(source, target, sems, reader, slot, index).wait_recv()
                        source[slot, at(index)] = (
                            own[store, at(index)] + target[slot, at(index)].astype(jnp.float32)
                        ).astype(jnp.bfloat16)

                    @pl.when(jnp.logical_not(takes))
                    def _():
                        source[slot, at(index)] = own[store, at(index)].astype(jnp.bfloat16)

                    line_copy(source, target, sems, reader, slot, index).start()
                    return carry

                lax.fori_loop(low(count), high(count), forward, 0)

            @pl.when(takes)
            def _():
                @pl.when(spot < count)
                def _():
                    line_copy(source, target, sems, reader, slot, spot).wait_recv()
                    own[store, at(spot)] += target[slot, at(spot)].astype(jnp.float32)

                pl.semaphore_signal(free, inc=1, device_id=sender, device_id_type=MESH)

    def tick(step):
        @pl.when(step < unit_total)
        def _():
            multiply(step)

        @pl.when(jnp.logical_and(step >= 1, step < unit_total + 1))
        def _():
            add_core(step - 1)

        @pl.when(jnp.logical_and(step >= side_lag(line), step < unit_total + side_lag(line)))
        def _():
            add_side(step - side_lag(line))

        falling = step - side_lag(line) - (last - spot) * line_lag(line)

        @pl.when(jnp.logical_and(falling >= 0, falling < unit_total + Z_SLOTS))
        def _():
            line_step(
                falling,
                down_out,
                down_in,
                down_sems,
                down_free,
                upper_device,
                lower_device,
                lambda count: 0,
                lambda count: jnp.minimum(spot, count),
                spot > 0,
                spot < last,
            )

        rising = step - side_lag(line) - spot * line_lag(line)

        @pl.when(jnp.logical_and(rising >= 0, rising < unit_total + Z_SLOTS))
        def _():
            line_step(
                rising,
                up_out,
                up_in,
                up_sems,
                up_free,
                lower_device,
                upper_device,
                lambda count: jnp.minimum(spot + 1, count),
                lambda count: count,
                spot < last,
                spot > 0,
            )

        final = step - side_lag(line) - last * line_lag(line)

        @pl.when(jnp.logical_and(final >= 0, final < unit_total))
        def _():
            pl.when(has_sum(final))(lambda: sum_copy(final, decode(is_text, final)[2]).start())

        settled = final - SUM_LAG

        @pl.when(jnp.logical_and(settled >= 0, settled < unit_total))
        def _():
            pl.when(has_sum(settled))(lambda: sum_copy(settled, 0).wait())

    def place_vectors(slot, keep):
        turned = jnp.concatenate(
            [vectors[...], jnp.zeros((LANES - 32, 1024), jnp.float32)], axis=0
        ).T
        tall_sums = hidden_vectors[...].T
        lane = lax.broadcasted_iota(jnp.int32, (piece, LANES), 1)
        for owner in range(4 * line):
            value = turned[owner * piece : (owner + 1) * piece]
            for group in range(3):
                number = owner * 3 + group
                part = tall_sums[number * piece : (number + 1) * piece]
                for which in range(2):
                    value = jnp.where(
                        lane == 6 + 3 * which + group, part[:, which : which + 1], value
                    )
            total[
                owner // 8 * piece : (owner // 8 + 1) * piece,
                owner % 8 * LANES : (owner % 8 + 1) * LANES,
            ] = value
        core_out[slot] = jnp.zeros((2, 256, UNIT), jnp.bfloat16)
        partial_own[keep] = jnp.zeros((2, 256, UNIT), jnp.float32)

        def step(owner, carry):
            value = total[
                pl.ds(pl.multiple_of(owner // 8 * piece, piece), piece),
                pl.ds(pl.multiple_of(lax.rem(owner, 8) * LANES, LANES), LANES),
            ]
            at = pl.ds(pl.multiple_of((owner // 4) * piece, piece), piece)
            half = lax.rem(owner // 2, 2)

            @pl.when(lax.rem(owner, 2) == core)
            def _():
                partial_own[keep, half, at, 0:LANES] = value

            @pl.when(lax.rem(owner, 2) != core)
            def _():
                core_out[slot, half, at, 0:LANES] = value.astype(jnp.bfloat16)

            return carry

        lax.fori_loop(0, 4 * line, step, 0)

    def run(cfg, own_lengths, far_lengths):
        width, inner = cfg.width, cfg.inner
        chunks = inner // 1024
        groups = width // LANES

        plan = [co_qkv.at[index, pl.ds(0, width)] for index in cfg.order]
        plan.append(co_out.at[:, pl.ds(0, width)])

        def mlp_plan(index, chunk):
            at = pl.ds(chunk * 1024, 1024)
            return mlp_up.at[index, pl.ds(0, width), at], mlp_down.at[index, at, pl.ds(0, width)]

        def square(index):
            return self_qkv.at[index, pl.ds(0, width), pl.ds(0, width)]

        for chunk in range(chunks):
            plan.extend(mlp_plan(0, chunk))
        plan.extend(square(index) for index in range(3))
        plan.append(self_out.at[pl.ds(0, width), pl.ds(0, width)])
        for chunk in range(chunks):
            plan.extend(mlp_plan(1, chunk))
        for chunk in range(chunks):
            plan.extend(mlp_plan(1, chunk)[::-1])
        plan.append(self_out.at[pl.ds(0, width), pl.ds(0, width)])
        plan.extend(square(index) for index in range(3))
        for chunk in range(chunks):
            plan.extend(mlp_plan(0, chunk)[::-1])
        plan.append(co_out.at[:, pl.ds(0, width)])
        plan.extend(co_qkv.at[index, pl.ds(0, width)] for index in range(3))

        def fetch(index):
            rows, columns = plan[index].shape
            return pltpu.make_async_copy(
                plan[index],
                ring.at[index % RING, pl.ds(0, rows), pl.ds(0, columns)],
                ring_sems.at[index % RING],
            )

        used = [0]
        def with_weight(body):
            index = used[0]
            used[0] += 1
            fetch(index).wait()
            rows, columns = plan[index].shape
            body(ring.at[index % RING], rows, columns)
            if index + RING < len(plan):
                fetch(index + RING).start()

        def forward_product(source, consume):
            def body(weight, rows, columns):
                def step(index, carry):
                    consume(
                        index,
                        jnp.dot(
                            source[:, 0:rows],
                            weight[0:rows, block(index)],
                            preferred_element_type=jnp.float32,
                        ),
                    )
                    return carry

                lax.fori_loop(0, columns // UNIT, step, 0)

            with_weight(body)

        segments = []

        def backward_items(source, consume):
            index = used[0]
            used[0] += 1
            rows, columns = plan[index].shape
            weight = ring.at[index % RING]
            count = rows // UNIT

            def item(number):
                @pl.when(number == 0)
                def _():
                    fetch(index).wait()

                consume(
                    number,
                    lax.dot_general(
                        source[:, 0:columns],
                        weight[block(number), 0:columns],
                        (((1,), (1,)), ((), ())),
                        preferred_element_type=jnp.float32,
                    ),
                )
                if index + RING < len(plan):

                    @pl.when(number == count - 1)
                    def _():
                        fetch(index + RING).start()

            segments.append((count, item))

        def add_total(first):
            def consume(index, value):
                if first:
                    total[:, block(index)] = value
                else:
                    total[:, block(index)] += value

            return consume

        def put_rows(at_block, index, value):
            turned = value.T
            for part in range(per_block):
                at_ref[
                    at_block,
                    part % 2,
                    (part // 2) % 2,
                    pl.ds(pl.multiple_of((index * (per_block // 4) + part // 4) * piece, piece), piece),
                ] = turned[part * piece : (part + 1) * piece]

        def put_hidden_rows(at_block, index, value):
            turned = value.T
            for part in range(per_block):
                number = index * per_block + part
                owner = number // 3
                at_ref[
                    at_block + lax.rem(number, 3),
                    lax.rem(owner, 2),
                    lax.rem(owner // 2, 2),
                    pl.ds(pl.multiple_of((owner // 4) * piece, piece), piece),
                ] = turned[part * piece : (part + 1) * piece]

        def put_low(at_block, columns, source=low):
            def step(index, carry):
                put_rows(at_block, index, source[:, block(index)])
                return carry

            lax.fori_loop(0, columns // UNIT, step, 0)

        def for_pairs(body):
            def step(pair, carry):
                body(pair)
                return carry

            lax.fori_loop(0, pairs, step, 0)

        def mean(value):
            return jnp.sum(value, axis=-1, keepdims=True) * (1.0 / width)

        def normalize(value):
            centered = value - mean(value)
            inverse = lax.rsqrt(mean(centered * centered) + EPSILON)
            return centered * inverse, inverse

        def norm_forward(index, bias_row, at_block):
            def body(pair):
                at = pair_rows(pair)
                rows, inverse = normalize(
                    state[at, 0:width] + total[at, 0:width] + params[bias_row : bias_row + 1, 0:width]
                )
                result = (
                    rows * params[8 + index : 9 + index, 0:width]
                    + params[12 + index : 13 + index, 0:width]
                )
                state[at, 0:width] = result
                low[at, 0:width] = result.astype(jnp.bfloat16)
                normal[index, at, 0:width] = rows.astype(jnp.bfloat16)
                spread[at, index : index + 1] = inverse

            for_pairs(body)
            put_low(at_block, width)

        def add_row(ref, row, value):
            ref[row : row + 1, 0 : value.shape[-1]] += jnp.sum(value, axis=0, keepdims=True)

        def norm_gradient(index, at, gradient, rows, inverse, g_block, bias_row):
            scaled = gradient * params[8 + index : 9 + index, 0:width]
            result = inverse * (scaled - mean(scaled) - rows * mean(scaled * rows))
            state[at, 0:width] = result
            rounded = result.astype(jnp.bfloat16)
            g_ref[g_block, at, 0:width] = rounded
            add_row(vectors, 14 + index, gradient * rows)
            add_row(vectors, 18 + index, gradient)
            add_row(vectors, bias_row if bias_row < 6 else bias_row + 6, rounded.astype(jnp.float32))

        def norm_backward(index, g_block, bias_row):
            def body(pair):
                at = pair_rows(pair)
                norm_gradient(
                    index,
                    at,
                    state[at, 0:width] + total[at, 0:width],
                    normal[index, at, 0:width].astype(jnp.float32),
                    spread[at, index : index + 1],
                    g_block,
                    bias_row,
                )

            segments.append((pairs, body))

        def mlp_forward(index):
            for chunk in range(chunks):

                def activate(number, value):
                    act, slope = gelu_parts(
                        value
                        + up_params[
                            index : index + 1,
                            pl.ds(pl.multiple_of(chunk * 1024 + number * UNIT, UNIT), UNIT),
                        ]
                    )
                    act = act.astype(jnp.bfloat16)
                    active[:, block(number)] = act
                    g_ref[8 + 3 * index + chunk, :, block(number)] = slope.astype(jnp.bfloat16)
                    put_hidden_rows(6 + 3 * index, chunk * 4 + number, act)

                forward_product(low, activate)
                forward_product(active, add_total(chunk == 0))

        def mlp_backward(index):
            for chunk in range(chunks):
                g_block = 8 + 3 * index + chunk

                def through(number, value, g_block=g_block, chunk=chunk):
                    slope = g_ref[g_block, :, block(number)].astype(jnp.float32)
                    rounded = (value * slope).astype(jnp.bfloat16)
                    g_ref[g_block, :, block(number)] = rounded
                    hidden_vectors[
                        index : index + 1,
                        pl.ds(pl.multiple_of(chunk * 1024 + number * UNIT, UNIT), UNIT),
                    ] = jnp.sum(rounded.astype(jnp.float32), axis=0, keepdims=True)

                backward_items(g_ref.at[14 + index], through)
                backward_items(g_ref.at[g_block], add_total(chunk == 0))

        def biased(target, bias_row):
            def consume(index, value):
                if bias_row is not None:
                    value = value + params[bias_row : bias_row + 1, block(index)]
                target[:, block(index)] = value.astype(jnp.bfloat16)

            return consume

        def column_sums(g_block, row, columns):
            def item(index):
                vectors[row : row + 1, block(index)] = jnp.sum(
                    g_ref[g_block, :, block(index)].astype(jnp.float32), axis=0, keepdims=True
                )

            segments.append((columns // UNIT, item))

        def stacked(value, split):
            if split == 1:
                return value
            lane = lax.broadcasted_iota(jnp.int32, value.shape, 1)
            zero = jnp.zeros_like(value)
            return jnp.concatenate(
                [jnp.where(lane < 64, value, zero), jnp.where(lane < 64, zero, value)], axis=0
            )

        def unstacked(value, split):
            if split == 1:
                return value
            half = value.shape[0] // 2
            lane = lax.broadcasted_iota(jnp.int32, (half, LANES), 1)
            return jnp.where(lane < 64, value[:half], value[half:])

        def over_keys(reduce, value, split):
            if split == 1:
                return reduce(value, axis=0, keepdims=True)
            half = value.shape[0] // 2
            return jnp.concatenate(
                [
                    jnp.broadcast_to(
                        reduce(part, axis=0, keepdims=True), part.shape
                    )
                    for part in (value[:half], value[half:])
                ],
                axis=0,
            )

        last_last = (((1,), (1,)), ((), ()))
        first_first = (((0,), (0,)), ((), ()))

        def attend_forward(query, keys, values, key_rows, probs, target, lengths, split, head, group_count):
            scale = 1.0 / math.sqrt(head)

            def body(pair):
                length = lengths[pair]
                for group in range(group_count):
                    at = pl.ds(group * LANES, LANES)
                    key = stacked(keys[key_rows(pair), at], split)
                    value = stacked(values[key_rows(pair), at], split)
                    count = key.shape[0] // split
                    scores = (
                        lax.dot_general(
                            key,
                            query[pair_rows(pair), at],
                            last_last,
                            preferred_element_type=jnp.float32,
                        )
                        * scale
                    )
                    number = lax.broadcasted_iota(jnp.int32, scores.shape, 0)
                    if split == 2:
                        number = jnp.where(number < count, number, number - count)
                    scores = jnp.where(number < length, scores, NEGATIVE)
                    raised = jnp.exp(scores - over_keys(jnp.max, scores, split))
                    shares = (raised * (1.0 / over_keys(jnp.sum, raised, split))).astype(
                        jnp.bfloat16
                    )
                    probs[pair, group, 0 : count * split] = shares
                    target[pair_rows(pair), at] = lax.dot_general(
                        shares,
                        value,
                        first_first,
                        preferred_element_type=jnp.float32,
                    ).astype(jnp.bfloat16)

            return body

        def attend_backward(query, keys, values, key_rows, probs, source, split, head, group_count):
            scale = 1.0 / math.sqrt(head)

            def body(pair):
                for group in range(group_count):
                    at = pl.ds(group * LANES, LANES)
                    key = stacked(keys[key_rows(pair), at], split)
                    value = stacked(values[key_rows(pair), at], split)
                    count = key.shape[0] // split
                    asked = query[pair_rows(pair), at]
                    gradient = source[pair_rows(pair), at]
                    rounded_shares = probs[pair, group, 0 : count * split]
                    shares = rounded_shares.astype(jnp.float32)
                    grad_shares = lax.dot_general(
                        value, gradient, last_last, preferred_element_type=jnp.float32
                    )
                    grad_scores = (
                        shares
                        * (grad_shares - over_keys(jnp.sum, grad_shares * shares, split))
                        * scale
                    ).astype(jnp.bfloat16)
                    grad_value = unstacked(
                        jnp.dot(
                            rounded_shares,
                            gradient,
                            preferred_element_type=jnp.float32,
                        ),
                        split,
                    )
                    grad_key = unstacked(
                        jnp.dot(grad_scores, asked, preferred_element_type=jnp.float32), split
                    )
                    grad_query = lax.dot_general(
                        grad_scores, key, first_first, preferred_element_type=jnp.float32
                    )
                    query[pair_rows(pair), at] = grad_query.astype(jnp.bfloat16)
                    keys[key_rows(pair), at] = grad_key.astype(jnp.bfloat16)
                    values[key_rows(pair), at] = grad_value.astype(jnp.bfloat16)

            return body

        def clear_tail(ref, pair, count):
            if count < tall:
                at = pl.ds(pl.multiple_of(pair * tall + count, 16), tall - count)
                ref[at, :] = jnp.zeros((tall - count, ref.shape[-1]), ref.dtype)

        own_refs = (g_ref.at[1], g_ref.at[2])
        def clear_rest(ref, pair):
            ref[pair * tall + SENT : (pair + 1) * tall] = jnp.zeros((tall - SENT, 1024), ref.dtype)

        self_refs = (g_ref.at[4], g_ref.at[5], g_ref.at[6])
        short_refs = (far.at[pl.ds(0, pairs * SHORT)], far.at[pl.ds(pairs * SHORT, pairs * SHORT)])

        def own_rows(pair):
            return pair_rows(pair, cfg.own_keys)

        def far_rows(pair):
            return pl.ds(pl.multiple_of(pair * SHORT, SHORT), SHORT)

        near_attention = (g_ref.at[0], *short_refs, far_rows, co_probs.at[:, pl.ds(8, 8)])
        far_attention = (far_query, *own_refs, own_rows, co_probs.at[:, pl.ds(0, 8)])
        self_attention = (*self_refs, own_rows, self_probs)

        def forward():
            for index in range(RING):
                fetch(index).start()
            if inner < 3072:
                for which in range(6, 12):
                    at_ref[which, :, :, 0:128] = jnp.zeros((2, 2, 128, height), jnp.bfloat16)
            low[...] = jnp.zeros_like(low)
            stage(0).wait()
            for pair in range(pairs):
                low[pair * tall : pair * tall + slots, 0:width] = hidden_ref[pair, :, 0:width]
            for index in cfg.order:
                forward_product(low, biased(g_ref.at[index], (0, None, 1)[index]))
                if cfg.asks and index == 0:
                    for pair in range(pairs):
                        ask(pair).start()
            put_low(0, width)
            for copy in blanks:
                copy.wait()
            state[:, 0:width] = low[:, 0:width].astype(jnp.float32)
            if cfg.asks:
                for pair in range(pairs):
                    ask(pair).wait_send()
                    clear_rest(g_ref.at[0], pair)
                for which in range(2):
                    for pair in range(pairs):
                        hand(which, pair).start()
                for pair in range(pairs):
                    answer(pair).wait_recv()
                context = far.at[pl.ds(0, height)]
                put_low(1, 1024, context)
                forward_product(context, add_total(True))
                norm_forward(0, 2, 4)
            else:

                def reply(pair):
                    ask(pair).wait_recv()
                    attend_forward(*far_attention, active, own_lengths, 1, 128, 8)(pair)
                    answer(pair).start()

                for_pairs(reply)

                def attend(pair):
                    for which in range(2):
                        hand(which, pair).wait_recv()
                    attend_forward(*near_attention, low, far_lengths, 1, 128, 8)(pair)

                for_pairs(attend)
                for pair in range(pairs):
                    answer(pair).wait_send()
                put_low(1, 1024)
                forward_product(low, add_total(True))
                norm_forward(0, 2, 4)
            mlp_forward(0)
            norm_forward(1, 6, 2)
            if cfg.asks:
                for pair in range(pairs):
                    for which in range(2):
                        hand(which, pair).wait_send()
                        clear_tail(own_refs[which], pair, SHORT)
                pl.semaphore_signal(landing_free, inc=1, device_id=partner, device_id_type=MESH)
            for index, bias_row in ((0, 3), (1, None), (2, 4)):
                forward_product(low, biased(self_refs[index], bias_row))
            for_pairs(
                attend_forward(*self_attention, low, own_lengths, cfg.split, cfg.head, groups)
            )
            put_low(3, width)
            forward_product(low, add_total(True))
            norm_forward(2, 5, 5)
            mlp_forward(1)
            if not cfg.asks:
                for pair in range(pairs):
                    clear_rest(active, pair)
                pl.semaphore_signal(landing_free, inc=1, device_id=partner, device_id_type=MESH)

            if width < 1024:
                result_ref[...] = jnp.zeros_like(result_ref)
            stage(1).wait()

            def last_norm(pair):
                at = pair_rows(pair)
                rows, inverse = normalize(
                    state[at, 0:width] + total[at, 0:width] + params[7:8, 0:width]
                )
                result = rows * params[11:12, 0:width] + params[15:16, 0:width]
                result_ref[pair, :, 0:width] = result[0:slots].astype(jnp.bfloat16)
                total[at, 0:width] = jnp.zeros((tall, width), jnp.float32)
                total[pl.ds(pl.multiple_of(pair * tall, tall), slots), 0:width] = cotangent_ref[
                    pair, :, 0:width
                ].astype(jnp.float32)
                norm_gradient(3, at, total[at, 0:width], rows, inverse, 15, 7)

            for_pairs(last_norm)
            unstage(0).start()


        def self_attention_item(pair):
            attend_backward(*self_attention, low, cfg.split, cfg.head, groups)(pair)
            for ref in self_refs[1:]:
                clear_tail(ref, pair, cfg.own_keys)

        def partner_ready(pair):
            @pl.when(pair == 0)
            def _():
                pl.semaphore_wait(landing_free, 1)

        def ask_item(pair):
            partner_ready(pair)
            ask_back(pair).start()

        def near_item(pair):
            attend_backward(*near_attention, low, 1, 128, 8)(pair)
            partner_ready(pair)
            for which in range(2):
                hand_back(which, pair).start()

        def answer_item(pair):
            ask_back(pair).wait_recv()
            attend_backward(*far_attention, active, 1, 128, 8)(pair)
            answer_back(pair).start()

        def landed_item(pair):
            if cfg.asks:
                answer_back(pair).wait_recv()
                ask_back(pair).wait_send()
                for which in range(2):
                    hand_back(which, pair).wait_recv()
            else:
                answer_back(pair).wait_send()
                for which in range(2):
                    hand_back(which, pair).wait_send()

        def clear_item(number):
            unstage(0).wait()
            if width < 1024:
                grad_ref[...] = jnp.zeros_like(grad_ref)

        def finish_item(pair):
            at = pl.ds(pl.multiple_of(pair * tall, tall), slots)
            grad_ref[pair, :, 0:width] = (state[at, 0:width] + total[at, 0:width]).astype(
                jnp.bfloat16
            )

            @pl.when(pair == pairs - 1)
            def _():
                unstage(1).start()

        def list_backward():
            mlp_backward(1)
            norm_backward(2, 7, 5)
            backward_items(g_ref.at[7], biased(low, None))
            segments.append((pairs, self_attention_item))
            for index in range(3):
                backward_items(self_refs[index], add_total(index == 0))
            column_sums(4, 3, width)
            column_sums(6, 4, width)
            norm_backward(1, 14, 6)
            mlp_backward(0)
            norm_backward(0, 3, 2)
            backward_items(g_ref.at[3], biased(low, None))

            if cfg.asks:
                segments.append((pairs, ask_item))
                segments.append((1, clear_item))
                early = sum(count for count, _ in segments)
                segments.append((pairs, landed_item))
                backward_items(g_ref.at[0], add_total(True))
                column_sums(0, 0, 1024)
            else:
                segments.append((pairs, near_item))
                backward_items(g_ref.at[0], add_total(True))
                column_sums(0, 0, 1024)
                segments.append((1, clear_item))
                early = sum(count for count, _ in segments)
                segments.append((pairs, answer_item))
            for which in range(2):
                backward_items(own_refs[which], add_total(False))
            column_sums(2, 1, 1024)
            if not cfg.asks:
                segments.append((pairs, landed_item))
            segments.append((pairs, finish_item))
            return early, segments

        return forward, list_backward

    text_forward, text_backward = run(TEXT, text_lengths, region_counts)
    image_forward, image_backward = run(IMAGE, region_counts, text_lengths)
    pl.when(is_text)(text_forward)
    pl.when(jnp.logical_not(is_text))(image_forward)

    def run_items(step, pace, early, segments):
        spread, held, rate = pace
        every = sum(count for count, _ in segments)

        def ahead_of(turn):
            first = jnp.minimum(turn * early // spread, early)
            return jnp.minimum(first + jnp.maximum(turn - held, 0) * rate, every)

        def dispatch(item, some, start):
            if len(some) == 1:
                some[0][1](item - start)
                return
            half = len(some) // 2
            middle = start + sum(count for count, _ in some[:half])
            pl.when(item < middle)(lambda: dispatch(item, some[:half], start))
            pl.when(item >= middle)(lambda: dispatch(item, some[half:], middle))

        def one(item, carry):
            dispatch(item, segments, 0)
            return carry

        lax.fori_loop(ahead_of(step), ahead_of(step + 1), one, 0)

    def turn(step, carry):
        @pl.when(is_text)
        def _():
            run_items(step, TEXT_PACE, *text_backward())

        @pl.when(jnp.logical_not(is_text))
        def _():
            run_items(step, IMAGE_PACE, *image_backward())

        tick(step)
        return carry

    lax.fori_loop(0, unit_total + side_lag(line) + last * line_lag(line) + Z_SLOTS, turn, 0)
    unstage(1).wait()


def layer(line, text_lengths, region_counts, hidden, cotangent, weights):
    _, pairs, slots, width = hidden.shape
    tall = (slots + 15) // 16 * 16
    height = pairs * tall
    piece = 256 // line
    own_slots = slots_held(line)
    vmem = pl.BlockSpec(memory_space=pltpu.VMEM)
    smem = pl.BlockSpec(memory_space=pltpu.SMEM)
    anywhere = pl.BlockSpec(memory_space=pl.ANY)
    bf16, f32 = jnp.bfloat16, jnp.float32
    return pl.pallas_call(
        partial(layer_kernel, line, pairs, slots, tall),
        out_shape=(
            jax.ShapeDtypeStruct(hidden.shape, bf16),
            jax.ShapeDtypeStruct(hidden.shape, bf16),
            jax.ShapeDtypeStruct((piece, OUT_BLOCKS * UNIT), f32),
        ),
        in_specs=[smem] * 2 + [anywhere] * 8 + [vmem] * 5,
        out_specs=(anywhere,) * 3,
        scratch_shapes=[
            pltpu.VMEM((12, 2, 2, 256, height), bf16),
            pltpu.VMEM((16, height, 1024), bf16),
            pltpu.VMEM((32, 1024), f32),
            pltpu.VMEM((8, 3072), f32),
            pltpu.VMEM((2,) + hidden.shape[1:], bf16),
            pltpu.VMEM((RING, 1024, 1024), bf16),
            pltpu.VMEM((pairs * 2 * SHORT, 1024), bf16),
            pltpu.VMEM((height, 1024), bf16),
            pltpu.VMEM((height, 1024), f32),
            pltpu.VMEM((height, 1024), f32),
            pltpu.VMEM((height, 1024), bf16),
            pltpu.VMEM((height, 1024), bf16),
            pltpu.VMEM((3, height, 1024), bf16),
            pltpu.VMEM((height, 4), f32),
            pltpu.VMEM((pairs, 8, 128, tall), bf16),
            pltpu.VMEM((pairs, 16, 112, tall), bf16),
            pltpu.VMEM((16, 1024), f32),
            pltpu.VMEM((8, 3072), f32),
            pltpu.SemaphoreType.DMA((RING,)),
            pltpu.SemaphoreType.DMA((3, pairs)),
            pltpu.SemaphoreType.DMA((3, pairs)),
            pltpu.SemaphoreType.DMA((3, pairs)),
            pltpu.SemaphoreType.DMA((3, pairs)),
            pltpu.SemaphoreType.REGULAR,
            pltpu.SemaphoreType.DMA((2,)),
            pltpu.VMEM((CORE_SLOTS, 2, 256, UNIT), bf16),
            pltpu.VMEM((CORE_SLOTS, 2, 256, UNIT), bf16),
            pltpu.VMEM((2, 2, 256, UNIT), f32),
            pltpu.VMEM((2 * side_lag(line), 256, UNIT), bf16),
            pltpu.VMEM((2 * side_lag(line), 256, UNIT), bf16),
            pltpu.VMEM((own_slots, 256, UNIT), f32),
            pltpu.VMEM((Z_SLOTS, 256, UNIT), bf16),
            pltpu.VMEM((Z_SLOTS, 256, UNIT), bf16),
            pltpu.VMEM((Z_SLOTS, 256, UNIT), bf16),
            pltpu.VMEM((Z_SLOTS, 256, UNIT), bf16),
            pltpu.SemaphoreType.DMA((2, CORE_SLOTS)),
            pltpu.SemaphoreType.DMA((2, 2 * side_lag(line))),
            pltpu.SemaphoreType.DMA((2, Z_SLOTS, line)),
            pltpu.SemaphoreType.DMA((2, Z_SLOTS, line)),
            pltpu.SemaphoreType.REGULAR,
            pltpu.SemaphoreType.REGULAR,
            pltpu.SemaphoreType.DMA((SUM_SLOTS,)),
            pltpu.SemaphoreType.DMA((-(-OUT_BLOCKS * UNIT // 1024),)),
        ],
        compiler_params=pltpu.CompilerParams(
            collective_id=0, has_side_effects=True, vmem_limit_bytes=VMEM_BYTES
        ),
        name="layer",
    )(text_lengths, region_counts, hidden, cotangent, *weights)


def place_kernel(
    line,
    result_in,
    grad_in,
    sums,
    result,
    grad,
    co_qkv,
    co_out,
    self_qkv,
    self_out,
    mlp_up,
    mlp_down,
    proj_bias,
    bias_up,
    bias_down,
    gain,
    shift,
    sems,
):
    piece = 256 // line

    def taken(first, width):
        return sums.at[:, pl.ds(first * UNIT, width)]

    moves = [
        (result_in, result),
        (grad_in, grad),
        (taken(12, 1024), co_out.at[0]),
        (taken(28, 1024), self_out.at[0]),
        (taken(32, 3072), mlp_up.at[0, 0]),
        (taken(44, 3072), mlp_up.at[0, 1]),
    ]
    for index in range(3):
        rows = pl.ds(index * piece, piece)
        moves += [
            (taken(4 * index, 1024), co_qkv.at[0, index]),
            (taken(16 + 4 * index, 1024), self_qkv.at[0, index]),
            (taken(56 + 4 * index, 1024), mlp_down.at[0, 0, rows]),
            (taken(68 + 4 * index, 1024), mlp_down.at[0, 1, rows]),
        ]
    copies = [
        pltpu.make_async_copy(source, target, sems.at[index])
        for index, (source, target) in enumerate(moves)
    ]
    for copy in copies:
        copy.start()
    rows = sums[:, 80 * UNIT : 80 * UNIT + LANES].T
    for half in range(2):
        proj_bias[0, half] = rows[3 * half : 3 * half + 3]
        for group in range(3):
            bias_up[0, half : half + 1, group * piece : (group + 1) * piece] = rows[
                6 + 3 * half + group : 7 + 3 * half + group
            ]
    bias_down[0] = rows[12:14]
    gain[0] = rows[14:18]
    shift[0] = rows[18:22]
    for copy in copies:
        copy.wait()


def place(line, result, grad, sums):
    piece = sums.shape[0]
    vmem = pl.BlockSpec(memory_space=pltpu.VMEM)
    anywhere = pl.BlockSpec(memory_space=pl.ANY)
    shapes = (
        (1, 3, piece, 1024),
        (1, piece, 1024),
        (1, 3, piece, 1024),
        (1, piece, 1024),
        (1, 2, piece, 3072),
        (1, 2, 3 * piece, 1024),
        (1, 2, 3, piece),
        (1, 2, 3 * piece),
        (1, 2, piece),
        (1, 4, piece),
        (1, 4, piece),
    )
    return pl.pallas_call(
        partial(place_kernel, line),
        out_shape=tuple(jax.ShapeDtypeStruct(result.shape, result.dtype) for _ in range(2))
        + tuple(jax.ShapeDtypeStruct(shape, jnp.float32) for shape in shapes),
        in_specs=[vmem] * 3,
        out_specs=(anywhere,) * 8 + (vmem,) * 5,
        scratch_shapes=[
            pltpu.SemaphoreType.DMA((18,)),
        ],
        name="place",
    )(result, grad, sums)


def on_device(
    hidden,
    text_lengths,
    region_counts,
    co_qkv,
    co_out,
    self_qkv,
    self_out,
    mlp_up,
    mlp_down,
    proj_bias,
    mlp_bias_up,
    mlp_bias_down,
    norm_gain_table,
    norm_bias,
    cotangent,
):
    line = lax.axis_size("dp") // 4
    result, grad, sums = layer(
        line,
        text_lengths,
        region_counts,
        hidden,
        cotangent,
        (
            co_qkv,
            co_out,
            self_qkv,
            self_out,
            mlp_up,
            mlp_down,
            proj_bias,
            mlp_bias_up,
            mlp_bias_down,
            norm_gain_table,
            norm_bias,
        ),
    )
    return place(line, result, grad, sums)


def solution(mesh):
    return jax.shard_map(
        on_device,
        mesh=mesh,
        in_specs=(
            P("stream", "dp", None, None),
            P("dp"),
            P("dp"),
            P("stream", None, None, None),
            P("stream", None, None),
            P("stream", None, None, None),
            P("stream", None, None),
            P("stream", None, None, None),
            P("stream", None, None, None),
            P("stream", None, None, None),
            P("stream", None, None),
            P("stream", None, None),
            P("stream", None, None),
            P("stream", None, None),
            P("stream", "dp", None, None),
        ),
        out_specs=(
            P("stream", "dp", None, None),
            P("stream", "dp", None, None),
            P("stream", None, "dp", None),
            P("stream", "dp", None),
            P("stream", None, "dp", None),
            P("stream", "dp", None),
            P("stream", None, "dp", None),
            P("stream", None, "dp", None),
            P("stream", None, None, "dp"),
            P("stream", None, "dp"),
            P("stream", None, "dp"),
            P("stream", None, "dp"),
            P("stream", None, "dp"),
        ),
        check_vma=False,
    )
```

```python
from functools import partial
from typing import NamedTuple
import math

import jax
import jax.numpy as jnp
from jax import lax
from jax.experimental import pallas as pl
from jax.experimental.pallas import tpu as pltpu
from jax.sharding import PartitionSpec as P

EPSILON = 1e-05
NEGATIVE = -1000000000.0
ROOT_HALF = 1.0 / math.sqrt(2.0)
GAUSS_NORM = 1.0 / math.sqrt(2.0 * math.pi)

MESH = pl.DeviceIdType.MESH
UNIT = 256
OUT_BLOCKS = 81
CORE_SLOTS = 4
Z_SLOTS = 6
SUM_LAG = 1
SUM_SLOTS = 4
VMEM_BYTES = 65200 * 1024

TEXT_UNITS = (
    (3, 3, 9, 1, 60, 0, 68, 4, 256),
    (1, 12, 5, 0, 44, 0, 44, 0, 192),
    (1, 3, 3, 0, 28, 0, 28, 0, 192),
    (3, 3, 2, 0, 16, 4, 16, 4, 192),
    (3, 3, 6, 1, 56, 0, 56, 4, 256),
    (1, 12, 4, 0, 32, 0, 32, 0, 192),
    (1, 3, 1, 0, 12, 0, 12, 0, 256),
    (3, 4, 0, 0, 0, 4, 0, 4, 192),
    (1, 1, 0, 0, 0, 0, 80, 0, 256),
)
IMAGE_UNITS = (
    (3, 4, 9, 1, 60, 0, 68, 4, 128),
    (1, 4, 5, 0, 44, 0, 44, 0, 256),
    (1, 4, 3, 0, 28, 0, 28, 0, 256),
    (3, 4, 2, 0, 16, 4, 16, 4, 256),
    (3, 4, 6, 1, 56, 0, 56, 4, 128),
    (1, 4, 4, 0, 32, 0, 32, 0, 256),
    (1, 4, 1, 0, 12, 0, 12, 0, 256),
    (3, 4, 0, 0, 0, 4, 0, 4, 256),
    (1, 1, 0, 0, 0, 0, 80, 0, 256),
)


def side_lag(line):
    return 6 if line <= 8 else 4


def line_lag(line):
    return 3 if line <= 8 else 1


def slots_held(line):
    return side_lag(line) + (line - 1) * line_lag(line) + 1 + SUM_LAG


def unit_count(table):
    return sum(entry[0] * entry[1] for entry in table)


def decode_one(table, unit):
    start = 0
    result = None
    for groups, blocks, a0, a1, g0, g1, o0, o1, kept in table:
        local = unit - start
        group = local // blocks
        block = local % blocks
        fields = (a0 + a1 * group, g0 + g1 * group + block, o0 + o1 * group + block, jnp.int32(kept))
        if result is None:
            result = fields
        else:
            result = tuple(jnp.where(unit >= start, new, old) for new, old in zip(fields, result))
        start += groups * blocks
    return result


def kept_one(table, unit):
    start = 0
    result = jnp.int32(table[0][-1])
    before = table[0][-1]
    for groups, blocks, *_, kept in table:
        if kept != before:
            result = jnp.where(unit >= start, kept, result)
            before = kept
        start += groups * blocks
    return result


def rows_kept(is_text, unit):
    return jnp.where(is_text, kept_one(TEXT_UNITS, unit), kept_one(IMAGE_UNITS, unit))


def decode(is_text, unit):
    text = decode_one(TEXT_UNITS, unit)
    image = decode_one(IMAGE_UNITS, unit)
    return tuple(jnp.where(is_text, one, other) for one, other in zip(text, image))


SENT = 104


class Stream(NamedTuple):
    asks: bool
    width: int
    inner: int
    split: int
    head: int
    own_keys: int
    order: tuple


SHORT = 64
TEXT = Stream(True, 768, 3072, 2, 64, SHORT, (0, 1, 2))
IMAGE = Stream(False, 1024, 1024, 1, 128, 112, (1, 2, 0))
TEXT_PACE = (36, 55, 4)
IMAGE_PACE = (42, 54, 4)
RING = 3
LANES = 128
TAIL = (
    0.28208317669832234,
    0.2824362970929616,
    0.24263030272423752,
    0.20467309203585946,
    -0.03157028123874516,
    0.28558060664263174,
    -0.4940359058844012,
    0.2879944144937219,
    -0.0597917499304742,
)


def gelu_parts(value):
    root = jnp.abs(value) * ROOT_HALF
    near = 1.0 / (1.0 + 0.5 * root)
    bell = jnp.exp(-(root * root))
    series = TAIL[-1] * near
    for factor in TAIL[-2::-1]:
        series = (series + factor) * near
    tail = 0.5 * bell * series
    below = jnp.where(value >= 0.0, 1.0 - tail, tail)
    return value * below, below + value * bell * GAUSS_NORM


def layer_kernel(
    line,
    pairs,
    slots,
    tall,
    text_lengths,
    region_counts,
    hidden,
    cotangent,
    co_qkv_whole,
    co_out_whole,
    self_qkv_whole,
    self_out_whole,
    mlp_up_whole,
    mlp_down_whole,
    proj_bias,
    bias_up,
    bias_down,
    gain,
    shift,
    result,
    grad,
    sums_out,
    at_ref,
    g_ref,
    vectors,
    hidden_vectors,
    staged,
    ring,
    far,
    far_query,
    state,
    total,
    low,
    active,
    normal,
    spread,
    self_probs,
    co_probs,
    params,
    up_params,
    ring_sems,
    send_sems,
    recv_sems,
    back_send_sems,
    back_recv_sems,
    landing_free,
    staged_sems,
    core_out,
    core_in,
    partial_own,
    x_out,
    x_in,
    own,
    down_out,
    down_in,
    up_out,
    up_in,
    core_sems,
    x_sems,
    down_sems,
    up_sems,
    down_free,
    up_free,
    sum_sems,
    blank_sems,
):
    stream = lax.axis_index("stream")
    place = lax.axis_index("dp")
    partner = (1 - stream, place)
    height = pairs * tall
    piece = 256 // line
    per_block = 256 // piece

    core = lax.rem(place, 2)
    side = lax.rem(place // 2, 2)
    spot = place // 4
    is_text = stream == 0
    unit_total = jnp.where(is_text, unit_count(TEXT_UNITS), unit_count(IMAGE_UNITS))
    core_device = (stream, place + 1 - 2 * core)
    side_device = (stream, place + 2 - 4 * side)
    lower_device = (stream, place - 4)
    upper_device = (stream, place + 4)
    own_slots = slots_held(line)
    last = line - 1
    co_qkv, co_out, self_qkv, self_out, mlp_up, mlp_down = (
        ref.at[0]
        for ref in (
            co_qkv_whole,
            co_out_whole,
            self_qkv_whole,
            self_out_whole,
            mlp_up_whole,
            mlp_down_whole,
        )
    )

    def stage(index):
        source = (hidden, cotangent)[index]
        return pltpu.make_async_copy(source.at[0], staged.at[index], staged_sems.at[index])

    def unstage(index):
        return pltpu.make_async_copy(low, (result, grad)[index], staged_sems.at[index])

    stage(0).start()
    stage(1).start()
    far[...] = jnp.zeros_like(far)
    far_query[...] = jnp.zeros_like(far_query)

    barrier = pltpu.get_barrier_semaphore()
    for device in (partner, core_device, side_device):
        pl.semaphore_signal(barrier, inc=1, device_id=device, device_id_type=MESH)

    @pl.when(spot > 0)
    def _():
        pl.semaphore_signal(barrier, inc=1, device_id=lower_device, device_id_type=MESH)

    @pl.when(spot < last)
    def _():
        pl.semaphore_signal(barrier, inc=1, device_id=upper_device, device_id_type=MESH)

    pl.semaphore_wait(
        barrier, 3 + (spot > 0).astype(jnp.int32) + (spot < last).astype(jnp.int32)
    )
    for index in range(3):
        for half in range(2):
            row = 3 * half + index
            params[row : row + 1] = proj_bias[0, index, half : half + 1].astype(jnp.float32)
    params[6:8] = bias_down[0].astype(jnp.float32)
    params[8:12] = gain[0].astype(jnp.float32)
    params[12:16] = shift[0].astype(jnp.float32)
    up_params[0:2] = bias_up[0].astype(jnp.float32)
    vectors[...] = jnp.zeros_like(vectors)
    hidden_vectors[...] = jnp.zeros_like(hidden_vectors)

    state[0:piece] = jnp.zeros((piece, 1024), jnp.float32)

    def blank(index):
        width = min(1024, OUT_BLOCKS * UNIT - index * 1024)
        return pltpu.make_async_copy(
            state.at[pl.ds(0, piece), pl.ds(0, width)],
            sums_out.at[:, pl.ds(index * 1024, width)],
            blank_sems.at[index],
        )

    blanks = [blank(index) for index in range(-(-OUT_BLOCKS * UNIT // 1024))]
    for copy in blanks:
        copy.start()

    def block(index):
        return pl.ds(pl.multiple_of(index * UNIT, UNIT), UNIT)

    def pair_rows(pair, count=tall):
        return pl.ds(pl.multiple_of(pair * tall, tall), count)

    def exchange(source, source_at, target, target_at, sends, receives, which, pair):
        return pltpu.make_async_remote_copy(
            src_ref=source.at[source_at],
            dst_ref=target.at[target_at],
            send_sem=sends.at[which, pair],
            recv_sem=receives.at[which, pair],
            device_id=partner,
            device_id_type=MESH,
        )

    def short_rows(which, pair):
        return pl.ds(
            pl.multiple_of((which * pairs + pair) * SHORT, SHORT), SHORT
        )

    def ask(pair):
        at = pair_rows(pair, SENT)
        return exchange(g_ref.at[0], at, far_query, at, send_sems, recv_sems, 0, pair)

    def hand(which, pair):
        return exchange(
            g_ref.at[1 + which],
            pair_rows(pair, SHORT),
            far,
            short_rows(which, pair),
            send_sems,
            recv_sems,
            1 + which,
            pair,
        )

    def answer(pair):
        at = pair_rows(pair, SENT)
        return exchange(active, at, far, at, send_sems, recv_sems, 0, pair)

    def ask_back(pair):
        at = pair_rows(pair, SENT)
        return exchange(low, at, active, at, back_send_sems, back_recv_sems, 0, pair)

    def hand_back(which, pair):
        return exchange(
            far,
            short_rows(which, pair),
            g_ref.at[1 + which],
            pair_rows(pair, SHORT),
            back_send_sems,
            back_recv_sems,
            1 + which,
            pair,
        )

    def answer_back(pair):
        at = pair_rows(pair, SENT)
        return exchange(far_query, at, g_ref.at[0], at, back_send_sems, back_recv_sems, 0, pair)

    def for_rows(kept, body):
        for rows in (128, 192, 256):

            @pl.when(kept == rows)
            def _():
                body(rows)

    def core_copy(unit, rows):
        slot = lax.rem(unit, CORE_SLOTS)
        return pltpu.make_async_remote_copy(
            src_ref=core_out.at[slot, :, pl.ds(0, rows)],
            dst_ref=core_in.at[slot, :, pl.ds(0, rows)],
            send_sem=core_sems.at[0, slot],
            recv_sem=core_sems.at[1, slot],
            device_id=core_device,
            device_id_type=MESH,
        )

    def side_copy(unit, rows):
        slot = lax.rem(unit, 2 * side_lag(line))
        return pltpu.make_async_remote_copy(
            src_ref=x_out.at[slot, pl.ds(0, rows)],
            dst_ref=x_in.at[slot, pl.ds(0, rows)],
            send_sem=x_sems.at[0, slot],
            recv_sem=x_sems.at[1, slot],
            device_id=side_device,
            device_id_type=MESH,
        )

    def line_copy(source, target, sems, device, slot, index):
        at = pl.ds(pl.multiple_of(index * piece, piece), piece)
        return pltpu.make_async_remote_copy(
            src_ref=source.at[slot, at],
            dst_ref=target.at[slot, at],
            send_sem=sems.at[0, slot, index],
            recv_sem=sems.at[1, slot, index],
            device_id=device,
            device_id_type=MESH,
        )

    def columns(block):
        return pl.ds(pl.multiple_of(block * UNIT, UNIT), UNIT)

    def multiply(unit):
        a_block, g_block, out_block, kept = decode(is_text, unit)
        slot = lax.rem(unit, CORE_SLOTS)
        keep = lax.rem(unit, 2)
        is_vector = unit == unit_total - 1

        @pl.when(jnp.logical_not(is_vector))
        def _():
            gradient = g_ref[g_block // 4, :, columns(lax.rem(g_block, 4))]

            def body(rows):
                def product(which):
                    operand = at_ref[a_block, which, :, pl.ds(0, rows)]
                    return jnp.dot(
                        operand.reshape(2 * rows, operand.shape[-1]),
                        gradient,
                        preferred_element_type=jnp.float32,
                    ).reshape(2, rows, UNIT)

                core_out[slot, :, pl.ds(0, rows)] = product(1 - core).astype(jnp.bfloat16)
                core_copy(unit, rows).start()
                partial_own[keep, :, pl.ds(0, rows)] = product(core)

            for_rows(kept, body)

        @pl.when(is_vector)
        def _():
            place_vectors(slot, keep)
            core_copy(unit, 256).start()

    def add_core(unit):
        kept = rows_kept(is_text, unit)
        slot = lax.rem(unit, CORE_SLOTS)
        keep = lax.rem(unit, 2)
        far = lax.rem(unit, 2 * side_lag(line))
        store = lax.rem(unit, own_slots)

        def body(rows):
            core_copy(unit, rows).wait()
            at = pl.ds(0, rows)
            x_out[far, at] = (
                partial_own[keep, 1 - side, at] + core_in[slot, 1 - side, at].astype(jnp.float32)
            ).astype(jnp.bfloat16)
            side_copy(unit, rows).start()
            own[store, at] = partial_own[keep, side, at] + core_in[slot, side, at].astype(
                jnp.float32
            )

        for_rows(kept, body)

    def add_side(unit):
        kept = rows_kept(is_text, unit)
        far = lax.rem(unit, 2 * side_lag(line))
        store = lax.rem(unit, own_slots)

        def body(rows):
            side_copy(unit, rows).wait()
            at = pl.ds(0, rows)
            own[store, at] += x_in[far, at].astype(jnp.float32)

        for_rows(kept, body)

    def sum_copy(unit, out_block):
        at = pl.ds(pl.multiple_of(spot * piece, piece), piece)
        return pltpu.make_async_copy(
            own.at[lax.rem(unit, own_slots), at],
            sums_out.at[:, columns(out_block)],
            sum_sems.at[lax.rem(unit, SUM_SLOTS)],
        )

    def has_sum(unit):
        return (spot + 1) * piece <= rows_kept(is_text, unit)

    def line_step(unit, source, target, sems, free, sender, reader, low, high, gives, takes):
        slot = lax.rem(unit + Z_SLOTS, Z_SLOTS)

        @pl.when(jnp.logical_and(unit >= Z_SLOTS, gives))
        def _():
            count = rows_kept(is_text, unit - Z_SLOTS) // piece
            pl.semaphore_wait(free, 1)

            def settle(index, carry):
                line_copy(source, target, sems, reader, slot, index).wait_send()
                return carry

            lax.fori_loop(low(count), high(count), settle, 0)

        @pl.when(unit < unit_total)
        def _():
            count = rows_kept(is_text, unit) // piece
            store = lax.rem(unit, own_slots)

            def at(index):
                return pl.ds(pl.multiple_of(index * piece, piece), piece)

            @pl.when(gives)
            def _():
                def forward(index, carry):
                    @pl.when(takes)
                    def _():
                        line_copy(source, target, sems, reader, slot, index).wait_recv()
                        source[slot, at(index)] = (
                            own[store, at(index)] + target[slot, at(index)].astype(jnp.float32)
                        ).astype(jnp.bfloat16)

                    @pl.when(jnp.logical_not(takes))
                    def _():
                        source[slot, at(index)] = own[store, at(index)].astype(jnp.bfloat16)

                    line_copy(source, target, sems, reader, slot, index).start()
                    return carry

                lax.fori_loop(low(count), high(count), forward, 0)

            @pl.when(takes)
            def _():
                @pl.when(spot < count)
                def _():
                    line_copy(source, target, sems, reader, slot, spot).wait_recv()
                    own[store, at(spot)] += target[slot, at(spot)].astype(jnp.float32)

                pl.semaphore_signal(free, inc=1, device_id=sender, device_id_type=MESH)

    def tick(step):
        @pl.when(step < unit_total)
        def _():
            multiply(step)

        @pl.when(jnp.logical_and(step >= 1, step < unit_total + 1))
        def _():
            add_core(step - 1)

        @pl.when(jnp.logical_and(step >= side_lag(line), step < unit_total + side_lag(line)))
        def _():
            add_side(step - side_lag(line))

        falling = step - side_lag(line) - (last - spot) * line_lag(line)

        @pl.when(jnp.logical_and(falling >= 0, falling < unit_total + Z_SLOTS))
        def _():
            line_step(
                falling,
                down_out,
                down_in,
                down_sems,
                down_free,
                upper_device,
                lower_device,
                lambda count: 0,
                lambda count: jnp.minimum(spot, count),
                spot > 0,
                spot < last,
            )

        rising = step - side_lag(line) - spot * line_lag(line)

        @pl.when(jnp.logical_and(rising >= 0, rising < unit_total + Z_SLOTS))
        def _():
            line_step(
                rising,
                up_out,
                up_in,
                up_sems,
                up_free,
                lower_device,
                upper_device,
                lambda count: jnp.minimum(spot + 1, count),
                lambda count: count,
                spot < last,
                spot > 0,
            )

        final = step - side_lag(line) - last * line_lag(line)

        @pl.when(jnp.logical_and(final >= 0, final < unit_total))
        def _():
            pl.when(has_sum(final))(lambda: sum_copy(final, decode(is_text, final)[2]).start())

        settled = final - SUM_LAG

        @pl.when(jnp.logical_and(settled >= 0, settled < unit_total))
        def _():
            pl.when(has_sum(settled))(lambda: sum_copy(settled, 0).wait())

    def place_vectors(slot, keep):
        turned = jnp.concatenate(
            [vectors[...], jnp.zeros((LANES - 32, 1024), jnp.float32)], axis=0
        ).T
        tall_sums = hidden_vectors[...].T
        lane = lax.broadcasted_iota(jnp.int32, (piece, LANES), 1)
        for owner in range(4 * line):
            value = turned[owner * piece : (owner + 1) * piece]
            for group in range(3):
                number = owner * 3 + group
                part = tall_sums[number * piece : (number + 1) * piece]
                for which in range(2):
                    value = jnp.where(
                        lane == 6 + 3 * which + group, part[:, which : which + 1], value
                    )
            total[
                owner // 8 * piece : (owner // 8 + 1) * piece,
                owner % 8 * LANES : (owner % 8 + 1) * LANES,
            ] = value
        core_out[slot] = jnp.zeros((2, 256, UNIT), jnp.bfloat16)
        partial_own[keep] = jnp.zeros((2, 256, UNIT), jnp.float32)

        def step(owner, carry):
            value = total[
                pl.ds(pl.multiple_of(owner // 8 * piece, piece), piece),
                pl.ds(pl.multiple_of(lax.rem(owner, 8) * LANES, LANES), LANES),
            ]
            at = pl.ds(pl.multiple_of((owner // 4) * piece, piece), piece)
            half = lax.rem(owner // 2, 2)

            @pl.when(lax.rem(owner, 2) == core)
            def _():
                partial_own[keep, half, at, 0:LANES] = value

            @pl.when(lax.rem(owner, 2) != core)
            def _():
                core_out[slot, half, at, 0:LANES] = value.astype(jnp.bfloat16)

            return carry

        lax.fori_loop(0, 4 * line, step, 0)

    def run(cfg, own_lengths, far_lengths):
        width, inner = cfg.width, cfg.inner
        chunks = inner // 1024
        groups = width // LANES

        plan = [co_qkv.at[index, pl.ds(0, width)] for index in cfg.order]
        plan.append(co_out.at[:, pl.ds(0, width)])

        def mlp_plan(index, chunk):
            at = pl.ds(chunk * 1024, 1024)
            return mlp_up.at[index, pl.ds(0, width), at], mlp_down.at[index, at, pl.ds(0, width)]

        def square(index):
            return self_qkv.at[index, pl.ds(0, width), pl.ds(0, width)]

        for chunk in range(chunks):
            plan.extend(mlp_plan(0, chunk))
        plan.extend(square(index) for index in range(3))
        plan.append(self_out.at[pl.ds(0, width), pl.ds(0, width)])
        for chunk in range(chunks):
            plan.extend(mlp_plan(1, chunk))
        for chunk in range(chunks):
            plan.extend(mlp_plan(1, chunk)[::-1])
        plan.append(self_out.at[pl.ds(0, width), pl.ds(0, width)])
        plan.extend(square(index) for index in range(3))
        for chunk in range(chunks):
            plan.extend(mlp_plan(0, chunk)[::-1])
        plan.append(co_out.at[:, pl.ds(0, width)])
        plan.extend(co_qkv.at[index, pl.ds(0, width)] for index in range(3))

        def fetch(index):
            rows, columns = plan[index].shape
            return pltpu.make_async_copy(
                plan[index],
                ring.at[index % RING, pl.ds(0, rows), pl.ds(0, columns)],
                ring_sems.at[index % RING],
            )

        used = [0]
        def with_weight(body):
            index = used[0]
            used[0] += 1
            fetch(index).wait()
            rows, columns = plan[index].shape
            body(ring.at[index % RING], rows, columns)
            if index + RING < len(plan):
                fetch(index + RING).start()

        def forward_product(source, consume):
            def body(weight, rows, columns):
                def step(index, carry):
                    consume(
                        index,
                        jnp.dot(
                            source[:, 0:rows],
                            weight[0:rows, block(index)],
                            preferred_element_type=jnp.float32,
                        ),
                    )
                    return carry

                lax.fori_loop(0, columns // UNIT, step, 0)

            with_weight(body)

        segments = []

        def backward_items(source, consume):
            index = used[0]
            used[0] += 1
            rows, columns = plan[index].shape
            weight = ring.at[index % RING]
            count = rows // UNIT

            def item(number):
                @pl.when(number == 0)
                def _():
                    fetch(index).wait()

                consume(
                    number,
                    lax.dot_general(
                        source[:, 0:columns],
                        weight[block(number), 0:columns],
                        (((1,), (1,)), ((), ())),
                        preferred_element_type=jnp.float32,
                    ),
                )
                if index + RING < len(plan):

                    @pl.when(number == count - 1)
                    def _():
                        fetch(index + RING).start()

            segments.append((count, item))

        def add_total(first):
            def consume(index, value):
                if first:
                    total[:, block(index)] = value
                else:
                    total[:, block(index)] += value

            return consume

        def put_rows(at_block, index, value):
            turned = value.T
            for part in range(per_block):
                at_ref[
                    at_block,
                    part % 2,
                    (part // 2) % 2,
                    pl.ds(pl.multiple_of((index * (per_block // 4) + part // 4) * piece, piece), piece),
                ] = turned[part * piece : (part + 1) * piece]

        def put_hidden_rows(at_block, index, value):
            turned = value.T
            for part in range(per_block):
                number = index * per_block + part
                owner = number // 3
                at_ref[
                    at_block + lax.rem(number, 3),
                    lax.rem(owner, 2),
                    lax.rem(owner // 2, 2),
                    pl.ds(pl.multiple_of((owner // 4) * piece, piece), piece),
                ] = turned[part * piece : (part + 1) * piece]

        def put_low(at_block, columns, source=low):
            def step(index, carry):
                put_rows(at_block, index, source[:, block(index)])
                return carry

            lax.fori_loop(0, columns // UNIT, step, 0)

        def for_pairs(body):
            def step(pair, carry):
                body(pair)
                return carry

            lax.fori_loop(0, pairs, step, 0)

        def mean(value):
            return jnp.sum(value, axis=-1, keepdims=True) * (1.0 / width)

        def normalize(value):
            centered = value - mean(value)
            inverse = lax.rsqrt(mean(centered * centered) + EPSILON)
            return centered * inverse, inverse

        def norm_forward(index, bias_row, at_block):
            def body(pair):
                at = pair_rows(pair)
                rows, inverse = normalize(
                    state[at, 0:width] + total[at, 0:width] + params[bias_row : bias_row + 1, 0:width]
                )
                result = (
                    rows * params[8 + index : 9 + index, 0:width]
                    + params[12 + index : 13 + index, 0:width]
                )
                state[at, 0:width] = result
                low[at, 0:width] = result.astype(jnp.bfloat16)
                normal[index, at, 0:width] = rows.astype(jnp.bfloat16)
                spread[at, index : index + 1] = inverse

            for_pairs(body)
            put_low(at_block, width)

        def add_row(ref, row, value):
            ref[row : row + 1, 0 : value.shape[-1]] += jnp.sum(value, axis=0, keepdims=True)

        def norm_gradient(index, at, gradient, rows, inverse, g_block, bias_row):
            scaled = gradient * params[8 + index : 9 + index, 0:width]
            result = inverse * (scaled - mean(scaled) - rows * mean(scaled * rows))
            state[at, 0:width] = result
            rounded = result.astype(jnp.bfloat16)
            g_ref[g_block, at, 0:width] = rounded
            add_row(vectors, 14 + index, gradient * rows)
            add_row(vectors, 18 + index, gradient)
            add_row(vectors, bias_row if bias_row < 6 else bias_row + 6, rounded.astype(jnp.float32))

        def norm_backward(index, g_block, bias_row):
            def body(pair):
                at = pair_rows(pair)
                norm_gradient(
                    index,
                    at,
                    state[at, 0:width] + total[at, 0:width],
                    normal[index, at, 0:width].astype(jnp.float32),
                    spread[at, index : index + 1],
                    g_block,
                    bias_row,
                )

            segments.append((pairs, body))

        def mlp_forward(index):
            for chunk in range(chunks):

                def activate(number, value):
                    act, slope = gelu_parts(
                        value
                        + up_params[
                            index : index + 1,
                            pl.ds(pl.multiple_of(chunk * 1024 + number * UNIT, UNIT), UNIT),
                        ]
                    )
                    act = act.astype(jnp.bfloat16)
                    active[:, block(number)] = act
                    g_ref[8 + 3 * index + chunk, :, block(number)] = slope.astype(jnp.bfloat16)
                    put_hidden_rows(6 + 3 * index, chunk * 4 + number, act)

                forward_product(low, activate)
                forward_product(active, add_total(chunk == 0))

        def mlp_backward(index):
            for chunk in range(chunks):
                g_block = 8 + 3 * index + chunk

                def through(number, value, g_block=g_block, chunk=chunk):
                    slope = g_ref[g_block, :, block(number)].astype(jnp.float32)
                    rounded = (value * slope).astype(jnp.bfloat16)
                    g_ref[g_block, :, block(number)] = rounded
                    hidden_vectors[
                        index : index + 1,
                        pl.ds(pl.multiple_of(chunk * 1024 + number * UNIT, UNIT), UNIT),
                    ] = jnp.sum(rounded.astype(jnp.float32), axis=0, keepdims=True)

                backward_items(g_ref.at[14 + index], through)
                backward_items(g_ref.at[g_block], add_total(chunk == 0))

        def biased(target, bias_row):
            def consume(index, value):
                if bias_row is not None:
                    value = value + params[bias_row : bias_row + 1, block(index)]
                target[:, block(index)] = value.astype(jnp.bfloat16)

            return consume

        def column_sums(g_block, row, columns):
            def item(index):
                vectors[row : row + 1, block(index)] = jnp.sum(
                    g_ref[g_block, :, block(index)].astype(jnp.float32), axis=0, keepdims=True
                )

            segments.append((columns // UNIT, item))

        def stacked(value, split):
            if split == 1:
                return value
            lane = lax.broadcasted_iota(jnp.int32, value.shape, 1)
            zero = jnp.zeros_like(value)
            return jnp.concatenate(
                [jnp.where(lane < 64, value, zero), jnp.where(lane < 64, zero, value)], axis=0
            )

        def unstacked(value, split):
            if split == 1:
                return value
            half = value.shape[0] // 2
            lane = lax.broadcasted_iota(jnp.int32, (half, LANES), 1)
            return jnp.where(lane < 64, value[:half], value[half:])

        def over_keys(reduce, value, split):
            if split == 1:
                return reduce(value, axis=0, keepdims=True)
            half = value.shape[0] // 2
            return jnp.concatenate(
                [
                    jnp.broadcast_to(
                        reduce(part, axis=0, keepdims=True), part.shape
                    )
                    for part in (value[:half], value[half:])
                ],
                axis=0,
            )

        last_last = (((1,), (1,)), ((), ()))
        first_first = (((0,), (0,)), ((), ()))

        def attend_forward(query, keys, values, key_rows, probs, target, lengths, split, head, group_count):
            scale = 1.0 / math.sqrt(head)

            def body(pair):
                length = lengths[pair]
                def one_group(group):
                    at = pl.ds(group * LANES, LANES)
                    key = stacked(keys[key_rows(pair), at], split)
                    value = stacked(values[key_rows(pair), at], split)
                    count = key.shape[0] // split
                    scores = (
                        lax.dot_general(
                            key,
                            query[pair_rows(pair), at],
                            last_last,
                            preferred_element_type=jnp.float32,
                        )
                        * scale
                    )
                    number = lax.broadcasted_iota(jnp.int32, scores.shape, 0)
                    if split == 2:
                        number = jnp.where(number < count, number, number - count)
                    scores = jnp.where(number < length, scores, NEGATIVE)
                    raised = jnp.exp(scores - over_keys(jnp.max, scores, split))
                    shares = (raised * (1.0 / over_keys(jnp.sum, raised, split))).astype(
                        jnp.bfloat16
                    )
                    probs[pair, group, 0 : count * split] = shares
                    target[pair_rows(pair), at] = lax.dot_general(
                        shares,
                        value,
                        first_first,
                        preferred_element_type=jnp.float32,
                    ).astype(jnp.bfloat16)

                for group in range(group_count):
                    one_group(group)

            return body

        def attend_backward(query, keys, values, key_rows, probs, source, split, head, group_count):
            scale = 1.0 / math.sqrt(head)

            def body(pair):
                def one_group(group):
                    at = pl.ds(group * LANES, LANES)
                    key = stacked(keys[key_rows(pair), at], split)
                    value = stacked(values[key_rows(pair), at], split)
                    count = key.shape[0] // split
                    asked = query[pair_rows(pair), at]
                    gradient = source[pair_rows(pair), at]
                    rounded_shares = probs[pair, group, 0 : count * split]
                    shares = rounded_shares.astype(jnp.float32)
                    grad_shares = lax.dot_general(
                        value, gradient, last_last, preferred_element_type=jnp.float32
                    )
                    grad_scores = (
                        shares
                        * (grad_shares - over_keys(jnp.sum, grad_shares * shares, split))
                        * scale
                    ).astype(jnp.bfloat16)
                    grad_value = unstacked(
                        jnp.dot(
                            rounded_shares,
                            gradient,
                            preferred_element_type=jnp.float32,
                        ),
                        split,
                    )
                    grad_key = unstacked(
                        jnp.dot(grad_scores, asked, preferred_element_type=jnp.float32), split
                    )
                    grad_query = lax.dot_general(
                        grad_scores, key, first_first, preferred_element_type=jnp.float32
                    )
                    query[pair_rows(pair), at] = grad_query.astype(jnp.bfloat16)
                    keys[key_rows(pair), at] = grad_key.astype(jnp.bfloat16)
                    values[key_rows(pair), at] = grad_value.astype(jnp.bfloat16)

                for group in range(group_count):
                    one_group(group)

            return body

        def clear_tail(ref, pair, count):
            if count < tall:
                at = pl.ds(pl.multiple_of(pair * tall + count, 16), tall - count)
                ref[at, :] = jnp.zeros((tall - count, ref.shape[-1]), ref.dtype)

        own_refs = (g_ref.at[1], g_ref.at[2])
        def clear_rest(ref, pair):
            ref[pair * tall + SENT : (pair + 1) * tall] = jnp.zeros((tall - SENT, 1024), ref.dtype)

        self_refs = (g_ref.at[4], g_ref.at[5], g_ref.at[6])
        short_refs = (far.at[pl.ds(0, pairs * SHORT)], far.at[pl.ds(pairs * SHORT, pairs * SHORT)])

        def own_rows(pair):
            return pair_rows(pair, cfg.own_keys)

        def far_rows(pair):
            return pl.ds(pl.multiple_of(pair * SHORT, SHORT), SHORT)

        near_attention = (g_ref.at[0], *short_refs, far_rows, co_probs.at[:, pl.ds(8, 8)])
        far_attention = (far_query, *own_refs, own_rows, co_probs.at[:, pl.ds(0, 8)])
        self_attention = (*self_refs, own_rows, self_probs)

        def forward():
            for index in range(RING):
                fetch(index).start()
            if inner < 3072:
                for which in range(6, 12):
                    at_ref[which, :, :, 0:128] = jnp.zeros((2, 2, 128, height), jnp.bfloat16)
            low[...] = jnp.zeros_like(low)
            stage(0).wait()
            for pair in range(pairs):
                low[pair * tall : pair * tall + slots, 0:width] = staged[0, :, pair, 0:width]
            for index in cfg.order:
                forward_product(low, biased(g_ref.at[index], (0, None, 1)[index]))
                if cfg.asks and index == 0:
                    for pair in range(pairs):
                        ask(pair).start()
            put_low(0, width)
            for copy in blanks:
                copy.wait()
            state[:, 0:width] = low[:, 0:width].astype(jnp.float32)
            if cfg.asks:
                for pair in range(pairs):
                    ask(pair).wait_send()
                    clear_rest(g_ref.at[0], pair)
                for which in range(2):
                    for pair in range(pairs):
                        hand(which, pair).start()
                for pair in range(pairs):
                    answer(pair).wait_recv()
                context = far.at[pl.ds(0, height)]
                put_low(1, 1024, context)
                forward_product(context, add_total(True))
                norm_forward(0, 2, 4)
            else:

                def reply(pair):
                    ask(pair).wait_recv()
                    attend_forward(*far_attention, active, own_lengths, 1, 128, 8)(pair)
                    answer(pair).start()

                for_pairs(reply)

                def attend(pair):
                    for which in range(2):
                        hand(which, pair).wait_recv()
                    attend_forward(*near_attention, low, far_lengths, 1, 128, 8)(pair)

                for_pairs(attend)
                for pair in range(pairs):
                    answer(pair).wait_send()
                put_low(1, 1024)
                forward_product(low, add_total(True))
                norm_forward(0, 2, 4)
            mlp_forward(0)
            norm_forward(1, 6, 2)
            if cfg.asks:
                for pair in range(pairs):
                    for which in range(2):
                        hand(which, pair).wait_send()
                        clear_tail(own_refs[which], pair, SHORT)
                pl.semaphore_signal(landing_free, inc=1, device_id=partner, device_id_type=MESH)
            for index, bias_row in ((0, 3), (1, None), (2, 4)):
                forward_product(low, biased(self_refs[index], bias_row))
            for_pairs(
                attend_forward(*self_attention, low, own_lengths, cfg.split, cfg.head, groups)
            )
            put_low(3, width)
            forward_product(low, add_total(True))
            norm_forward(2, 5, 5)
            mlp_forward(1)

            stage(1).wait()
            for pair in range(pairs):
                active[pair * tall : pair * tall + slots] = staged[1, :, pair]
                active[pair * tall + slots : (pair + 1) * tall] = jnp.zeros(
                    (tall - slots, 1024), jnp.bfloat16
                )

            def last_norm(pair):
                at = pair_rows(pair)
                rows, inverse = normalize(
                    state[at, 0:width] + total[at, 0:width] + params[7:8, 0:width]
                )
                output = rows * params[11:12, 0:width] + params[15:16, 0:width]
                low[at, 0:width] = output.astype(jnp.bfloat16)
                gradient = active[at, 0:width].astype(jnp.float32)
                norm_gradient(3, at, gradient, rows, inverse, 15, 7)

            for_pairs(last_norm)
            unstage(0).start()
            if not cfg.asks:
                pl.semaphore_signal(landing_free, inc=1, device_id=partner, device_id_type=MESH)

        def self_attention_item(pair):
            attend_backward(*self_attention, low, cfg.split, cfg.head, groups)(pair)
            for ref in self_refs[1:]:
                clear_tail(ref, pair, cfg.own_keys)

        def partner_ready(pair):
            @pl.when(pair == 0)
            def _():
                pl.semaphore_wait(landing_free, 1)

        def ask_item(pair):
            partner_ready(pair)
            ask_back(pair).start()

        def near_item(pair):
            attend_backward(*near_attention, low, 1, 128, 8)(pair)
            partner_ready(pair)
            for which in range(2):
                hand_back(which, pair).start()

        def answer_item(pair):
            ask_back(pair).wait_recv()
            attend_backward(*far_attention, active, 1, 128, 8)(pair)
            answer_back(pair).start()

        def landed_item(pair):
            if cfg.asks:
                answer_back(pair).wait_recv()
                ask_back(pair).wait_send()
                for which in range(2):
                    hand_back(which, pair).wait_recv()
            else:
                answer_back(pair).wait_send()
                for which in range(2):
                    hand_back(which, pair).wait_send()

        def shown_item(number):
            unstage(0).wait()

        def finish_item(pair):
            at = pair_rows(pair)
            low[at, 0:width] = (state[at, 0:width] + total[at, 0:width]).astype(jnp.bfloat16)
            if width < 1024:
                low[at, width:1024] = jnp.zeros((tall, 1024 - width), jnp.bfloat16)

            @pl.when(pair == pairs - 1)
            def _():
                unstage(1).start()

        def list_backward():
            mlp_backward(1)
            norm_backward(2, 7, 5)
            segments.append((1, shown_item))
            backward_items(g_ref.at[7], biased(low, None))
            segments.append((pairs, self_attention_item))
            for index in range(3):
                backward_items(self_refs[index], add_total(index == 0))
            column_sums(4, 3, width)
            column_sums(6, 4, width)
            norm_backward(1, 14, 6)
            mlp_backward(0)
            norm_backward(0, 3, 2)
            backward_items(g_ref.at[3], biased(low, None))

            if cfg.asks:
                segments.append((pairs, ask_item))
                early = sum(count for count, _ in segments)
                segments.append((pairs, landed_item))
                backward_items(g_ref.at[0], add_total(True))
                column_sums(0, 0, 1024)
            else:
                segments.append((pairs, near_item))
                backward_items(g_ref.at[0], add_total(True))
                column_sums(0, 0, 1024)
                early = sum(count for count, _ in segments)
                segments.append((pairs, answer_item))
            for which in range(2):
                backward_items(own_refs[which], add_total(False))
            column_sums(2, 1, 1024)
            if not cfg.asks:
                segments.append((pairs, landed_item))
            segments.append((pairs, finish_item))
            return early, segments

        return forward, list_backward

    text_forward, text_backward = run(TEXT, text_lengths, region_counts)
    image_forward, image_backward = run(IMAGE, region_counts, text_lengths)
    pl.when(is_text)(text_forward)
    pl.when(jnp.logical_not(is_text))(image_forward)

    def run_items(step, pace, early, segments):
        spread, held, rate = pace
        every = sum(count for count, _ in segments)

        def ahead_of(turn):
            first = jnp.minimum(turn * early // spread, early)
            return jnp.minimum(first + jnp.maximum(turn - held, 0) * rate, every)

        def dispatch(item, some, start):
            if len(some) == 1:
                some[0][1](item - start)
                return
            half = len(some) // 2
            middle = start + sum(count for count, _ in some[:half])
            pl.when(item < middle)(lambda: dispatch(item, some[:half], start))
            pl.when(item >= middle)(lambda: dispatch(item, some[half:], middle))

        def one(item, carry):
            dispatch(item, segments, 0)
            return carry

        lax.fori_loop(ahead_of(step), ahead_of(step + 1), one, 0)

    def turn(step, carry):
        @pl.when(is_text)
        def _():
            run_items(step, TEXT_PACE, *text_backward())

        @pl.when(jnp.logical_not(is_text))
        def _():
            run_items(step, IMAGE_PACE, *image_backward())

        tick(step)
        return carry

    lax.fori_loop(0, unit_total + side_lag(line) + last * line_lag(line) + Z_SLOTS, turn, 0)
    unstage(1).wait()


def layer(line, text_lengths, region_counts, hidden, cotangent, weights):
    _, slots, pairs, width = hidden.shape
    tall = (slots + 15) // 16 * 16
    height = pairs * tall
    piece = 256 // line
    own_slots = slots_held(line)
    vmem = pl.BlockSpec(memory_space=pltpu.VMEM)
    smem = pl.BlockSpec(memory_space=pltpu.SMEM)
    anywhere = pl.BlockSpec(memory_space=pl.ANY)
    bf16, f32 = jnp.bfloat16, jnp.float32
    return pl.pallas_call(
        partial(layer_kernel, line, pairs, slots, tall),
        out_shape=(
            jax.ShapeDtypeStruct((height, width), bf16),
            jax.ShapeDtypeStruct((height, width), bf16),
            jax.ShapeDtypeStruct((piece, OUT_BLOCKS * UNIT), f32),
        ),
        in_specs=[smem] * 2 + [anywhere] * 8 + [vmem] * 5,
        out_specs=(anywhere,) * 3,
        scratch_shapes=[
            pltpu.VMEM((12, 2, 2, 256, height), bf16),
            pltpu.VMEM((16, height, 1024), bf16),
            pltpu.VMEM((32, 1024), f32),
            pltpu.VMEM((8, 3072), f32),
            pltpu.VMEM((2,) + hidden.shape[1:], bf16),
            pltpu.VMEM((RING, 1024, 1024), bf16),
            pltpu.VMEM((pairs * 2 * SHORT, 1024), bf16),
            pltpu.VMEM((height, 1024), bf16),
            pltpu.VMEM((height, 1024), f32),
            pltpu.VMEM((height, 1024), f32),
            pltpu.VMEM((height, 1024), bf16),
            pltpu.VMEM((height, 1024), bf16),
            pltpu.VMEM((3, height, 1024), bf16),
            pltpu.VMEM((height, 4), f32),
            pltpu.VMEM((pairs, 8, 128, tall), bf16),
            pltpu.VMEM((pairs, 16, 112, tall), bf16),
            pltpu.VMEM((16, 1024), f32),
            pltpu.VMEM((8, 3072), f32),
            pltpu.SemaphoreType.DMA((RING,)),
            pltpu.SemaphoreType.DMA((3, pairs)),
            pltpu.SemaphoreType.DMA((3, pairs)),
            pltpu.SemaphoreType.DMA((3, pairs)),
            pltpu.SemaphoreType.DMA((3, pairs)),
            pltpu.SemaphoreType.REGULAR,
            pltpu.SemaphoreType.DMA((2,)),
            pltpu.VMEM((CORE_SLOTS, 2, 256, UNIT), bf16),
            pltpu.VMEM((CORE_SLOTS, 2, 256, UNIT), bf16),
            pltpu.VMEM((2, 2, 256, UNIT), f32),
            pltpu.VMEM((2 * side_lag(line), 256, UNIT), bf16),
            pltpu.VMEM((2 * side_lag(line), 256, UNIT), bf16),
            pltpu.VMEM((own_slots, 256, UNIT), f32),
            pltpu.VMEM((Z_SLOTS, 256, UNIT), bf16),
            pltpu.VMEM((Z_SLOTS, 256, UNIT), bf16),
            pltpu.VMEM((Z_SLOTS, 256, UNIT), bf16),
            pltpu.VMEM((Z_SLOTS, 256, UNIT), bf16),
            pltpu.SemaphoreType.DMA((2, CORE_SLOTS)),
            pltpu.SemaphoreType.DMA((2, 2 * side_lag(line))),
            pltpu.SemaphoreType.DMA((2, Z_SLOTS, line)),
            pltpu.SemaphoreType.DMA((2, Z_SLOTS, line)),
            pltpu.SemaphoreType.REGULAR,
            pltpu.SemaphoreType.REGULAR,
            pltpu.SemaphoreType.DMA((SUM_SLOTS,)),
            pltpu.SemaphoreType.DMA((-(-OUT_BLOCKS * UNIT // 1024),)),
        ],
        compiler_params=pltpu.CompilerParams(
            collective_id=0, has_side_effects=True, vmem_limit_bytes=VMEM_BYTES
        ),
        name="layer",
    )(text_lengths, region_counts, hidden, cotangent, *weights)


def place_kernel(
    line,
    result_in,
    grad_in,
    sums_in,
    result,
    grad,
    co_qkv,
    co_out,
    self_qkv,
    self_out,
    mlp_up,
    mlp_down,
    proj_bias,
    bias_up,
    bias_down,
    gain,
    shift,
    sums,
    rows_in,
    in_sems,
    sems,
):
    piece = 256 // line
    _, slots, pairs, _ = result.shape
    tall = result_in.shape[0] // pairs

    def span(first, width):
        return pl.ds(first * UNIT, width)

    moves = [
        (span(80, UNIT), None),
        (span(12, 1024), co_out.at[0]),
        (span(28, 1024), self_out.at[0]),
        (span(32, 3072), mlp_up.at[0, 0]),
        (span(44, 3072), mlp_up.at[0, 1]),
    ]
    for index in range(3):
        rows = pl.ds(index * piece, piece)
        moves += [
            (span(4 * index, 1024), co_qkv.at[0, index]),
            (span(16 + 4 * index, 1024), self_qkv.at[0, index]),
            (span(56 + 4 * index, 1024), mlp_down.at[0, 0, rows]),
            (span(68 + 4 * index, 1024), mlp_down.at[0, 1, rows]),
        ]
    whole = [
        pltpu.make_async_copy(source, rows_in.at[index], sems.at[index])
        for index, source in enumerate((result_in, grad_in))
    ]
    loads = [
        pltpu.make_async_copy(sums_in.at[:, at], sums.at[:, at], in_sems.at[index])
        for index, (at, _) in enumerate(moves)
    ]
    stores = [
        pltpu.make_async_copy(sums.at[:, at], target, sems.at[2 + index])
        for index, (at, target) in enumerate(moves[1:])
    ]
    for copy in whole + loads:
        copy.start()
    for index, target in enumerate((result, grad)):
        whole[index].wait()
        for pair in range(pairs):
            target[0, :, pair, :] = rows_in[index, pair * tall : pair * tall + slots]
    loads[0].wait()
    for load, store in zip(loads[1:], stores, strict=True):
        load.wait()
        store.start()
    rows = sums[:, 80 * UNIT : 80 * UNIT + LANES].T
    for half in range(2):
        for index in range(3):
            proj_bias[0, index, half : half + 1] = rows[3 * half + index : 3 * half + index + 1]
        for group in range(3):
            bias_up[0, half : half + 1, group * piece : (group + 1) * piece] = rows[
                6 + 3 * half + group : 7 + 3 * half + group
            ]
    bias_down[0] = rows[12:14]
    gain[0] = rows[14:18]
    shift[0] = rows[18:22]
    for store in stores:
        store.wait()


def place(line, slots, pairs, result, grad, sums):
    piece = sums.shape[0]
    vmem = pl.BlockSpec(memory_space=pltpu.VMEM)
    anywhere = pl.BlockSpec(memory_space=pl.ANY)
    shapes = (
        (1, 3, piece, 1024),
        (1, piece, 1024),
        (1, 3, piece, 1024),
        (1, piece, 1024),
        (1, 2, piece, 3072),
        (1, 2, 3 * piece, 1024),
        (1, 3, 2, piece),
        (1, 2, 3 * piece),
        (1, 2, piece),
        (1, 4, piece),
        (1, 4, piece),
    )
    rows = jax.ShapeDtypeStruct((1, slots, pairs, 1024), result.dtype)
    return pl.pallas_call(
        partial(place_kernel, line),
        out_shape=(rows, rows)
        + tuple(jax.ShapeDtypeStruct(shape, jnp.float32) for shape in shapes),
        in_specs=[anywhere] * 3,
        out_specs=(vmem,) * 2 + (anywhere,) * 6 + (vmem,) * 5,
        scratch_shapes=[
            pltpu.VMEM(sums.shape, jnp.float32),
            pltpu.VMEM((2,) + result.shape, result.dtype),
            pltpu.SemaphoreType.DMA((17,)),
            pltpu.SemaphoreType.DMA((18,)),
        ],
        compiler_params=pltpu.CompilerParams(vmem_limit_bytes=62 * 1024 * 1024),
        name="place",
    )(result, grad, sums)


def on_device(
    hidden,
    text_lengths,
    region_counts,
    co_qkv,
    co_out,
    self_qkv,
    self_out,
    mlp_up,
    mlp_down,
    proj_bias,
    mlp_bias_up,
    mlp_bias_down,
    norm_gain_table,
    norm_bias,
    cotangent,
):
    line = lax.axis_size("dp") // 4
    result, grad, sums = layer(
        line,
        text_lengths,
        region_counts,
        jnp.swapaxes(hidden, 1, 2),
        jnp.swapaxes(cotangent, 1, 2),
        (
            co_qkv,
            co_out,
            self_qkv,
            self_out,
            mlp_up,
            mlp_down,
            jnp.swapaxes(proj_bias, 1, 2),
            mlp_bias_up,
            mlp_bias_down,
            norm_gain_table,
            norm_bias,
        ),
    )
    outputs = place(line, hidden.shape[2], hidden.shape[1], result, grad, sums)
    return tuple(
        jnp.swapaxes(output, 1, 2) if index in (0, 1, 8) else output
        for index, output in enumerate(outputs)
    )


def solution(mesh):
    return jax.shard_map(
        on_device,
        mesh=mesh,
        in_specs=(
            P("stream", "dp", None, None),
            P("dp"),
            P("dp"),
            P("stream", None, None, None),
            P("stream", None, None),
            P("stream", None, None, None),
            P("stream", None, None),
            P("stream", None, None, None),
            P("stream", None, None, None),
            P("stream", None, None, None),
            P("stream", None, None),
            P("stream", None, None),
            P("stream", None, None),
            P("stream", None, None),
            P("stream", "dp", None, None),
        ),
        out_specs=(
            P("stream", "dp", None, None),
            P("stream", "dp", None, None),
            P("stream", None, "dp", None),
            P("stream", "dp", None),
            P("stream", None, "dp", None),
            P("stream", "dp", None),
            P("stream", None, "dp", None),
            P("stream", None, "dp", None),
            P("stream", None, None, "dp"),
            P("stream", None, "dp"),
            P("stream", None, "dp"),
            P("stream", None, "dp"),
            P("stream", None, "dp"),
        ),
        check_vma=False,
    )
```

```python
from functools import partial
from typing import NamedTuple
import math

import jax
import jax.numpy as jnp
from jax import lax
from jax.experimental import pallas as pl
from jax.experimental.pallas import tpu as pltpu
from jax.sharding import PartitionSpec as P

EPSILON = 1e-05
NEGATIVE = -1000000000.0
ROOT_HALF = 1.0 / math.sqrt(2.0)
GAUSS_NORM = 1.0 / math.sqrt(2.0 * math.pi)

MESH = pl.DeviceIdType.MESH
UNIT = 256
OUT_BLOCKS = 81
CORE_SLOTS = 4
Z_SLOTS = 6
SUM_LAG = 1
SUM_SLOTS = 4
VMEM_BYTES = 65200 * 1024

TEXT_UNITS = (
    (3, 3, 9, 1, 60, 0, 68, 4, 256),
    (1, 12, 5, 0, 44, 0, 44, 0, 192),
    (1, 3, 3, 0, 28, 0, 28, 0, 192),
    (3, 3, 2, 0, 16, 4, 16, 4, 192),
    (3, 3, 6, 1, 56, 0, 56, 4, 256),
    (1, 12, 4, 0, 32, 0, 32, 0, 192),
    (1, 3, 1, 0, 12, 0, 12, 0, 256),
    (3, 4, 0, 0, 0, 4, 0, 4, 192),
    (1, 1, 0, 0, 0, 0, 80, 0, 256),
)
IMAGE_UNITS = (
    (3, 4, 9, 1, 60, 0, 68, 4, 128),
    (1, 4, 5, 0, 44, 0, 44, 0, 256),
    (1, 4, 3, 0, 28, 0, 28, 0, 256),
    (3, 4, 2, 0, 16, 4, 16, 4, 256),
    (3, 4, 6, 1, 56, 0, 56, 4, 128),
    (1, 4, 4, 0, 32, 0, 32, 0, 256),
    (1, 4, 1, 0, 12, 0, 12, 0, 256),
    (3, 4, 0, 0, 0, 4, 0, 4, 256),
    (1, 1, 0, 0, 0, 0, 80, 0, 256),
)


def side_lag(line):
    return 6 if line <= 8 else 4


def line_lag(line):
    return 3 if line <= 8 else 1


def slots_held(line):
    return side_lag(line) + (line - 1) * line_lag(line) + 1 + SUM_LAG


def unit_count(table):
    return sum(entry[0] * entry[1] for entry in table)


def decode_one(table, unit):
    start = 0
    result = None
    for groups, blocks, a0, a1, g0, g1, o0, o1, kept in table:
        local = unit - start
        group = local // blocks
        block = local % blocks
        fields = (a0 + a1 * group, g0 + g1 * group + block, o0 + o1 * group + block, jnp.int32(kept))
        if result is None:
            result = fields
        else:
            result = tuple(jnp.where(unit >= start, new, old) for new, old in zip(fields, result))
        start += groups * blocks
    return result


def kept_one(table, unit):
    start = 0
    result = jnp.int32(table[0][-1])
    before = table[0][-1]
    for groups, blocks, *_, kept in table:
        if kept != before:
            result = jnp.where(unit >= start, kept, result)
            before = kept
        start += groups * blocks
    return result


def rows_kept(is_text, unit):
    return jnp.where(is_text, kept_one(TEXT_UNITS, unit), kept_one(IMAGE_UNITS, unit))


def decode(is_text, unit):
    text = decode_one(TEXT_UNITS, unit)
    image = decode_one(IMAGE_UNITS, unit)
    return tuple(jnp.where(is_text, one, other) for one, other in zip(text, image))


SENT = 104


class Stream(NamedTuple):
    asks: bool
    width: int
    inner: int
    split: int
    head: int
    own_keys: int
    order: tuple


SHORT = 64
TEXT = Stream(True, 768, 3072, 2, 64, SHORT, (0, 1, 2))
IMAGE = Stream(False, 1024, 1024, 1, 128, 112, (1, 2, 0))
TEXT_PACE = (40, 57, 4)
IMAGE_PACE = (42, 51, 4)
RING = 3
LANES = 128
TAIL = (
    0.28208317669832234,
    0.2824362970929616,
    0.24263030272423752,
    0.20467309203585946,
    -0.03157028123874516,
    0.28558060664263174,
    -0.4940359058844012,
    0.2879944144937219,
    -0.0597917499304742,
)


def gelu_parts(value):
    near = 1.0 / (1.0 + (0.5 * ROOT_HALF) * jnp.abs(value))
    bell = jnp.exp(-0.5 * (value * value))
    series = (0.5 * TAIL[-1]) * near
    for factor in TAIL[-2::-1]:
        series = (series + 0.5 * factor) * near
    tail = bell * series
    below = jnp.where(value >= 0.0, 1.0 - tail, tail)
    return value * below, below + value * bell * GAUSS_NORM


def layer_kernel(
    line,
    pairs,
    slots,
    tall,
    text_lengths,
    region_counts,
    hidden,
    cotangent,
    co_qkv_whole,
    co_out_whole,
    self_qkv_whole,
    self_out_whole,
    mlp_up_whole,
    mlp_down_whole,
    proj_bias,
    bias_up,
    bias_down,
    gain,
    shift,
    result,
    grad,
    sums_out,
    at_ref,
    g_ref,
    vectors,
    hidden_vectors,
    staged,
    ring,
    far,
    far_query,
    state,
    total,
    low,
    active,
    normal,
    spread,
    self_probs,
    co_probs,
    params,
    up_params,
    ring_sems,
    send_sems,
    recv_sems,
    back_send_sems,
    back_recv_sems,
    landing_free,
    staged_sems,
    core_out,
    core_in,
    partial_own,
    x_out,
    x_in,
    own,
    down_out,
    down_in,
    up_out,
    up_in,
    core_sems,
    x_sems,
    down_sems,
    up_sems,
    down_free,
    up_free,
    sum_sems,
    blank_sems,
):
    stream = lax.axis_index("stream")
    place = lax.axis_index("dp")
    partner = (1 - stream, place)
    height = pairs * tall
    piece = 256 // line
    per_block = 256 // piece

    core = lax.rem(place, 2)
    side = lax.rem(place // 2, 2)
    spot = place // 4
    is_text = stream == 0
    unit_total = jnp.where(is_text, unit_count(TEXT_UNITS), unit_count(IMAGE_UNITS))
    core_device = (stream, place + 1 - 2 * core)
    side_device = (stream, place + 2 - 4 * side)
    lower_device = (stream, place - 4)
    upper_device = (stream, place + 4)
    own_slots = slots_held(line)
    last = line - 1
    co_qkv, co_out, self_qkv, self_out, mlp_up, mlp_down = (
        ref.at[0]
        for ref in (
            co_qkv_whole,
            co_out_whole,
            self_qkv_whole,
            self_out_whole,
            mlp_up_whole,
            mlp_down_whole,
        )
    )

    def stage(index):
        source = (hidden, cotangent)[index]
        return pltpu.make_async_copy(source.at[0], staged.at[index], staged_sems.at[index])

    def unstage(index):
        return pltpu.make_async_copy(low, (result, grad)[index], staged_sems.at[index])

    stage(0).start()
    stage(1).start()
    far[...] = jnp.zeros_like(far)
    far_query[...] = jnp.zeros_like(far_query)

    barrier = pltpu.get_barrier_semaphore()
    for device in (partner, core_device, side_device):
        pl.semaphore_signal(barrier, inc=1, device_id=device, device_id_type=MESH)

    @pl.when(spot > 0)
    def _():
        pl.semaphore_signal(barrier, inc=1, device_id=lower_device, device_id_type=MESH)

    @pl.when(spot < last)
    def _():
        pl.semaphore_signal(barrier, inc=1, device_id=upper_device, device_id_type=MESH)

    pl.semaphore_wait(
        barrier, 3 + (spot > 0).astype(jnp.int32) + (spot < last).astype(jnp.int32)
    )
    for index in range(3):
        for half in range(2):
            row = 3 * half + index
            params[row : row + 1] = proj_bias[0, index, half : half + 1].astype(jnp.float32)
    params[6:8] = bias_down[0].astype(jnp.float32)
    params[8:12] = gain[0].astype(jnp.float32)
    params[12:16] = shift[0].astype(jnp.float32)
    up_params[0:2] = bias_up[0].astype(jnp.float32)
    vectors[...] = jnp.zeros_like(vectors)
    hidden_vectors[...] = jnp.zeros_like(hidden_vectors)

    state[0:piece] = jnp.zeros((piece, 1024), jnp.float32)

    def blank(index):
        width = min(1024, OUT_BLOCKS * UNIT - index * 1024)
        return pltpu.make_async_copy(
            state.at[pl.ds(0, piece), pl.ds(0, width)],
            sums_out.at[:, pl.ds(index * 1024, width)],
            blank_sems.at[index],
        )

    blanks = [blank(index) for index in range(-(-OUT_BLOCKS * UNIT // 1024))]
    for copy in blanks:
        copy.start()

    def block(index):
        return pl.ds(pl.multiple_of(index * UNIT, UNIT), UNIT)

    def pair_rows(pair, count=tall):
        return pl.ds(pl.multiple_of(pair * tall, tall), count)

    def exchange(source, source_at, target, target_at, sends, receives, which, pair):
        return pltpu.make_async_remote_copy(
            src_ref=source.at[source_at],
            dst_ref=target.at[target_at],
            send_sem=sends.at[which, pair],
            recv_sem=receives.at[which, pair],
            device_id=partner,
            device_id_type=MESH,
        )

    def short_rows(which, pair):
        return pl.ds(
            pl.multiple_of((which * pairs + pair) * SHORT, SHORT), SHORT
        )

    def ask(pair):
        at = pair_rows(pair, SENT)
        return exchange(g_ref.at[0], at, far_query, at, send_sems, recv_sems, 0, pair)

    def hand(which, pair):
        return exchange(
            g_ref.at[1 + which],
            pair_rows(pair, SHORT),
            far,
            short_rows(which, pair),
            send_sems,
            recv_sems,
            1 + which,
            pair,
        )

    def answer(pair):
        at = pair_rows(pair, SENT)
        return exchange(active, at, far, at, send_sems, recv_sems, 0, pair)

    def ask_back(pair):
        at = pair_rows(pair, SENT)
        return exchange(low, at, active, at, back_send_sems, back_recv_sems, 0, pair)

    def hand_back(which, pair):
        return exchange(
            far,
            short_rows(which, pair),
            g_ref.at[1 + which],
            pair_rows(pair, SHORT),
            back_send_sems,
            back_recv_sems,
            1 + which,
            pair,
        )

    def answer_back(pair):
        at = pair_rows(pair, SENT)
        return exchange(far_query, at, g_ref.at[0], at, back_send_sems, back_recv_sems, 0, pair)

    def for_rows(kept, body):
        for rows in (128, 192, 256):

            @pl.when(kept == rows)
            def _():
                body(rows)

    def core_copy(unit, rows):
        slot = lax.rem(unit, CORE_SLOTS)
        return pltpu.make_async_remote_copy(
            src_ref=core_out.at[slot, :, pl.ds(0, rows)],
            dst_ref=core_in.at[slot, :, pl.ds(0, rows)],
            send_sem=core_sems.at[0, slot],
            recv_sem=core_sems.at[1, slot],
            device_id=core_device,
            device_id_type=MESH,
        )

    def side_copy(unit, rows):
        slot = lax.rem(unit, 2 * side_lag(line))
        return pltpu.make_async_remote_copy(
            src_ref=x_out.at[slot, pl.ds(0, rows)],
            dst_ref=x_in.at[slot, pl.ds(0, rows)],
            send_sem=x_sems.at[0, slot],
            recv_sem=x_sems.at[1, slot],
            device_id=side_device,
            device_id_type=MESH,
        )

    def line_copy(source, target, sems, device, slot, index):
        at = pl.ds(pl.multiple_of(index * piece, piece), piece)
        return pltpu.make_async_remote_copy(
            src_ref=source.at[slot, at],
            dst_ref=target.at[slot, at],
            send_sem=sems.at[0, slot, index],
            recv_sem=sems.at[1, slot, index],
            device_id=device,
            device_id_type=MESH,
        )

    def columns(block):
        return pl.ds(pl.multiple_of(block * UNIT, UNIT), UNIT)

    def multiply(unit):
        a_block, g_block, out_block, kept = decode(is_text, unit)
        slot = lax.rem(unit, CORE_SLOTS)
        keep = lax.rem(unit, 2)
        is_vector = unit == unit_total - 1

        @pl.when(jnp.logical_not(is_vector))
        def _():
            gradient = g_ref[g_block // 4, :, columns(lax.rem(g_block, 4))]

            def body(rows):
                def product(which):
                    operand = at_ref[a_block, which, :, pl.ds(0, rows)]
                    return jnp.dot(
                        operand.reshape(2 * rows, operand.shape[-1]),
                        gradient,
                        preferred_element_type=jnp.float32,
                    ).reshape(2, rows, UNIT)

                core_out[slot, :, pl.ds(0, rows)] = product(1 - core).astype(jnp.bfloat16)
                core_copy(unit, rows).start()
                partial_own[keep, :, pl.ds(0, rows)] = product(core)

            for_rows(kept, body)

        @pl.when(is_vector)
        def _():
            place_vectors(slot, keep)
            core_copy(unit, 256).start()

    def add_core(unit):
        kept = rows_kept(is_text, unit)
        slot = lax.rem(unit, CORE_SLOTS)
        keep = lax.rem(unit, 2)
        far = lax.rem(unit, 2 * side_lag(line))
        store = lax.rem(unit, own_slots)

        def body(rows):
            core_copy(unit, rows).wait()
            at = pl.ds(0, rows)
            x_out[far, at] = (
                partial_own[keep, 1 - side, at] + core_in[slot, 1 - side, at].astype(jnp.float32)
            ).astype(jnp.bfloat16)
            side_copy(unit, rows).start()
            own[store, at] = partial_own[keep, side, at] + core_in[slot, side, at].astype(
                jnp.float32
            )

        for_rows(kept, body)

    def add_side(unit):
        kept = rows_kept(is_text, unit)
        far = lax.rem(unit, 2 * side_lag(line))
        store = lax.rem(unit, own_slots)

        def body(rows):
            side_copy(unit, rows).wait()
            at = pl.ds(0, rows)
            own[store, at] += x_in[far, at].astype(jnp.float32)

        for_rows(kept, body)

    def sum_copy(unit, out_block):
        at = pl.ds(pl.multiple_of(spot * piece, piece), piece)
        return pltpu.make_async_copy(
            own.at[lax.rem(unit, own_slots), at],
            sums_out.at[:, columns(out_block)],
            sum_sems.at[lax.rem(unit, SUM_SLOTS)],
        )

    def has_sum(unit):
        return (spot + 1) * piece <= rows_kept(is_text, unit)

    def line_step(unit, source, target, sems, free, sender, reader, low, high, gives, takes):
        slot = lax.rem(unit + Z_SLOTS, Z_SLOTS)

        @pl.when(jnp.logical_and(unit >= Z_SLOTS, gives))
        def _():
            count = rows_kept(is_text, unit - Z_SLOTS) // piece
            pl.semaphore_wait(free, 1)

            def settle(index, carry):
                line_copy(source, target, sems, reader, slot, index).wait_send()
                return carry

            lax.fori_loop(low(count), high(count), settle, 0)

        @pl.when(unit < unit_total)
        def _():
            count = rows_kept(is_text, unit) // piece
            store = lax.rem(unit, own_slots)

            def at(index):
                return pl.ds(pl.multiple_of(index * piece, piece), piece)

            @pl.when(gives)
            def _():
                def forward(index, carry):
                    @pl.when(takes)
                    def _():
                        line_copy(source, target, sems, reader, slot, index).wait_recv()
                        source[slot, at(index)] = (
                            own[store, at(index)] + target[slot, at(index)].astype(jnp.float32)
                        ).astype(jnp.bfloat16)

                    @pl.when(jnp.logical_not(takes))
                    def _():
                        source[slot, at(index)] = own[store, at(index)].astype(jnp.bfloat16)

                    line_copy(source, target, sems, reader, slot, index).start()
                    return carry

                lax.fori_loop(low(count), high(count), forward, 0)

            @pl.when(takes)
            def _():
                @pl.when(spot < count)
                def _():
                    line_copy(source, target, sems, reader, slot, spot).wait_recv()
                    own[store, at(spot)] += target[slot, at(spot)].astype(jnp.float32)

                pl.semaphore_signal(free, inc=1, device_id=sender, device_id_type=MESH)

    def tick(step):
        @pl.when(step < unit_total)
        def _():
            multiply(step)

        @pl.when(jnp.logical_and(step >= 1, step < unit_total + 1))
        def _():
            add_core(step - 1)

        @pl.when(jnp.logical_and(step >= side_lag(line), step < unit_total + side_lag(line)))
        def _():
            add_side(step - side_lag(line))

        falling = step - side_lag(line) - (last - spot) * line_lag(line)

        @pl.when(jnp.logical_and(falling >= 0, falling < unit_total + Z_SLOTS))
        def _():
            line_step(
                falling,
                down_out,
                down_in,
                down_sems,
                down_free,
                upper_device,
                lower_device,
                lambda count: 0,
                lambda count: jnp.minimum(spot, count),
                spot > 0,
                spot < last,
            )

        rising = step - side_lag(line) - spot * line_lag(line)

        @pl.when(jnp.logical_and(rising >= 0, rising < unit_total + Z_SLOTS))
        def _():
            line_step(
                rising,
                up_out,
                up_in,
                up_sems,
                up_free,
                lower_device,
                upper_device,
                lambda count: jnp.minimum(spot + 1, count),
                lambda count: count,
                spot < last,
                spot > 0,
            )

        final = step - side_lag(line) - last * line_lag(line)

        @pl.when(jnp.logical_and(final >= 0, final < unit_total))
        def _():
            pl.when(has_sum(final))(lambda: sum_copy(final, decode(is_text, final)[2]).start())

        settled = final - SUM_LAG

        @pl.when(jnp.logical_and(settled >= 0, settled < unit_total))
        def _():
            pl.when(has_sum(settled))(lambda: sum_copy(settled, 0).wait())

    def place_vectors(slot, keep):
        turned = jnp.concatenate(
            [vectors[...], jnp.zeros((LANES - 32, 1024), jnp.float32)], axis=0
        ).T
        tall_sums = hidden_vectors[...].T
        lane = lax.broadcasted_iota(jnp.int32, (piece, LANES), 1)
        for owner in range(4 * line):
            value = turned[owner * piece : (owner + 1) * piece]
            for group in range(3):
                number = owner * 3 + group
                part = tall_sums[number * piece : (number + 1) * piece]
                for which in range(2):
                    value = jnp.where(
                        lane == 6 + 3 * which + group, part[:, which : which + 1], value
                    )
            total[
                owner // 8 * piece : (owner // 8 + 1) * piece,
                owner % 8 * LANES : (owner % 8 + 1) * LANES,
            ] = value
        core_out[slot] = jnp.zeros((2, 256, UNIT), jnp.bfloat16)
        partial_own[keep] = jnp.zeros((2, 256, UNIT), jnp.float32)

        def step(owner, carry):
            value = total[
                pl.ds(pl.multiple_of(owner // 8 * piece, piece), piece),
                pl.ds(pl.multiple_of(lax.rem(owner, 8) * LANES, LANES), LANES),
            ]
            at = pl.ds(pl.multiple_of((owner // 4) * piece, piece), piece)
            half = lax.rem(owner // 2, 2)

            @pl.when(lax.rem(owner, 2) == core)
            def _():
                partial_own[keep, half, at, 0:LANES] = value

            @pl.when(lax.rem(owner, 2) != core)
            def _():
                core_out[slot, half, at, 0:LANES] = value.astype(jnp.bfloat16)

            return carry

        lax.fori_loop(0, 4 * line, step, 0)

    def run(cfg, own_lengths, far_lengths):
        width, inner = cfg.width, cfg.inner
        chunks = inner // 1024
        groups = width // LANES

        plan = [co_qkv.at[index, pl.ds(0, width)] for index in cfg.order]
        plan.append(co_out.at[:, pl.ds(0, width)])

        def mlp_plan(index, chunk):
            at = pl.ds(chunk * 1024, 1024)
            return mlp_up.at[index, pl.ds(0, width), at], mlp_down.at[index, at, pl.ds(0, width)]

        def square(index):
            return self_qkv.at[index, pl.ds(0, width), pl.ds(0, width)]

        for chunk in range(chunks):
            plan.extend(mlp_plan(0, chunk))
        plan.extend(square(index) for index in range(3))
        plan.append(self_out.at[pl.ds(0, width), pl.ds(0, width)])
        for chunk in range(chunks):
            plan.extend(mlp_plan(1, chunk))
        for chunk in range(chunks):
            plan.extend(mlp_plan(1, chunk)[::-1])
        plan.append(self_out.at[pl.ds(0, width), pl.ds(0, width)])
        plan.extend(square(index) for index in range(3))
        for chunk in range(chunks):
            plan.extend(mlp_plan(0, chunk)[::-1])
        plan.append(co_out.at[:, pl.ds(0, width)])
        plan.extend(co_qkv.at[index, pl.ds(0, width)] for index in range(3))

        def fetch(index):
            rows, columns = plan[index].shape
            return pltpu.make_async_copy(
                plan[index],
                ring.at[index % RING, pl.ds(0, rows), pl.ds(0, columns)],
                ring_sems.at[index % RING],
            )

        used = [0]
        def with_weight(body):
            index = used[0]
            used[0] += 1
            fetch(index).wait()
            rows, columns = plan[index].shape
            body(ring.at[index % RING], rows, columns)
            if index + RING < len(plan):
                fetch(index + RING).start()

        def forward_product(source, consume):
            def body(weight, rows, columns):
                def step(index, carry):
                    consume(
                        index,
                        jnp.dot(
                            source[:, 0:rows],
                            weight[0:rows, block(index)],
                            preferred_element_type=jnp.float32,
                        ),
                    )
                    return carry

                lax.fori_loop(0, columns // UNIT, step, 0)

            with_weight(body)

        segments = []

        def backward_items(source, consume):
            index = used[0]
            used[0] += 1
            rows, columns = plan[index].shape
            weight = ring.at[index % RING]
            count = rows // UNIT

            def item(number):
                @pl.when(number == 0)
                def _():
                    fetch(index).wait()

                consume(
                    number,
                    lax.dot_general(
                        source[:, 0:columns],
                        weight[block(number), 0:columns],
                        (((1,), (1,)), ((), ())),
                        preferred_element_type=jnp.float32,
                    ),
                )
                if index + RING < len(plan):

                    @pl.when(number == count - 1)
                    def _():
                        fetch(index + RING).start()

            segments.append((count, item))

        def add_total(first):
            def consume(index, value):
                if first:
                    total[:, block(index)] = value
                else:
                    total[:, block(index)] += value

            return consume

        def put_rows(at_block, index, value):
            turned = value.T
            for part in range(per_block):
                at_ref[
                    at_block,
                    part % 2,
                    (part // 2) % 2,
                    pl.ds(pl.multiple_of((index * (per_block // 4) + part // 4) * piece, piece), piece),
                ] = turned[part * piece : (part + 1) * piece]

        def put_hidden_rows(at_block, index, value):
            turned = value.T
            for part in range(per_block):
                number = index * per_block + part
                owner = number // 3
                at_ref[
                    at_block + lax.rem(number, 3),
                    lax.rem(owner, 2),
                    lax.rem(owner // 2, 2),
                    pl.ds(pl.multiple_of((owner // 4) * piece, piece), piece),
                ] = turned[part * piece : (part + 1) * piece]

        def put_low(at_block, columns, source=low):
            def step(index, carry):
                put_rows(at_block, index, source[:, block(index)])
                return carry

            lax.fori_loop(0, columns // UNIT, step, 0)

        def for_pairs(body):
            def step(pair, carry):
                body(pair)
                return carry

            lax.fori_loop(0, pairs, step, 0)

        def mean(value):
            return jnp.sum(value, axis=-1, keepdims=True) * (1.0 / width)

        def normalize(value):
            centered = value - mean(value)
            inverse = lax.rsqrt(mean(centered * centered) + EPSILON)
            return centered * inverse, inverse

        def norm_forward(index, bias_row, at_block):
            def body(pair):
                at = pair_rows(pair)
                rows, inverse = normalize(
                    state[at, 0:width] + total[at, 0:width] + params[bias_row : bias_row + 1, 0:width]
                )
                result = (
                    rows * params[8 + index : 9 + index, 0:width]
                    + params[12 + index : 13 + index, 0:width]
                )
                state[at, 0:width] = result
                low[at, 0:width] = result.astype(jnp.bfloat16)
                normal[index, at, 0:width] = rows.astype(jnp.bfloat16)
                spread[at, index : index + 1] = inverse

            for_pairs(body)
            put_low(at_block, width)

        def add_row(ref, row, value):
            ref[row : row + 1, 0 : value.shape[-1]] += jnp.sum(value, axis=0, keepdims=True)

        def norm_gradient(index, at, gradient, rows, inverse, g_block, bias_row):
            scaled = gradient * params[8 + index : 9 + index, 0:width]
            result = inverse * (scaled - mean(scaled) - rows * mean(scaled * rows))
            state[at, 0:width] = result
            rounded = result.astype(jnp.bfloat16)
            g_ref[g_block, at, 0:width] = rounded
            add_row(vectors, 14 + index, gradient * rows)
            add_row(vectors, 18 + index, gradient)
            add_row(vectors, bias_row if bias_row < 6 else bias_row + 6, rounded.astype(jnp.float32))

        def norm_backward(index, g_block, bias_row):
            def body(pair):
                at = pair_rows(pair)
                norm_gradient(
                    index,
                    at,
                    state[at, 0:width] + total[at, 0:width],
                    normal[index, at, 0:width].astype(jnp.float32),
                    spread[at, index : index + 1],
                    g_block,
                    bias_row,
                )

            segments.append((pairs, body))

        def mlp_forward(index):
            for chunk in range(chunks):

                def activate(number, value):
                    act, slope = gelu_parts(
                        value
                        + up_params[
                            index : index + 1,
                            pl.ds(pl.multiple_of(chunk * 1024 + number * UNIT, UNIT), UNIT),
                        ]
                    )
                    act = act.astype(jnp.bfloat16)
                    active[:, block(number)] = act
                    g_ref[8 + 3 * index + chunk, :, block(number)] = slope.astype(jnp.bfloat16)
                    put_hidden_rows(6 + 3 * index, chunk * 4 + number, act)

                forward_product(low, activate)
                forward_product(active, add_total(chunk == 0))

        def mlp_backward(index):
            for chunk in range(chunks):
                g_block = 8 + 3 * index + chunk

                def through(number, value, g_block=g_block, chunk=chunk):
                    slope = g_ref[g_block, :, block(number)].astype(jnp.float32)
                    rounded = (value * slope).astype(jnp.bfloat16)
                    g_ref[g_block, :, block(number)] = rounded
                    hidden_vectors[
                        index : index + 1,
                        pl.ds(pl.multiple_of(chunk * 1024 + number * UNIT, UNIT), UNIT),
                    ] = jnp.sum(rounded.astype(jnp.float32), axis=0, keepdims=True)

                backward_items(g_ref.at[14 + index], through)
                backward_items(g_ref.at[g_block], add_total(chunk == 0))

        def biased(target, bias_row):
            def consume(index, value):
                if bias_row is not None:
                    value = value + params[bias_row : bias_row + 1, block(index)]
                target[:, block(index)] = value.astype(jnp.bfloat16)

            return consume

        def column_sums(g_block, row, columns):
            def item(index):
                vectors[row : row + 1, block(index)] = jnp.sum(
                    g_ref[g_block, :, block(index)].astype(jnp.float32), axis=0, keepdims=True
                )

            segments.append((columns // UNIT, item))

        def stacked(value, split):
            if split == 1:
                return value
            lane = lax.broadcasted_iota(jnp.int32, value.shape, 1)
            zero = jnp.zeros_like(value)
            return jnp.concatenate(
                [jnp.where(lane < 64, value, zero), jnp.where(lane < 64, zero, value)], axis=0
            )

        def unstacked(value, split):
            if split == 1:
                return value
            half = value.shape[0] // 2
            lane = lax.broadcasted_iota(jnp.int32, (half, LANES), 1)
            return jnp.where(lane < 64, value[:half], value[half:])

        def over_keys(reduce, value, split):
            if split == 1:
                return reduce(value, axis=0, keepdims=True)
            half = value.shape[0] // 2
            return jnp.concatenate(
                [
                    jnp.broadcast_to(
                        reduce(part, axis=0, keepdims=True), part.shape
                    )
                    for part in (value[:half], value[half:])
                ],
                axis=0,
            )

        last_last = (((1,), (1,)), ((), ()))
        first_first = (((0,), (0,)), ((), ()))

        def attend_forward(query, keys, values, key_rows, probs, target, lengths, split, head, group_count):
            scale = 1.0 / math.sqrt(head)

            def body(pair):
                length = lengths[pair]
                def one_group(group):
                    at = pl.ds(group * LANES, LANES)
                    key = stacked(keys[key_rows(pair), at], split)
                    value = stacked(values[key_rows(pair), at], split)
                    count = key.shape[0] // split
                    scores = (
                        lax.dot_general(
                            key,
                            query[pair_rows(pair), at],
                            last_last,
                            preferred_element_type=jnp.float32,
                        )
                        * scale
                    )
                    number = lax.broadcasted_iota(jnp.int32, scores.shape, 0)
                    if split == 2:
                        number = jnp.where(number < count, number, number - count)
                    scores = jnp.where(number < length, scores, NEGATIVE)
                    raised = jnp.exp(scores - over_keys(jnp.max, scores, split))
                    shares = (raised * (1.0 / over_keys(jnp.sum, raised, split))).astype(
                        jnp.bfloat16
                    )
                    probs[pair, group, 0 : count * split] = shares
                    target[pair_rows(pair), at] = lax.dot_general(
                        shares,
                        value,
                        first_first,
                        preferred_element_type=jnp.float32,
                    ).astype(jnp.bfloat16)

                for group in range(group_count):
                    one_group(group)

            return body

        def attend_backward(query, keys, values, key_rows, probs, source, split, head, group_count):
            scale = 1.0 / math.sqrt(head)

            def body(pair):
                def one_group(group):
                    at = pl.ds(group * LANES, LANES)
                    key = stacked(keys[key_rows(pair), at], split)
                    value = stacked(values[key_rows(pair), at], split)
                    count = key.shape[0] // split
                    asked = query[pair_rows(pair), at]
                    gradient = source[pair_rows(pair), at]
                    rounded_shares = probs[pair, group, 0 : count * split]
                    shares = rounded_shares.astype(jnp.float32)
                    grad_shares = lax.dot_general(
                        value, gradient, last_last, preferred_element_type=jnp.float32
                    )
                    grad_scores = (
                        shares
                        * (grad_shares - over_keys(jnp.sum, grad_shares * shares, split))
                        * scale
                    ).astype(jnp.bfloat16)
                    grad_value = unstacked(
                        jnp.dot(
                            rounded_shares,
                            gradient,
                            preferred_element_type=jnp.float32,
                        ),
                        split,
                    )
                    grad_key = unstacked(
                        jnp.dot(grad_scores, asked, preferred_element_type=jnp.float32), split
                    )
                    grad_query = lax.dot_general(
                        grad_scores, key, first_first, preferred_element_type=jnp.float32
                    )
                    query[pair_rows(pair), at] = grad_query.astype(jnp.bfloat16)
                    keys[key_rows(pair), at] = grad_key.astype(jnp.bfloat16)
                    values[key_rows(pair), at] = grad_value.astype(jnp.bfloat16)

                for group in range(group_count):
                    one_group(group)

            return body

        def clear_tail(ref, pair, count):
            if count < tall:
                at = pl.ds(pl.multiple_of(pair * tall + count, 16), tall - count)
                ref[at, :] = jnp.zeros((tall - count, ref.shape[-1]), ref.dtype)

        own_refs = (g_ref.at[1], g_ref.at[2])
        def clear_rest(ref, pair):
            ref[pair * tall + SENT : (pair + 1) * tall] = jnp.zeros((tall - SENT, 1024), ref.dtype)

        self_refs = (g_ref.at[4], g_ref.at[5], g_ref.at[6])
        short_refs = (far.at[pl.ds(0, pairs * SHORT)], far.at[pl.ds(pairs * SHORT, pairs * SHORT)])

        def own_rows(pair):
            return pair_rows(pair, cfg.own_keys)

        def far_rows(pair):
            return pl.ds(pl.multiple_of(pair * SHORT, SHORT), SHORT)

        near_attention = (g_ref.at[0], *short_refs, far_rows, co_probs.at[:, pl.ds(8, 8)])
        far_attention = (far_query, *own_refs, own_rows, co_probs.at[:, pl.ds(0, 8)])
        self_attention = (*self_refs, own_rows, self_probs)

        def forward():
            for index in range(RING):
                fetch(index).start()
            if inner < 3072:
                for which in range(6, 12):
                    at_ref[which, :, :, 0:128] = jnp.zeros((2, 2, 128, height), jnp.bfloat16)
            low[...] = jnp.zeros_like(low)
            stage(0).wait()
            for pair in range(pairs):
                low[pair * tall : pair * tall + slots, 0:width] = staged[0, :, pair, 0:width]
            for index in cfg.order:
                forward_product(low, biased(g_ref.at[index], (0, None, 1)[index]))
                if cfg.asks and index == 0:
                    for pair in range(pairs):
                        ask(pair).start()
            put_low(0, width)
            for copy in blanks:
                copy.wait()
            state[:, 0:width] = low[:, 0:width].astype(jnp.float32)
            if cfg.asks:
                for pair in range(pairs):
                    ask(pair).wait_send()
                    clear_rest(g_ref.at[0], pair)
                for which in range(2):
                    for pair in range(pairs):
                        hand(which, pair).start()
                for pair in range(pairs):
                    answer(pair).wait_recv()
                context = far.at[pl.ds(0, height)]
                put_low(1, 1024, context)
                forward_product(context, add_total(True))
                norm_forward(0, 2, 4)
            else:

                def reply(pair):
                    ask(pair).wait_recv()
                    attend_forward(*far_attention, active, own_lengths, 1, 128, 8)(pair)
                    answer(pair).start()

                for_pairs(reply)

                def attend(pair):
                    for which in range(2):
                        hand(which, pair).wait_recv()
                    attend_forward(*near_attention, low, far_lengths, 1, 128, 8)(pair)

                for_pairs(attend)
                for pair in range(pairs):
                    answer(pair).wait_send()
                put_low(1, 1024)
                forward_product(low, add_total(True))
                norm_forward(0, 2, 4)
            mlp_forward(0)
            norm_forward(1, 6, 2)
            if cfg.asks:
                for pair in range(pairs):
                    for which in range(2):
                        hand(which, pair).wait_send()
                        clear_tail(own_refs[which], pair, SHORT)
                pl.semaphore_signal(landing_free, inc=1, device_id=partner, device_id_type=MESH)
            for index, bias_row in ((0, 3), (1, None), (2, 4)):
                forward_product(low, biased(self_refs[index], bias_row))
            for_pairs(
                attend_forward(*self_attention, low, own_lengths, cfg.split, cfg.head, groups)
            )
            put_low(3, width)
            forward_product(low, add_total(True))
            norm_forward(2, 5, 5)
            mlp_forward(1)

            stage(1).wait()
            for pair in range(pairs):
                active[pair * tall : pair * tall + slots] = staged[1, :, pair]
                active[pair * tall + slots : (pair + 1) * tall] = jnp.zeros(
                    (tall - slots, 1024), jnp.bfloat16
                )

            def last_norm(pair):
                at = pair_rows(pair)
                rows, inverse = normalize(
                    state[at, 0:width] + total[at, 0:width] + params[7:8, 0:width]
                )
                output = rows * params[11:12, 0:width] + params[15:16, 0:width]
                low[at, 0:width] = output.astype(jnp.bfloat16)
                gradient = active[at, 0:width].astype(jnp.float32)
                norm_gradient(3, at, gradient, rows, inverse, 15, 7)

            for_pairs(last_norm)
            unstage(0).start()
            if not cfg.asks:
                pl.semaphore_signal(landing_free, inc=1, device_id=partner, device_id_type=MESH)

        def self_attention_item(pair):
            attend_backward(*self_attention, low, cfg.split, cfg.head, groups)(pair)
            for ref in self_refs[1:]:
                clear_tail(ref, pair, cfg.own_keys)

        def partner_ready(pair):
            @pl.when(pair == 0)
            def _():
                pl.semaphore_wait(landing_free, 1)

        def ask_item(pair):
            partner_ready(pair)
            ask_back(pair).start()

        def near_item(pair):
            attend_backward(*near_attention, low, 1, 128, 8)(pair)
            partner_ready(pair)
            for which in range(2):
                hand_back(which, pair).start()

        def answer_item(pair):
            ask_back(pair).wait_recv()
            attend_backward(*far_attention, active, 1, 128, 8)(pair)
            answer_back(pair).start()

        def landed_item(pair):
            if cfg.asks:
                answer_back(pair).wait_recv()
                ask_back(pair).wait_send()
                for which in range(2):
                    hand_back(which, pair).wait_recv()
            else:
                answer_back(pair).wait_send()
                for which in range(2):
                    hand_back(which, pair).wait_send()

        def shown_item(number):
            unstage(0).wait()

        def finish_item(pair):
            at = pair_rows(pair)
            low[at, 0:width] = (state[at, 0:width] + total[at, 0:width]).astype(jnp.bfloat16)
            if width < 1024:
                low[at, width:1024] = jnp.zeros((tall, 1024 - width), jnp.bfloat16)

            @pl.when(pair == pairs - 1)
            def _():
                unstage(1).start()

        def list_backward():
            mlp_backward(1)
            norm_backward(2, 7, 5)
            segments.append((1, shown_item))
            backward_items(g_ref.at[7], biased(low, None))
            segments.append((pairs, self_attention_item))
            for index in range(3):
                backward_items(self_refs[index], add_total(index == 0))
            column_sums(4, 3, width)
            column_sums(6, 4, width)
            norm_backward(1, 14, 6)
            mlp_backward(0)
            norm_backward(0, 3, 2)
            backward_items(g_ref.at[3], biased(low, None))

            if cfg.asks:
                segments.append((pairs, ask_item))
                early = sum(count for count, _ in segments)
                segments.append((pairs, landed_item))
                backward_items(g_ref.at[0], add_total(True))
                column_sums(0, 0, 1024)
            else:
                segments.append((pairs, near_item))
                backward_items(g_ref.at[0], add_total(True))
                column_sums(0, 0, 1024)
                early = sum(count for count, _ in segments)
                segments.append((pairs, answer_item))
            for which in range(2):
                backward_items(own_refs[which], add_total(False))
            column_sums(2, 1, 1024)
            if not cfg.asks:
                segments.append((pairs, landed_item))
            segments.append((pairs, finish_item))
            return early, segments

        return forward, list_backward

    text_forward, text_backward = run(TEXT, text_lengths, region_counts)
    image_forward, image_backward = run(IMAGE, region_counts, text_lengths)
    pl.when(is_text)(text_forward)
    pl.when(jnp.logical_not(is_text))(image_forward)

    def run_items(step, pace, early, segments):
        spread, held, rate = pace
        every = sum(count for count, _ in segments)

        def ahead_of(turn):
            first = jnp.minimum(turn * early // spread, early)
            return jnp.minimum(first + jnp.maximum(turn - held, 0) * rate, every)

        def dispatch(item, some, start):
            if len(some) == 1:
                some[0][1](item - start)
                return
            half = len(some) // 2
            middle = start + sum(count for count, _ in some[:half])
            pl.when(item < middle)(lambda: dispatch(item, some[:half], start))
            pl.when(item >= middle)(lambda: dispatch(item, some[half:], middle))

        def one(item, carry):
            dispatch(item, segments, 0)
            return carry

        lax.fori_loop(ahead_of(step), ahead_of(step + 1), one, 0)

    def turn(step, carry):
        @pl.when(is_text)
        def _():
            run_items(step, TEXT_PACE, *text_backward())

        @pl.when(jnp.logical_not(is_text))
        def _():
            run_items(step, IMAGE_PACE, *image_backward())

        tick(step)
        return carry

    lax.fori_loop(0, unit_total + side_lag(line) + last * line_lag(line) + Z_SLOTS, turn, 0)
    unstage(1).wait()


def layer(line, text_lengths, region_counts, hidden, cotangent, weights):
    _, slots, pairs, width = hidden.shape
    tall = (slots + 15) // 16 * 16
    height = pairs * tall
    piece = 256 // line
    own_slots = slots_held(line)
    vmem = pl.BlockSpec(memory_space=pltpu.VMEM)
    smem = pl.BlockSpec(memory_space=pltpu.SMEM)
    anywhere = pl.BlockSpec(memory_space=pl.ANY)
    bf16, f32 = jnp.bfloat16, jnp.float32
    return pl.pallas_call(
        partial(layer_kernel, line, pairs, slots, tall),
        out_shape=(
            jax.ShapeDtypeStruct((height, width), bf16),
            jax.ShapeDtypeStruct((height, width), bf16),
            jax.ShapeDtypeStruct((piece, OUT_BLOCKS * UNIT), f32),
        ),
        in_specs=[smem] * 2 + [anywhere] * 8 + [vmem] * 5,
        out_specs=(anywhere,) * 3,
        scratch_shapes=[
            pltpu.VMEM((12, 2, 2, 256, height), bf16),
            pltpu.VMEM((16, height, 1024), bf16),
            pltpu.VMEM((32, 1024), f32),
            pltpu.VMEM((8, 3072), f32),
            pltpu.VMEM((2,) + hidden.shape[1:], bf16),
            pltpu.VMEM((RING, 1024, 1024), bf16),
            pltpu.VMEM((pairs * 2 * SHORT, 1024), bf16),
            pltpu.VMEM((height, 1024), bf16),
            pltpu.VMEM((height, 1024), f32),
            pltpu.VMEM((height, 1024), f32),
            pltpu.VMEM((height, 1024), bf16),
            pltpu.VMEM((height, 1024), bf16),
            pltpu.VMEM((3, height, 1024), bf16),
            pltpu.VMEM((height, 4), f32),
            pltpu.VMEM((pairs, 8, 128, tall), bf16),
            pltpu.VMEM((pairs, 16, 112, tall), bf16),
            pltpu.VMEM((16, 1024), f32),
            pltpu.VMEM((8, 3072), f32),
            pltpu.SemaphoreType.DMA((RING,)),
            pltpu.SemaphoreType.DMA((3, pairs)),
            pltpu.SemaphoreType.DMA((3, pairs)),
            pltpu.SemaphoreType.DMA((3, pairs)),
            pltpu.SemaphoreType.DMA((3, pairs)),
            pltpu.SemaphoreType.REGULAR,
            pltpu.SemaphoreType.DMA((2,)),
            pltpu.VMEM((CORE_SLOTS, 2, 256, UNIT), bf16),
            pltpu.VMEM((CORE_SLOTS, 2, 256, UNIT), bf16),
            pltpu.VMEM((2, 2, 256, UNIT), f32),
            pltpu.VMEM((2 * side_lag(line), 256, UNIT), bf16),
            pltpu.VMEM((2 * side_lag(line), 256, UNIT), bf16),
            pltpu.VMEM((own_slots, 256, UNIT), f32),
            pltpu.VMEM((Z_SLOTS, 256, UNIT), bf16),
            pltpu.VMEM((Z_SLOTS, 256, UNIT), bf16),
            pltpu.VMEM((Z_SLOTS, 256, UNIT), bf16),
            pltpu.VMEM((Z_SLOTS, 256, UNIT), bf16),
            pltpu.SemaphoreType.DMA((2, CORE_SLOTS)),
            pltpu.SemaphoreType.DMA((2, 2 * side_lag(line))),
            pltpu.SemaphoreType.DMA((2, Z_SLOTS, line)),
            pltpu.SemaphoreType.DMA((2, Z_SLOTS, line)),
            pltpu.SemaphoreType.REGULAR,
            pltpu.SemaphoreType.REGULAR,
            pltpu.SemaphoreType.DMA((SUM_SLOTS,)),
            pltpu.SemaphoreType.DMA((-(-OUT_BLOCKS * UNIT // 1024),)),
        ],
        compiler_params=pltpu.CompilerParams(
            collective_id=0, has_side_effects=True, vmem_limit_bytes=VMEM_BYTES
        ),
        name="layer",
    )(text_lengths, region_counts, hidden, cotangent, *weights)


def place_kernel(
    line,
    result_in,
    grad_in,
    sums_in,
    result,
    grad,
    co_qkv,
    co_out,
    self_qkv,
    self_out,
    mlp_up,
    mlp_down,
    proj_bias,
    bias_up,
    bias_down,
    gain,
    shift,
    sums,
    rows_in,
    in_sems,
    sems,
):
    piece = 256 // line
    _, slots, pairs, _ = result.shape
    tall = result_in.shape[0] // pairs

    def span(first, width):
        return pl.ds(first * UNIT, width)

    moves = [
        (span(80, UNIT), None),
        (span(12, 1024), co_out.at[0]),
        (span(28, 1024), self_out.at[0]),
        (span(32, 3072), mlp_up.at[0, 0]),
        (span(44, 3072), mlp_up.at[0, 1]),
    ]
    for index in range(3):
        rows = pl.ds(index * piece, piece)
        moves += [
            (span(4 * index, 1024), co_qkv.at[0, index]),
            (span(16 + 4 * index, 1024), self_qkv.at[0, index]),
            (span(56 + 4 * index, 1024), mlp_down.at[0, 0, rows]),
            (span(68 + 4 * index, 1024), mlp_down.at[0, 1, rows]),
        ]
    whole = [
        pltpu.make_async_copy(source, rows_in.at[index], sems.at[index])
        for index, source in enumerate((result_in, grad_in))
    ]
    loads = [
        pltpu.make_async_copy(sums_in.at[:, at], sums.at[:, at], in_sems.at[index])
        for index, (at, _) in enumerate(moves)
    ]
    stores = [
        pltpu.make_async_copy(sums.at[:, at], target, sems.at[2 + index])
        for index, (at, target) in enumerate(moves[1:])
    ]
    for copy in whole + loads:
        copy.start()
    for index, target in enumerate((result, grad)):
        whole[index].wait()
        for pair in range(pairs):
            target[0, :, pair, :] = rows_in[index, pair * tall : pair * tall + slots]
    loads[0].wait()
    for load, store in zip(loads[1:], stores, strict=True):
        load.wait()
        store.start()
    rows = sums[:, 80 * UNIT : 80 * UNIT + LANES].T
    for half in range(2):
        for index in range(3):
            proj_bias[0, index, half : half + 1] = rows[3 * half + index : 3 * half + index + 1]
        for group in range(3):
            bias_up[0, half : half + 1, group * piece : (group + 1) * piece] = rows[
                6 + 3 * half + group : 7 + 3 * half + group
            ]
    bias_down[0] = rows[12:14]
    gain[0] = rows[14:18]
    shift[0] = rows[18:22]
    for store in stores:
        store.wait()


def place(line, slots, pairs, result, grad, sums):
    piece = sums.shape[0]
    vmem = pl.BlockSpec(memory_space=pltpu.VMEM)
    anywhere = pl.BlockSpec(memory_space=pl.ANY)
    shapes = (
        (1, 3, piece, 1024),
        (1, piece, 1024),
        (1, 3, piece, 1024),
        (1, piece, 1024),
        (1, 2, piece, 3072),
        (1, 2, 3 * piece, 1024),
        (1, 3, 2, piece),
        (1, 2, 3 * piece),
        (1, 2, piece),
        (1, 4, piece),
        (1, 4, piece),
    )
    rows = jax.ShapeDtypeStruct((1, slots, pairs, 1024), result.dtype)
    return pl.pallas_call(
        partial(place_kernel, line),
        out_shape=(rows, rows)
        + tuple(jax.ShapeDtypeStruct(shape, jnp.float32) for shape in shapes),
        in_specs=[anywhere] * 3,
        out_specs=(vmem,) * 2 + (anywhere,) * 6 + (vmem,) * 5,
        scratch_shapes=[
            pltpu.VMEM(sums.shape, jnp.float32),
            pltpu.VMEM((2,) + result.shape, result.dtype),
            pltpu.SemaphoreType.DMA((17,)),
            pltpu.SemaphoreType.DMA((18,)),
        ],
        compiler_params=pltpu.CompilerParams(vmem_limit_bytes=62 * 1024 * 1024),
        name="place",
    )(result, grad, sums)


def on_device(
    hidden,
    text_lengths,
    region_counts,
    co_qkv,
    co_out,
    self_qkv,
    self_out,
    mlp_up,
    mlp_down,
    proj_bias,
    mlp_bias_up,
    mlp_bias_down,
    norm_gain_table,
    norm_bias,
    cotangent,
):
    line = lax.axis_size("dp") // 4
    result, grad, sums = layer(
        line,
        text_lengths,
        region_counts,
        jnp.swapaxes(hidden, 1, 2),
        jnp.swapaxes(cotangent, 1, 2),
        (
            co_qkv,
            co_out,
            self_qkv,
            self_out,
            mlp_up,
            mlp_down,
            jnp.swapaxes(proj_bias, 1, 2),
            mlp_bias_up,
            mlp_bias_down,
            norm_gain_table,
            norm_bias,
        ),
    )
    outputs = place(line, hidden.shape[2], hidden.shape[1], result, grad, sums)
    return tuple(
        jnp.swapaxes(output, 1, 2) if index in (0, 1, 8) else output
        for index, output in enumerate(outputs)
    )


def solution(mesh):
    return jax.shard_map(
        on_device,
        mesh=mesh,
        in_specs=(
            P("stream", "dp", None, None),
            P("dp"),
            P("dp"),
            P("stream", None, None, None),
            P("stream", None, None),
            P("stream", None, None, None),
            P("stream", None, None),
            P("stream", None, None, None),
            P("stream", None, None, None),
            P("stream", None, None, None),
            P("stream", None, None),
            P("stream", None, None),
            P("stream", None, None),
            P("stream", None, None),
            P("stream", "dp", None, None),
        ),
        out_specs=(
            P("stream", "dp", None, None),
            P("stream", "dp", None, None),
            P("stream", None, "dp", None),
            P("stream", "dp", None),
            P("stream", None, "dp", None),
            P("stream", "dp", None),
            P("stream", None, "dp", None),
            P("stream", None, "dp", None),
            P("stream", None, None, "dp"),
            P("stream", None, "dp"),
            P("stream", None, "dp"),
            P("stream", None, "dp"),
            P("stream", None, "dp"),
        ),
        check_vma=False,
    )
```
